128 devices in a mesh: gx: 16 (over x, y_hi, core), gy: 8 (over z, y_lo).
Axes of the slice: x: 4, y: 4 (y_hi: 2, y_lo: 2; y = y_hi * 2 + y_lo), z: 4, core: 2. Of those that a mesh axis runs over, the one named last changes fastest.
Arguments:
- soil_velocity: float32 [3, 32, 256, 1024], P(None, None, 'gx', 'gy'), may hold values from -6 to 6
- soil_stress: float32 [6, 32, 256, 1024], P(None, None, 'gx', 'gy'), may hold values from -6 to 6
- buoyancy: float32 [32, 256, 1024], P(None, 'gx', 'gy'), may hold values from 0.5 to 1
- lame_first: float32 [32, 256, 1024], P(None, 'gx', 'gy'), may hold values from 0.2 to 0.8
- shear_modulus: float32 [32, 256, 1024], P(None, 'gx', 'gy'), may hold values from 0.1 to 0.6
- stiffness: bfloat16 [8192, 256, 256], P(('gx', 'gy')), may hold values from -1 to 5
- storey_drift: float32 [8192, 256], P(('gx', 'gy')), may hold values from -6 to 6
- drift_rate: float32 [8192, 256], P(('gx', 'gy')), may hold values from -6 to 6
- coupling: float32 [8192, 256], P(('gx', 'gy')), may hold values from 0.05 to 0.5
- contact: float32 [8192, 64], P(('gx', 'gy')), may hold values from 0.1 to 10
- dof_counts: int32 [8192], P(('gx', 'gy')), may hold values from 3 to 255, as said below
- owner_tile: int32 [8192, 1], P(('gx', 'gy')), may hold values from 0 to 127; in each aligned block of 64 rows (0 to 63, 64 to 127, ...) at most 2 rows name the same one
- corner_cell: int32 [8192], P(('gx', 'gy')), may hold values from 0 to 1088
Outputs:
- final_velocity: float32 [3, 32, 256, 1024], P(None, None, 'gx', 'gy')
- final_drift: float32 [8192, 256], P(('gx', 'gy'))
- final_rate: float32 [8192, 256], P(('gx', 'gy'))
The draws below stay inside these ranges and needn't reach their ends.
Inputs may be any that keep to these rules, and one draw needn't show every extreme that they name: `dof_counts`: a multiple of 3; the first building of every device holds the most. `owner_tile`: the index of the tile's device along gx then gy; among the 64 buildings of one device no tile appears more than 2 times, and some tile appears exactly 2 times in some device's buildings; every tile holds some building. `corner_cell`: encodes the footprint's first cell within the owner tile as x * 121 + y, so that the whole footprint lies in that tile.
All inputs are finite; a program needn't handle non-finite values.
Results may differ from the reference program's by a relative error of at most 0.002.
Values sent between devices are 32-bit elements; how exact they have to be, the bound alone decides.
A program may use at most 128 MiB of HBM per device.

```python
import math
import jax
import jax.numpy as jnp
import numpy as np
from jax import lax

LAYERS = 32
CX = 16
CY = 128
FOOT = 8
DOF = 256
BLD_DEV = 64
CAP = 2
NX = 256
NY = 1024
BUILDINGS = 8192
DEVICES = 128


def draw_stiffness(key, part):
    diag_key, spread_key = jax.random.split(jax.random.fold_in(key, 17))
    diagonal = jax.random.uniform(diag_key, (BUILDINGS, DOF), jnp.float32, 1.0, 4.0)
    off_diag = jnp.clip(jax.random.normal(spread_key, (BUILDINGS, DOF, DOF), jnp.float32) * (0.5 / math.sqrt(DOF)), -0.5, 0.5)
    identity = jnp.arange(DOF)[:, None] == jnp.arange(DOF)[None, :]
    return jnp.where(identity[None], diagonal[:, :, None], off_diag).astype(jnp.bfloat16)


def draw_dof_counts(key, part):
    storeys = jax.random.randint(jax.random.fold_in(key, 23), (BUILDINGS,), 1, DOF // 3 + 1)
    leading = jnp.arange(BUILDINGS) % BLD_DEV == 0
    return (3 * jnp.where(leading, DOF // 3, storeys)).astype(jnp.int32)


def set_ends(values, rng, low, largest):
    shape = values.shape
    spot = [jax.random.randint(jax.random.fold_in(rng, axis), (), 0, shape[axis]) for axis in range(len(shape))]
    values = values.at[tuple(spot)].set(low)
    longest = shape.index(max(shape))
    spot[longest] = (spot[longest] + 1) % shape[longest]
    return values.at[tuple(spot)].set(largest)


def level_of(stream_key, shape, shards, least, high):
    def one(position, shards_of):
        heights = jax.random.uniform(jax.random.fold_in(jax.random.fold_in(stream_key, 6), position), (shards_of,), jnp.float32, least / len(shards), high / len(shards))
        return jnp.repeat(jnp.exp(heights), shape[position] // shards_of).reshape((-1,) + (1,) * (len(shape) - position - 1))

    factor_of = one(*shards[0])
    for cut in shards[1:]:
        factor_of = factor_of * one(*cut)
    return factor_of


def assign_block(key, own, number, rows, count, top, most, slope):
    ranking = jax.random.permutation(key, count)
    packed, ordinary = portions_of(count, rows * top, most, slope, True), portions_of(count, rows * top, most, slope, False)
    places = jnp.arange(count)

    def named(sizes, rotation):
        used = int((sizes > 0).sum())
        fixed = max(1, used // 4)
        moved = fixed + (places - fixed + rotation * (used - fixed)) % max(1, count - fixed)
        return jnp.zeros((count,), jnp.int32).at[ranking[jnp.where(places < fixed, places, moved)]].set(jnp.asarray(sizes, jnp.int32))

    sizes = jnp.where(number % 4 == 0, named(packed, number // 4), named(ordinary, number - number // 4 - 1))
    mixed = jax.random.permutation(jax.random.fold_in(own, 3), count)
    source_of, taker = mixed[0:count // 2 * 2:2], mixed[1:count // 2 * 2:2]
    slack = jnp.minimum(sizes[source_of] - 1, most - sizes[taker]) // 2
    slack = jnp.where((source_of == ranking[0]) | (taker == ranking[0]) | (sizes[taker] == 0), 0, jnp.maximum(slack, 0))
    moved = jax.random.randint(jax.random.fold_in(own, 4), (count // 2,), 0, 1 << 20) % (slack + 1)
    sizes = sizes.at[source_of].add(-moved).at[taker].add(moved)
    members = jnp.searchsorted(jnp.cumsum(sizes), jnp.arange(rows * top), side="right").astype(jnp.int32)
    grid = members.reshape(top, rows).T
    grid = grid[jax.random.permutation(jax.random.fold_in(own, 1), rows)]
    rotation = jax.random.randint(jax.random.fold_in(own, 2), (rows, 1), 0, top)
    return jnp.take_along_axis(grid, (jnp.arange(top)[None, :] + rotation) % top, axis=1)


def portions_of(count, total, limit, lean, full):
    portions = [(1 << 20) // math.isqrt(rank ** lean) + 1 for rank in range(1, count + 1)]
    largest = limit if full else min(limit, max(-(-total // count), total * portions[0] // sum(portions)))
    least = 1 if total - largest >= count - 1 else 0
    counts, rest = [largest] + [least] * (count - 1), total - largest - least * (count - 1)
    while rest > 0:
        candidates = [i for i in range(1, count) if counts[i] < largest] or [i for i in range(1, count) if counts[i] < limit]
        mass, left = sum([portions[i] for i in candidates]), rest
        for i in candidates:
            extra = min(limit - counts[i], max(1, left * portions[i] // mass), rest)
            counts[i] = counts[i] + extra
            rest = rest - extra
    return np.array(counts)


def gaussian(stream_key, extent, scale, most, pieces=(), kind=jnp.bfloat16):
    array = jax.random.normal(stream_key, extent, jnp.float32) * scale
    if len(pieces) > 0:
        array = level_of(stream_key, extent, pieces, -0.22, 0.18) * array
    return jnp.clip(array, min=-most, max=most).astype(kind)


def setup_inputs(seed: int = 0) -> dict:
    splits = jax.random.split(jax.random.key(seed), 14)
    soil_velocity = gaussian(splits[0], (3, LAYERS, NX, NY), 1.0, 6.0, ((2, 16), (3, 8)), jnp.float32)
    soil_stress = gaussian(splits[1], (6, LAYERS, NX, NY), 1.0, 6.0, ((2, 16), (3, 8)), jnp.float32)
    buoyancy = jnp.clip(jnp.exp(math.log(1.0) - 0.6931472 * jax.random.uniform(splits[2], (LAYERS, NX, NY), jnp.float32) ** level_of(splits[2], (LAYERS, NX, NY), ((1, 16), (2, 8)), -0.2, 0.2)), 0.5, 1.0)
    lame_first = jnp.clip(jnp.exp(math.log(0.8) - 1.3862944 * jax.random.uniform(splits[3], (LAYERS, NX, NY), jnp.float32) ** level_of(splits[3], (LAYERS, NX, NY), ((1, 16), (2, 8)), -0.2, 0.2)), 0.2, 0.8)
    shear_modulus = jnp.clip(jnp.exp(math.log(0.6) - 1.7917595 * jax.random.uniform(splits[4], (LAYERS, NX, NY), jnp.float32) ** level_of(splits[4], (LAYERS, NX, NY), ((1, 16), (2, 8)), -0.2, 0.2)), 0.1, 0.6)
    stiffness = draw_stiffness(jax.random.fold_in(splits[13], 71), 0)
    storey_drift = gaussian(splits[6], (BUILDINGS, DOF), 1.0, 6.0, ((0, 128),), jnp.float32)
    drift_rate = gaussian(splits[7], (BUILDINGS, DOF), 1.0, 6.0, ((0, 128),), jnp.float32)
    coupling = jnp.clip(jnp.exp(math.log(0.5) - 2.3025851 * jax.random.uniform(splits[8], (BUILDINGS, DOF), jnp.float32) ** level_of(splits[8], (BUILDINGS, DOF), ((0, 128),), -0.2, 0.2)), 0.05, 0.5)
    contact = jnp.clip(jnp.exp(math.log(10.0) - 4.6051702 * jax.random.uniform(splits[9], (BUILDINGS, FOOT * FOOT), jnp.float32) ** level_of(splits[9], (BUILDINGS, FOOT * FOOT), ((0, 128),), -0.2, 0.2)), 0.1, 10.0)
    dof_counts = draw_dof_counts(jax.random.fold_in(splits[13], 71), 0)
    owner_tile_keys = jax.random.split(jax.random.fold_in(splits[11], 1), BUILDINGS // BLD_DEV)
    owner_tile_turns = jax.random.permutation(jax.random.fold_in(splits[11], 3), BUILDINGS // BLD_DEV)
    owner_tile = jax.vmap(lambda own, number: assign_block(jax.random.fold_in(splits[11], 2), own, number, BLD_DEV, DEVICES, 1, CAP, 2))(owner_tile_keys, owner_tile_turns).reshape((BUILDINGS, 1))
    corner_cell = set_ends(jax.random.randint(splits[12], (BUILDINGS,), 0, (CX - FOOT + 1) * (CY - FOOT + 1)), jax.random.fold_in(splits[12], 1), 0, ((CX - FOOT + 1) * (CY - FOOT + 1)) - 1).astype(jnp.int32)
    return dict(soil_velocity=soil_velocity, soil_stress=soil_stress, buoyancy=buoyancy, lame_first=lame_first, shear_modulus=shear_modulus, stiffness=stiffness, storey_drift=storey_drift, drift_rate=drift_rate, coupling=coupling, contact=contact, dof_counts=dof_counts, owner_tile=owner_tile, corner_cell=corner_cell)


inner_coef = 9.0 / 8.0
outer_coef = 1.0 / 24.0
time_step = 0.3


def trim_axis(source, direction, amount):
    return lax.slice_in_dim(source, amount, source.shape[direction] - amount, axis=direction)


def derive(source, direction, forward):
    length = source.shape[direction] - 4

    def window(offset):
        return lax.slice_in_dim(source, offset, offset + length, axis=direction)

    if forward:
        return inner_coef * (window(3) - window(2)) - outer_coef * (window(4) - window(1))
    return inner_coef * (window(2) - window(1)) - outer_coef * (window(3) - window(0))


def gradient(source, direction, forward):
    result = derive(source, direction, forward)
    for other_axis in range(3):
        if other_axis != direction:
            result = trim_axis(result, other_axis, 2)
    return result


def neighbour(source, inside_x, inside_y, step_z, step_x, step_y):
    extent_x = source.shape[1]
    extent_y = source.shape[2]
    itself = source[:, 1:extent_x - 1, 1:extent_y - 1]
    shifted = source[:, 1 + step_x:extent_x - 1 + step_x, 1 + step_y:extent_y - 1 + step_y]
    usable = inside_x[1 + step_x:extent_x - 1 + step_x][None, :, None] & inside_y[1 + step_y:extent_y - 1 + step_y][None, None, :]
    if step_z:
        shifted = jnp.concatenate([shifted[1:], shifted[-1:]], axis=0)
        layer_ok = jnp.arange(source.shape[0]) < source.shape[0] - 1
        usable = usable & layer_ok[:, None, None]
    return jnp.where(usable, shifted, itself)


def mean_of(source, inside_x, inside_y, shifts):
    summed = neighbour(source, inside_x, inside_y, 0, 0, 0)
    for triple in shifts:
        summed = summed + neighbour(source, inside_x, inside_y, triple[0], triple[1], triple[2])
    return summed * (1.0 / (len(shifts) + 1))


def averages(buoy_field, lame_field, shear_field, inside_x, inside_y):
    buoy_avg = [mean_of(buoy_field, inside_x, inside_y, [(0, 1, 0)]),
                mean_of(buoy_field, inside_x, inside_y, [(0, 0, 1)]),
                mean_of(buoy_field, inside_x, inside_y, [(1, 0, 0)])]
    shear_avg = [mean_of(shear_field, inside_x, inside_y, [(0, 1, 0), (0, 0, 1), (0, 1, 1)]),
                 mean_of(shear_field, inside_x, inside_y, [(0, 1, 0), (1, 0, 0), (1, 1, 0)]),
                 mean_of(shear_field, inside_x, inside_y, [(0, 0, 1), (1, 0, 0), (1, 0, 1)])]
    return buoy_avg, lame_field[:, 1:-1, 1:-1], shear_field[:, 1:-1, 1:-1], shear_avg


def stress_update(speeds, stresses, lame_cell, shear_cell, shear_avg):
    stretch_x = gradient(speeds[0], 1, False)
    stretch_y = gradient(speeds[1], 2, False)
    stretch_z = gradient(speeds[2], 0, False)
    summed = stretch_x + stretch_y + stretch_z
    doubled = 2.0 * shear_cell
    return [
        stresses[0] + time_step * (lame_cell * summed + doubled * stretch_x),
        stresses[1] + time_step * (lame_cell * summed + doubled * stretch_y),
        stresses[2] + time_step * (lame_cell * summed + doubled * stretch_z),
        stresses[3] + time_step * shear_avg[0] * (gradient(speeds[0], 2, True) + gradient(speeds[1], 1, True)),
        stresses[4] + time_step * shear_avg[1] * (gradient(speeds[0], 0, True) + gradient(speeds[2], 1, True)),
        stresses[5] + time_step * shear_avg[2] * (gradient(speeds[1], 0, True) + gradient(speeds[2], 2, True)),
    ]


def velocity_update(speeds, stresses, buoy_avg):
    accel_x = gradient(stresses[0], 1, True) + gradient(stresses[3], 2, False) + gradient(stresses[4], 0, False)
    accel_y = gradient(stresses[3], 1, False) + gradient(stresses[1], 2, True) + gradient(stresses[5], 0, False)
    accel_z = gradient(stresses[4], 1, False) + gradient(stresses[5], 2, False) + gradient(stresses[2], 0, True)
    return [speeds[0] + time_step * buoy_avg[0] * accel_x,
            speeds[1] + time_step * buoy_avg[1] * accel_y,
            speeds[2] + time_step * buoy_avg[2] * accel_z]


def pad_cells(source, width_z, width_xy):
    return jnp.pad(source, ((width_z, width_z), (width_xy, width_xy), (width_xy, width_xy)))


def reference(soil_velocity, soil_stress, buoyancy, lame_first, shear_modulus, stiffness, storey_drift, drift_rate, coupling, contact, dof_counts, owner_tile, corner_cell):
    inside_x = jnp.pad(jnp.ones((NX,), dtype=jnp.bool_), 1)
    inside_y = jnp.pad(jnp.ones((NY,), dtype=jnp.bool_), 1)
    buoy_avg, lame_cell, shear_cell, shear_avg = averages(pad_cells(buoyancy, 0, 1), pad_cells(lame_first, 0, 1), pad_cells(shear_modulus, 0, 1), inside_x, inside_y)
    speeds = [soil_velocity[index] for index in range(3)]
    stresses = [soil_stress[index] for index in range(6)]
    dof_mask = jnp.arange(DOF)[None, :] < dof_counts[:, None]
    select = (jnp.arange(DOF)[:, None] % 3 == jnp.arange(3)[None, :]).astype(jnp.float32)
    drifts = jnp.where(dof_mask, storey_drift, 0.0)
    rates = jnp.where(dof_mask, drift_rate, 0.0)
    owners = owner_tile[:, 0]
    corner_span = CY - FOOT + 1
    tiles_y = NY // CY
    start_x = (owners // tiles_y) * CX + corner_cell // corner_span
    start_y = (owners % tiles_y) * CY + corner_cell % corner_span
    offsets = jnp.arange(FOOT)
    cell_index = ((start_x[:, None, None] + offsets[None, :, None]) * NY + start_y[:, None, None] + offsets[None, None, :]).reshape(BUILDINGS, FOOT * FOOT)
    weights = contact / jnp.sum(contact, axis=1, keepdims=True)
    for time_index in range(2):
        surface = jnp.stack([speeds[0][0], speeds[1][0], speeds[2][0]]).reshape(3, NX * NY)
        values = surface[:, cell_index]
        base_motion = jnp.sum(values * weights[None], axis=2).T
        relative = jnp.where(dof_mask, rates - jnp.dot(base_motion, select.T, precision=lax.Precision.HIGHEST), 0.0)
        rounded = drifts.astype(jnp.bfloat16)
        restoring = jnp.einsum("bij,bj->bi", stiffness.astype(jnp.float32), rounded.astype(jnp.float32))
        rates = jnp.where(dof_mask, rates - time_step * restoring - time_step * coupling * relative, 0.0)
        drifts = jnp.where(dof_mask, drifts + time_step * rates, 0.0)
        reaction = jnp.dot(coupling * relative, select, precision=lax.Precision.HIGHEST)
        cell_push = (time_step * FOOT) * reaction.T[:, :, None] * weights[None]
        forcing = jnp.zeros((3, NX * NY), jnp.float32).at[:, cell_index.reshape(-1)].add(cell_push.reshape(3, -1)).reshape(3, NX, NY)
        padded = [pad_cells(component_field, 2, 2) for component_field in speeds]
        stresses = stress_update(padded, stresses, lame_cell, shear_cell, shear_avg)
        stress_padded = [pad_cells(component_field, 2, 2) for component_field in stresses]
        speeds = velocity_update(speeds, stress_padded, buoy_avg)
        speeds = [speeds[index].at[0].add(forcing[index]) for index in range(3)]
    return jnp.stack(speeds), drifts, rates
```

```python
import jax
import jax.numpy as jnp
from jax import lax
from jax.experimental import pallas as pl
from jax.experimental.pallas import tpu as pltpu
from jax.sharding import PartitionSpec as P

MESH = pl.DeviceIdType.MESH
F32 = jnp.float32
BF16 = jnp.bfloat16
DT = 0.3
INNER = 9.0 / 8.0
OUTER = 1.0 / 24.0
FOOT = 8
GX, GY = 16, 8
NZ, CX, CY = 32, 16, 128
NB, DOF = 64, 256
SPAN = CY - FOOT + 1
ROWS = NZ * CX
R0, CC, QQ, PP, XS, YS = 64, 72, 80, 88, 96, 97
exact = lax.Precision.HIGHEST


def iota(shape, dim):
    return lax.broadcasted_iota(jnp.int32, shape, dim)


def mm(a, b, dims, precision=exact):
    return lax.dot_general(a, b, (dims, ((), ())), precision=precision, preferred_element_type=F32)


def split(x):
    hi = x.astype(BF16)
    return hi, (x - hi.astype(F32)).astype(BF16)


def kernel(
    vel, stress, buoy, lame, shear, stiff, drift, rate, coup, contact, dof, owner, corner,
    ovel, odrift, orate,
    vp, sp, mp, lam, av, hy, hm, kk, bd, ct, dofv, ownv, corv,
    send_a, recv_a, send_b, tab, gh, gl, surf, forc,
    bm_s, m_r, m_p, m_q, rest, bds,
    xs, xr, ys, yr,
    ld, ldk, st, a1s, a1r, a2s, a2r, m1s, m1r, m2s, m2r, hs, hr,
):
    me_x = lax.axis_index("gx")
    me_y = lax.axis_index("gy")

    def wrap(value, n):
        return lax.rem(value + n, n)

    east, west = wrap(me_x + 1, GX), wrap(me_x - 1, GX)
    north, south = wrap(me_y + 1, GY), wrap(me_y - 1, GY)

    inside = (pl.ds(2, NZ), pl.ds(8, CX))
    loads = [
        pltpu.make_async_copy(vel, vp.at[:, pl.ds(2, NZ), pl.ds(8, CX), :], ld.at[0]),
        pltpu.make_async_copy(buoy, mp.at[0, pl.ds(0, NZ), pl.ds(8, CX), :], ld.at[1]),
        pltpu.make_async_copy(shear, mp.at[1, pl.ds(0, NZ), pl.ds(8, CX), :], ld.at[2]),
        pltpu.make_async_copy(drift, bd.at[0], ld.at[3]),
        pltpu.make_async_copy(rate, bd.at[1], ld.at[4]),
        pltpu.make_async_copy(coup, bd.at[2], ld.at[5]),
        pltpu.make_async_copy(contact, ct, ld.at[6]),
        pltpu.make_async_copy(dof, dofv, ld.at[7]),
        pltpu.make_async_copy(owner, ownv, ld.at[8]),
        pltpu.make_async_copy(corner, corv, ld.at[9]),
        pltpu.make_async_copy(stress, sp.at[:, pl.ds(2, NZ), pl.ds(8, CX), :], ld.at[10]),
        pltpu.make_async_copy(lame, lam, ld.at[11]),
    ]
    kloads = [
        pltpu.make_async_copy(stiff.at[pl.ds(16 * i, 16)], kk.at[pl.ds(16 * i, 16)], ldk.at[i])
        for i in range(4)
    ]
    for i in range(10):
        loads[i].start()
    for c in kloads:
        c.start()
    loads[10].start()
    loads[11].start()

    barrier = pltpu.get_barrier_semaphore()
    for d in range(1, GX):
        pl.semaphore_signal(
            barrier, inc=1, device_id={"gx": wrap(me_x + d, GX), "gy": me_y}, device_id_type=MESH
        )
    for d in range(1, GY):
        pl.semaphore_signal(
            barrier, inc=1, device_id={"gx": me_x, "gy": wrap(me_y + d, GY)}, device_id_type=MESH
        )
    for gx, gy in ((west, south), (east, north)):
        pl.semaphore_signal(barrier, inc=1, device_id={"gx": gx, "gy": gy}, device_id_type=MESH)

    zero = jnp.zeros((2, 32, CY), F32)
    for f in range(3):
        vp[f, 0:2] = zero
        vp[f, 34:36] = zero
    for f in (2, 4, 5):
        sp[f, 0:2] = zero
        sp[f, 34:36] = zero
    mp[0, NZ] = zero[0]
    mp[1, NZ] = zero[0]
    hm[0, NZ] = zero[0]
    hm[1, NZ] = zero[0]
    surf[...] = jnp.zeros_like(surf)

    rows_v = vp.reshape(3 * 36 * 32, CY)
    rows_s = sp.reshape(6 * 36 * 32, CY)
    rows_m = mp.reshape(2 * 34 * 32, CY)
    rows_h = hm.reshape(2 * 34 * 32, CY)

    def layer_rows(ref, field, depth, first, row):
        return ref[pl.ds((field * depth + first) * 32 + row, NZ, stride=32), :]

    def put_rows(ref, field, depth, first, row, value):
        ref[pl.ds((field * depth + first) * 32 + row, NZ, stride=32), :] = value

    def columns(blocks, picks):
        total = None
        for f, block in enumerate(blocks):
            row, lane = iota((16, CY), 0), iota((16, CY), 1)
            want = jnp.zeros((16, CY), jnp.bool_)
            for r, pick in enumerate(picks):
                if pick is not None and pick[0] == f:
                    want = want | ((row == r) & (lane == pick[1]))
            part = mm(want.astype(F32), block, ((1,), (1,)))
            total = part if total is None else total + part
        return total

    def halo_copy(src, dst, index, gx, gy):
        return pltpu.make_async_remote_copy(
            src_ref=src,
            dst_ref=dst,
            send_sem=hs.at[index],
            recv_sem=hr.at[index],
            device_id={"gx": gx, "gy": gy},
            device_id_type=MESH,
        )

    keep_w = (me_x > 0).astype(F32)
    keep_e = (me_x < GX - 1).astype(F32)
    keep_s = (me_y > 0).astype(F32)
    keep_n = (me_y < GY - 1).astype(F32)

    pairs_v = [(0, 2, 1), (1, 1, 2), (2, 1, 2)]
    pairs_s = [(0, 1, 2), (3, 2, 1), (4, 2, 1)]

    def pack_x(ref, depth, first, pairs, slot):
        at = 0
        for field, before, _ in pairs:
            for i in range(before):
                xs[slot, 0, pl.ds(32 * at, 32), :] = layer_rows(
                    ref, field, depth, first, 8 + CX - before + i
                )
                at += 1
        at = 0
        for field, _, after in pairs:
            for i in range(after):
                xs[slot, 1, pl.ds(32 * at, 32), :] = layer_rows(ref, field, depth, first, 8 + i)
                at += 1
        return sum(p[1] for p in pairs), sum(p[2] for p in pairs)

    def unpack_x(ref, depth, first, pairs, slot):
        at = 0
        for field, before, _ in pairs:
            for i in range(before):
                value = xr[slot, 0, pl.ds(32 * at, 32), :] * keep_w
                put_rows(ref, field, depth, first, 8 - before + i, value)
                at += 1
        at = 0
        for field, _, after in pairs:
            for i in range(after):
                value = xr[slot, 1, pl.ds(32 * at, 32), :] * keep_e
                put_rows(ref, field, depth, first, 8 + CX + i, value)
                at += 1

    def pack_y(ref, fields, extra, slot):
        blocks = [ref[f, pl.ds(2, NZ), pl.ds(8, CX), :].reshape(ROWS, CY) for f in fields] + extra
        picks = [(f, c) for f in range(3) for c in (CY - 2, CY - 1)] + [None, None]
        picks += [(f, c) for f in range(3) for c in (0, 1)]
        picks += [(3 + f, 0) for f in range(len(extra))]
        packed = columns(blocks, picks)
        ys[slot, 0] = packed[0:8]
        ys[slot, 1] = packed[8:16]

    def unpack_y(slot):
        both = jnp.concatenate([yr[slot, 0] * keep_s, yr[slot, 1] * keep_n], axis=0)
        row, lane = iota((16, CY), 0), iota((16, CY), 1)
        for f in range(3):
            place = ((row == 2 * f) & (lane == CY - 2)) | ((row == 2 * f + 1) & (lane == CY - 1))
            place = place | ((row == 8 + 2 * f) & (lane == 0)) | ((row == 8 + 2 * f + 1) & (lane == 1))
            hy[f] = mm(both, place.astype(F32), ((0,), (0,))).reshape(NZ, CX, CY)

    def halo_set(slot, up, down, base):
        return [
            halo_copy(
                xs.at[slot, 0, pl.ds(0, 32 * up)], xr.at[slot, 0, pl.ds(0, 32 * up)], base, east, me_y
            ),
            halo_copy(
                xs.at[slot, 1, pl.ds(0, 32 * down)],
                xr.at[slot, 1, pl.ds(0, 32 * down)],
                base + 1,
                west,
                me_y,
            ),
            halo_copy(ys.at[slot, 0], yr.at[slot, 0], base + 2, me_x, north),
            halo_copy(ys.at[slot, 1], yr.at[slot, 1], base + 3, me_x, south),
        ]

    loads[0].wait()
    loads[1].wait()
    loads[2].wait()
    up, down = pack_x(rows_v, 36, 2, pairs_v, 0)
    for f in range(2):
        xs[0, 1, pl.ds(32 * (down + f), 32), :] = layer_rows(rows_m, f, 34, 0, 8)
    mats = [mp[f, pl.ds(0, NZ), pl.ds(8, CX), :].reshape(ROWS, CY) for f in range(2)]
    pack_y(vp, (0, 1, 2), mats, 0)
    halos0 = halo_set(0, up, down + 2, 0)
    halos0.append(halo_copy(ys.at[0, 1], yr.at[0, 2], 16, west, south))
    pl.semaphore_wait(barrier, GX + GY)
    for c in halos0:
        c.start()

    for i in range(3, 10):
        loads[i].wait()
    eye = iota((NB, NB), 0) == iota((NB, NB), 1)

    def to_col(row):
        return jnp.sum(jnp.where(eye, jnp.broadcast_to(row, (NB, NB)), 0.0), axis=1, keepdims=True)

    dof_col = to_col(dofv[...].astype(F32))
    cor_col = to_col(corv[...].astype(F32))
    own_col = ownv[...].astype(F32)
    own_row = jnp.sum(jnp.where(eye, jnp.broadcast_to(own_col, (NB, NB)), 0.0), axis=0, keepdims=True)
    same = jnp.broadcast_to(own_col, (NB, NB)) == jnp.broadcast_to(own_row, (NB, NB))
    upper = iota((NB, NB), 0) < iota((NB, NB), 1)
    lower = iota((NB, NB), 0) > iota((NB, NB), 1)
    pos_row = jnp.sum(jnp.where(same & upper, 1.0, 0.0), axis=0, keepdims=True)
    pos_col = jnp.sum(jnp.where(same & lower, 1.0, 0.0), axis=1, keepdims=True)
    mask = iota((NB, DOF), 1).astype(F32) < dof_col
    cpl = coupling = jnp.where(mask, bd[2], 0.0)
    rate0 = jnp.where(mask, bd[1], 0.0)
    drift0 = jnp.where(mask, bd[0], 0.0)

    def restore(value, wait):
        bds[...] = value.astype(BF16)

        def block(i, carry):
            mine = bds[pl.ds(pl.multiple_of(16 * i, 16), 16), :]
            row = iota((16, DOF), 0)
            total = jnp.zeros((16, DOF), F32)
            for b in range(16):
                part = mm(mine, kk[16 * i + b], ((1,), (1,)), None)
                total = jnp.where(row == b, part, total)
            rest[pl.ds(pl.multiple_of(16 * i, 16), 16), :] = total
            return carry

        if wait:
            for i in range(4):
                kloads[i].wait()
        lax.fori_loop(0, 4, block, 0)

    restore(drift0, True)
    rest0 = rest[...]

    def gather_dofs(value, lane):
        want = (iota((DOF, CY), 0) % 3 + lane) == iota((DOF, CY), 1)
        return mm(value, want.astype(F32), ((1,), (0,)))

    weights = ct[:, 0:64] / jnp.sum(ct[:, 0:64], axis=1, keepdims=True)
    moved = rate0 - DT * rest0 - DT * cpl * rate0
    info = gather_dofs(cpl * rate0, R0) + gather_dofs(cpl, CC)
    info = info + gather_dofs(DT * cpl * cpl, QQ) + gather_dofs(cpl * moved, PP)
    lane = iota((NB, CY), 1)
    start_x = jnp.floor((cor_col + 0.5) * (1.0 / SPAN))
    start_y = cor_col - SPAN * start_x
    info = jnp.where(lane == XS, start_x, jnp.where(lane == YS, start_y, info))
    info = info + jnp.concatenate([weights, jnp.zeros((NB, CY - 64), F32)], axis=1)
    own_x = jnp.floor((own_row + 0.5) * (1.0 / GY))
    dest = own_row + 8.0 * own_x + 8.0 * pos_row
    route = iota((256, NB), 0).astype(F32) == dest
    send_a[...] = mm(route.astype(F32), info, ((1,), (0,)))

    def a1(peer, slot):
        return pltpu.make_async_remote_copy(
            src_ref=send_a.at[pl.ds(pl.multiple_of(16 * peer, 16), 16)],
            dst_ref=recv_a.at[pl.ds(pl.multiple_of(16 * slot, 16), 16)],
            send_sem=a1s.at[peer],
            recv_sem=a1r.at[slot],
            device_id={"gx": peer, "gy": me_y},
            device_id_type=MESH,
        )

    def a2(peer, slot):
        return pltpu.make_async_remote_copy(
            src_ref=send_b.at[pl.ds(pl.multiple_of(32 * peer, 32), 32)],
            dst_ref=tab.at[pl.ds(pl.multiple_of(32 * slot, 32), 32)],
            send_sem=a2s.at[peer],
            recv_sem=a2r.at[slot],
            device_id={"gx": me_x, "gy": peer},
            device_id_type=MESH,
        )

    def over(n, me, action):
        def one(d, carry):
            action(wrap(me + d, n))
            return carry

        lax.fori_loop(1, n, one, 0)

    over(GX, me_x, lambda peer: a1(peer, me_x).start())
    own16 = pl.ds(pl.multiple_of(16 * me_x, 16), 16)
    recv_a[own16, :] = send_a[own16, :]

    for c in halos0:
        c.wait_recv()
    unpack_x(rows_v, 36, 2, pairs_v, 0)
    unpack_y(0)
    for f in range(2):
        put_rows(rows_m, f, 34, 0, 24, xr[0, 1, pl.ds(32 * (down + f), 32), :])
    row8, lane8 = iota((8, CY), 0), iota((8, CY), 1)
    for f in range(2):
        place = ((row8 == 6 + f) & (lane8 == 0)).astype(F32)
        hm[f, pl.ds(0, NZ), pl.ds(8, CX), :] = mm(yr[0, 1], place, ((0,), (0,))).reshape(NZ, CX, CY)
    place = ((row8 == 7) & (lane8 == 0)).astype(F32)
    diag = mm(yr[0, 2], place, ((0,), (0,))).reshape(NZ, CX, CY)
    hm[1, pl.ds(0, NZ), pl.ds(24, 8), :] = diag[:, 0:8, :]

    lane16, row16 = iota((CX, CY), 1), iota((CX, CY), 0)
    out_x = (row16 == CX - 1) & (me_x == GX - 1)
    out_y = (lane16 == CY - 1) & (me_y == GY - 1)
    out_xy = out_x | out_y

    def shifted(value, halo, step):
        if step > 0:
            return pltpu.roll(jnp.where(lane16 < step, halo, value), CY - step, 1)
        return pltpu.roll(jnp.where(lane16 >= CY + step, halo, value), -step, 1)

    def average(k, carry):
        last = k == NZ - 1
        b, m = mp[0, k, 8:24, :], mp[1, k, 8:24, :]
        bx = jnp.where(out_x, b, mp[0, k, 9:25, :])
        by = jnp.where(out_y, b, shifted(b, hm[0, k, 8:24, :], 1))
        bz = jnp.where(last, b, mp[0, k + 1, 8:24, :])
        east_m = mp[1, k, 9:25, :]
        mx = jnp.where(out_x, m, east_m)
        my = jnp.where(out_y, m, shifted(m, hm[1, k, 8:24, :], 1))
        mxy = jnp.where(out_xy, m, shifted(east_m, hm[1, k, 9:25, :], 1))
        mz = mp[1, k + 1, 8:24, :]
        mxz = jnp.where(out_x | last, m, mp[1, k + 1, 9:25, :])
        myz = jnp.where(out_y | last, m, shifted(mz, hm[1, k + 1, 8:24, :], 1))
        mz = jnp.where(last, m, mz)
        av[0, k] = (b + bx) * (0.5 * DT)
        av[1, k] = (b + by) * (0.5 * DT)
        av[2, k] = (b + bz) * (0.5 * DT)
        av[3, k] = (m + mx + my + mxy) * (0.25 * DT)
        av[4, k] = (m + mx + mz + mxz) * (0.25 * DT)
        av[5, k] = (m + my + mz + myz) * (0.25 * DT)
        return carry

    lax.fori_loop(0, NZ, average, 0)

    over(GX, me_x, lambda peer: a1(me_x, peer).wait_recv())
    for j in range(GY):
        send_b[pl.ds(32 * j, 32), :] = recv_a[pl.ds(j, 32, stride=8), :]
    over(GY, me_y, lambda peer: a2(peer, me_y).start())
    own32 = pl.ds(pl.multiple_of(32 * me_y, 32), 32)
    tab[own32, :] = send_b[own32, :]

    def fwd(minus, zero_, plus, plus2):
        return INNER * (plus - zero_) - OUTER * (plus2 - minus)

    def bwd(minus2, minus, zero_, plus):
        return INNER * (zero_ - minus) - OUTER * (plus - minus2)

    def dx(ref, f, k, forward):
        first = 7 if forward else 6
        parts = [ref[f, k + 2, first + i : first + i + CX, :] for i in range(4)]
        return (fwd if forward else bwd)(*parts)

    def dz(ref, f, k, forward):
        first = 1 if forward else 0
        parts = [ref[f, k + first + i, 8:24, :] for i in range(4)]
        return (fwd if forward else bwd)(*parts)

    def dy(ref, f, h, k, forward):
        value, halo = ref[f, k + 2, 8:24, :], hy[h, k]
        if forward:
            return fwd(shifted(value, halo, -1), value, shifted(value, halo, 1), shifted(value, halo, 2))
        return bwd(shifted(value, halo, -2), shifted(value, halo, -1), value, shifted(value, halo, 1))

    def stress_layer(k, carry):
        sx, sy, sz = dx(vp, 0, k, False), dy(vp, 1, 1, k, False), dz(vp, 2, k, False)
        m2 = (2.0 * DT) * mp[1, k, 8:24, :]
        volume = (DT * lam[k]) * (sx + sy + sz)
        for f, s in ((0, sx), (1, sy), (2, sz)):
            sp[f, k + 2, 8:24, :] += volume + m2 * s
        sp[3, k + 2, 8:24, :] += av[3, k] * (dy(vp, 0, 0, k, True) + dx(vp, 1, k, True))
        sp[4, k + 2, 8:24, :] += av[4, k] * (dz(vp, 0, k, True) + dx(vp, 2, k, True))
        sp[5, k + 2, 8:24, :] += av[5, k] * (dz(vp, 1, k, True) + dy(vp, 2, 2, k, True))
        return carry

    def velocity_layer(k, carry):
        ax = dx(sp, 0, k, True) + dy(sp, 3, 0, k, False) + dz(sp, 4, k, False)
        ay = dx(sp, 3, k, False) + dy(sp, 1, 1, k, True) + dz(sp, 5, k, False)
        az = dx(sp, 4, k, False) + dy(sp, 5, 2, k, False) + dz(sp, 2, k, True)
        for f, a in ((0, ax), (1, ay), (2, az)):
            vp[f, k + 2, 8:24, :] += av[f, k] * a
        return carry

    loads[10].wait()
    loads[11].wait()
    lax.fori_loop(0, NZ, stress_layer, 0)
    up1, down1 = pack_x(rows_s, 36, 2, pairs_s, 1)
    pack_y(sp, (3, 1, 5), [], 1)
    halos1 = halo_set(1, up1, down1, 4)
    for c in halos1:
        c.start()

    over(GY, me_y, lambda peer: a2(me_y, peer).wait_recv())

    def spread(i, carry):
        at = pl.ds(pl.multiple_of(16 * i, 16), 16)
        rows = tab[at, :]
        ly = iota((16, CY), 1) - rows[:, YS : YS + 1].astype(jnp.int32)
        lx = rows[:, XS : XS + 1].astype(jnp.int32)
        ok_y = (ly >= 0) & (ly < FOOT)
        for x in range(CX):
            a = x - lx
            ok = ok_y & ((a >= 0) & (a < FOOT))
            picked = jnp.take_along_axis(rows, jnp.where(ok, a * FOOT + ly, 0), axis=1, mode="promise_in_bounds")
            hi, lo = split(jnp.where(ok, picked, 0.0))
            gh[x, at, :] = hi
            gl[x, at, :] = lo
        return carry

    lax.fori_loop(0, 16, spread, 0)
    params = [jnp.transpose(tab[pl.ds(128 * i, 128), :])[64:96] for i in range(2)]
    params = jnp.concatenate(params, axis=1)
    r0, c0, q0, p0 = (params[8 * i : 8 * i + 8] for i in range(4))

    def motion():
        for f in range(3):
            surf[pl.ds(f, CX, stride=8), :] = vp[f, 2, 8:24, :]
        upper_, lower_ = jnp.zeros((16, 256), F32), jnp.zeros((16, 256), F32)
        for x in range(CX):
            hi, lo = split(surf[8 * x : 8 * x + 8, :])
            both = jnp.concatenate([hi.astype(F32), lo.astype(F32)], axis=0).astype(BF16)
            upper_ = upper_ + mm(both, gh[x], ((1,), (1,)), None)
            lower_ = lower_ + mm(both, gl[x], ((1,), (1,)), None)
        return upper_[0:8] + upper_[8:16] + lower_[0:8]

    def push(reaction):
        hi, lo = split(reaction * (DT * FOOT))
        both = jnp.concatenate([hi.astype(F32), lo.astype(F32)], axis=0).astype(BF16)
        for x in range(CX):
            upper_ = mm(both, gh[x], ((1,), (0,)), None)
            lower_ = mm(both, gl[x], ((1,), (0,)), None)
            forc[8 * x : 8 * x + 8, :] = upper_[0:8] + upper_[8:16] + lower_[0:8]

    def add_push():
        for f in range(3):
            vp[f, 2, 8:24, :] += forc[pl.ds(f, CX, stride=8), :]

    def m1(step, peer, slot):
        return pltpu.make_async_remote_copy(
            src_ref=bm_s.at[step, lax.div(peer, 4)],
            dst_ref=m_r.at[step, slot],
            send_sem=m1s.at[step, peer],
            recv_sem=m1r.at[step, slot],
            device_id={"gx": me_x, "gy": peer},
            device_id_type=MESH,
        )

    def m2(step, peer, slot):
        return pltpu.make_async_remote_copy(
            src_ref=m_p.at[step],
            dst_ref=m_q.at[step, slot],
            send_sem=m2s.at[step, peer],
            recv_sem=m2r.at[step, slot],
            device_id={"gx": peer, "gy": me_y},
            device_id_type=MESH,
        )

    def send_motion(step, value):
        bm_s[step, 0] = value[:, 0:128]
        bm_s[step, 1] = value[:, 128:256]
        over(GY, me_y, lambda peer: m1(step, peer, me_y).start())
        m_r[step, me_y] = bm_s[step, lax.div(me_y, 4)]

    def pass_motion(step):
        over(GY, me_y, lambda peer: m1(step, me_y, peer).wait_recv())
        offset = 32 * lax.rem(me_y, 4)
        total = jnp.zeros((8, CY), F32)
        for j in range(GY):
            value = pltpu.roll(m_r[step, j], lax.rem(32 * (j // 2) - offset + CY, CY), 1)
            if j % 2:
                value = pltpu.roll(value, 4, 0)
            want = (row8 // 4 == j % 2) & (lane8 // 32 == j // 2)
            total = jnp.where(want, value, total)
        m_p[step] = total
        over(GX, me_x, lambda peer: m2(step, peer, me_x).start())
        m_q[step, me_x] = total

    own_xc = jnp.floor((own_col + 0.5) * (1.0 / GY))
    own_yc = own_col - GY * own_xc
    half = jnp.floor(own_yc * 0.5)
    want_lane = half * 32.0 + pos_col + 2.0 * me_x.astype(F32)
    want_row = own_xc * 2.0 + (own_yc - 2.0 * half)

    def take_motion(step):
        over(GX, me_x, lambda peer: m2(step, me_x, peer).wait_recv())
        where_ = (lane.astype(F32) == want_lane).astype(F32)
        found = mm(where_, m_q[step].reshape(128, CY), ((1,), (1,)))
        found = jnp.where((lane // 4).astype(F32) == want_row, found, 0.0)
        onto = (iota((CY, DOF), 0) % 4 == iota((CY, DOF), 1) % 3).astype(F32)
        return mm(found, onto, ((1,), (0,)))

    bm1 = motion()
    send_motion(0, bm1)
    push(r0 - c0 * bm1)

    for c in halos1:
        c.wait_recv()
    unpack_x(rows_s, 36, 2, pairs_s, 1)
    unpack_y(1)
    lax.fori_loop(0, NZ, velocity_layer, 0)
    add_push()

    up2, down2 = pack_x(rows_v, 36, 2, pairs_v, 2)
    pack_y(vp, (0, 1, 2), [], 2)
    halos2 = halo_set(2, up2, down2, 8)
    for c in halos2:
        c.start()

    bm2 = motion()
    send_motion(1, bm2)
    pass_motion(0)
    push(p0 + q0 * bm1 - c0 * bm2)
    pass_motion(1)

    for c in halos2:
        c.wait_recv()
    unpack_x(rows_v, 36, 2, pairs_v, 2)
    unpack_y(2)
    lax.fori_loop(0, NZ, stress_layer, 0)
    up3, down3 = pack_x(rows_s, 36, 2, pairs_s, 3)
    pack_y(sp, (3, 1, 5), [], 3)
    halos3 = halo_set(3, up3, down3, 12)
    for c in halos3:
        c.start()

    def advance(rates, drifts, restoring, base):
        relative = jnp.where(mask, rates - base, 0.0)
        rates = jnp.where(mask, rates - DT * restoring - DT * coupling * relative, 0.0)
        return rates, jnp.where(mask, drifts + DT * rates, 0.0)

    rate1, drift1 = advance(rate0, drift0, rest0, take_motion(0))
    restore(drift1, False)
    rate2, drift2 = advance(rate1, drift1, rest[...], take_motion(1))
    bd[0] = drift2
    bd[1] = rate2
    stores = [
        pltpu.make_async_copy(bd.at[0], odrift, st.at[0]),
        pltpu.make_async_copy(bd.at[1], orate, st.at[1]),
    ]
    for c in stores:
        c.start()

    for c in halos3:
        c.wait_recv()
    unpack_x(rows_s, 36, 2, pairs_s, 3)
    unpack_y(3)
    lax.fori_loop(0, NZ, velocity_layer, 0)
    add_push()
    stores.append(pltpu.make_async_copy(vp.at[:, pl.ds(2, NZ), pl.ds(8, CX), :], ovel, st.at[2]))
    stores[2].start()

    for c in halos0 + halos1 + halos2 + halos3:
        c.wait_send()
    over(GX, me_x, lambda peer: a1(peer, me_x).wait_send())
    over(GY, me_y, lambda peer: a2(peer, me_y).wait_send())
    for step in range(2):
        over(GY, me_y, lambda peer: m1(step, peer, me_y).wait_send())
        over(GX, me_x, lambda peer: m2(step, peer, me_x).wait_send())
    for c in stores:
        c.wait()


def body(vel, stress, buoy, lame, shear, stiff, drift, rate, coup, contact, dof, owner, corner):
    anywhere = pl.BlockSpec(memory_space=pl.ANY)
    vmem = pltpu.VMEM
    dma = pltpu.SemaphoreType.DMA
    return pl.pallas_call(
        kernel,
        out_shape=(
            jax.ShapeDtypeStruct((3, NZ, CX, CY), F32),
            jax.ShapeDtypeStruct((NB, DOF), F32),
            jax.ShapeDtypeStruct((NB, DOF), F32),
        ),
        in_specs=[anywhere] * 13,
        out_specs=(anywhere,) * 3,
        scratch_shapes=[
            vmem((3, 36, 32, CY), F32),
            vmem((6, 36, 32, CY), F32),
            vmem((2, 34, 32, CY), F32),
            vmem((NZ, CX, CY), F32),
            vmem((6, NZ, CX, CY), F32),
            vmem((3, NZ, CX, CY), F32),
            vmem((2, 34, 32, CY), F32),
            vmem((NB, DOF, DOF), BF16),
            vmem((3, NB, DOF), F32),
            vmem((NB, 64), F32),
            vmem((1, NB), jnp.int32),
            vmem((NB, 1), jnp.int32),
            vmem((1, NB), jnp.int32),
            vmem((256, CY), F32),
            vmem((256, CY), F32),
            vmem((256, CY), F32),
            vmem((256, CY), F32),
            vmem((CX, 256, CY), BF16),
            vmem((CX, 256, CY), BF16),
            vmem((128, CY), F32),
            vmem((128, CY), F32),
            vmem((2, 2, 8, CY), F32),
            vmem((2, GY, 8, CY), F32),
            vmem((2, 8, CY), F32),
            vmem((2, GX, 8, CY), F32),
            vmem((NB, DOF), F32),
            vmem((NB, DOF), BF16),
            vmem((4, 2, 224, CY), F32),
            vmem((4, 2, 224, CY), F32),
            vmem((4, 2, 8, ROWS), F32),
            vmem((4, 3, 8, ROWS), F32),
            dma((12,)),
            dma((4,)),
            dma((3,)),
            dma((GX,)),
            dma((GX,)),
            dma((GY,)),
            dma((GY,)),
            dma((2, GY)),
            dma((2, GY)),
            dma((2, GX)),
            dma((2, GX)),
            dma((17,)),
            dma((17,)),
        ],
        compiler_params=pltpu.CompilerParams(
            collective_id=0, has_side_effects=True, vmem_limit_bytes=60 * 1024 * 1024
        ),
    )(
        vel, stress, buoy, lame, shear, stiff, drift, rate, coup, contact,
        dof.reshape(1, NB), owner, corner.reshape(1, NB),
    )


def solution(mesh):
    placed = (
        P(None, None, "gx", "gy"),
        P(None, None, "gx", "gy"),
        P(None, "gx", "gy"),
        P(None, "gx", "gy"),
        P(None, "gx", "gy"),
        P(("gx", "gy"), None, None),
        P(("gx", "gy"), None),
        P(("gx", "gy"), None),
        P(("gx", "gy"), None),
        P(("gx", "gy"), None),
        P(("gx", "gy")),
        P(("gx", "gy"), None),
        P(("gx", "gy")),
    )
    return jax.shard_map(
        body,
        mesh=mesh,
        in_specs=placed,
        out_specs=(P(None, None, "gx", "gy"), P(("gx", "gy"), None), P(("gx", "gy"), None)),
        check_vma=False,
    )
```

```python
import jax
import jax.numpy as jnp
from jax import lax
from jax.experimental import pallas as pl
from jax.experimental.pallas import tpu as pltpu
from jax.sharding import PartitionSpec as P

MESH = pl.DeviceIdType.MESH
F32 = jnp.float32
BF16 = jnp.bfloat16
DT = 0.3
INNER = 9.0 / 8.0
OUTER = 1.0 / 24.0
FOOT = 8
GX, GY = 16, 8
NZ, CX, CY = 32, 16, 128
NB, DOF = 64, 256
SPAN = CY - FOOT + 1
ROWS = NZ * CX
GROUP = 4
R0, CC, QQ, YS = 0, 8, 16, 24


def iota(shape, dim):
    return lax.broadcasted_iota(jnp.int32, shape, dim)


def mm(a, b, dims):
    return lax.dot_general(a, b, (dims, ((), ())), preferred_element_type=F32)


def split(x):
    hi = x.astype(BF16)
    return hi, (x - hi.astype(F32)).astype(BF16)


NN, NT = ((1,), (0,)), ((1,), (1,))


def pick_lhs(exact, value, dims):
    hi, lo = split(value)
    exact = exact.astype(BF16)
    return mm(exact, hi, dims) + mm(exact, lo, dims)


def pick_rhs(value, exact, dims):
    hi, lo = split(value)
    exact = exact.astype(BF16)
    return mm(hi, exact, dims) + mm(lo, exact, dims)


def kernel(
    vel, stress, buoy, lame, shear, stiff, drift, rate, coup, contact, dof, owner, corner,
    ovel, odrift, orate,
    vp, sp, mp, lam, av, kk, bd, ct, dofv, ownv, corv,
    send_a, recv_a, send_b, tab, send_c, recv_c, send_d, tab_p, wxt, forc,
    bm_s, m_r, m_p, m_q, rest, bds,
    b0, r0b, b1, r1b, b2, r2b, b3, r3b,
    ld, ldk, xa, xm, hs, hr,
):
    me_x = lax.axis_index("gx")
    me_y = lax.axis_index("gy")

    def wrap(value, n):
        return lax.rem(value + n, n)

    east, west = wrap(me_x + 1, GX), wrap(me_x - 1, GX)
    north, south = wrap(me_y + 1, GY), wrap(me_y - 1, GY)

    inner = (pl.ds(2, NZ), pl.ds(8, CX), slice(None))
    loads = [
        pltpu.make_async_copy(contact, ct, ld.at[0]),
        pltpu.make_async_copy(dof, dofv, ld.at[1]),
        pltpu.make_async_copy(owner, ownv, ld.at[2]),
        pltpu.make_async_copy(corner, corv, ld.at[3]),
        pltpu.make_async_copy(drift, bd.at[0], ld.at[4]),
        pltpu.make_async_copy(rate, bd.at[1], ld.at[5]),
        pltpu.make_async_copy(coup, bd.at[2], ld.at[6]),
        pltpu.make_async_copy(vel, vp.at[(slice(None),) + inner], ld.at[7]),
        pltpu.make_async_copy(buoy, mp.at[0, pl.ds(0, NZ), pl.ds(8, CX), :], ld.at[8]),
        pltpu.make_async_copy(shear, mp.at[1, pl.ds(0, NZ), pl.ds(8, CX), :], ld.at[9]),
        pltpu.make_async_copy(lame, lam, ld.at[10]),
        pltpu.make_async_copy(stress, sp.at[(slice(None),) + inner], ld.at[11]),
    ]
    kloads = [
        pltpu.make_async_copy(stiff.at[pl.ds(16 * i, 16)], kk.at[pl.ds(16 * i, 16)], ldk.at[i])
        for i in range(4)
    ]
    for c in loads[:10] + kloads + loads[10:]:
        c.start()

    barrier = pltpu.get_barrier_semaphore()

    def greet(gx, gy):
        pl.semaphore_signal(barrier, inc=1, device_id={"gx": gx, "gy": gy}, device_id_type=MESH)

    for d in range(1, GX):
        greet(wrap(me_x + d, GX), me_y)
    for d in range(1, GY):
        greet(me_x, wrap(me_y + d, GY))
    greet(west, south)
    greet(east, north)

    zero = jnp.zeros((2, 32, CY), F32)
    for f in range(3):
        vp[f, 0:2] = zero
        vp[f, 34:36] = zero
    for f in (2, 4, 5):
        sp[f, 0:2] = zero
        sp[f, 34:36] = zero
    mp[0, NZ] = zero[0]
    mp[1, NZ] = zero[0]

    rows_v = vp.reshape(3 * 36 * 32, CY)
    rows_s = sp.reshape(6 * 36 * 32, CY)
    rows_m = mp.reshape(2 * 34 * 32, CY)
    lane16, row16 = iota((CX, CY), 1), iota((CX, CY), 0)
    row8, lane8 = iota((8, CY), 0), iota((8, CY), 1)

    def layer_rows(ref, field, depth, first, row):
        return ref[pl.ds((field * depth + first) * 32 + row, NZ, stride=32), :]

    def put_rows(ref, field, depth, first, row, value):
        ref[pl.ds((field * depth + first) * 32 + row, NZ, stride=32), :] = value

    keep_w = (me_x > 0).astype(F32)
    keep_e = (me_x < GX - 1).astype(F32)
    keep_s = (me_y > 0).astype(F32)
    keep_n = (me_y < GY - 1).astype(F32)

    pairs_v = [(0, 2, 1), (1, 1, 2), (2, 1, 2)]
    pairs_s = [(0, 1, 2), (3, 2, 1), (4, 2, 1)]

    def pack_x(ref, pairs, buf):
        at = 0
        for field, before, _ in pairs:
            for i in range(before):
                buf[pl.ds(at, 32), :] = layer_rows(ref, field, 36, 2, 8 + CX - before + i)
                at += 32
        for field, _, after in pairs:
            for i in range(after):
                buf[pl.ds(at, 32), :] = layer_rows(ref, field, 36, 2, 8 + i)
                at += 32

    def unpack_x(ref, pairs, buf):
        at = 0
        for field, before, _ in pairs:
            for i in range(before):
                put_rows(ref, field, 36, 2, 8 - before + i, buf[pl.ds(at, 32), :] * keep_w)
                at += 32
        for field, _, after in pairs:
            for i in range(after):
                put_rows(ref, field, 36, 2, 8 + CX + i, buf[pl.ds(at, 32), :] * keep_e)
                at += 32

    def pack_layer(total, value, k):
        return jnp.where(lane16 // 4 == k, pltpu.roll(value, 4 * k + 2, 1), total)

    def halo_of(packed, k):
        return pltpu.roll(packed, CY - 2 - 4 * k, 1)

    def merge_y(buf, at):
        from_south = buf[pl.ds(at[0], CX), :] * keep_s
        return jnp.where(lane16 % 4 >= 2, buf[pl.ds(at[1], CX), :] * keep_n, from_south)

    def halo_set(slot, buf, rbuf, up, down, ny, extra=None):
        def copy(at, to, n, gx, gy):
            return pltpu.make_async_remote_copy(
                src_ref=buf.at[pl.ds(at, n)],
                dst_ref=rbuf.at[pl.ds(to, n)],
                send_sem=hs.at[slot],
                recv_sem=hr.at[slot],
                device_id={"gx": gx, "gy": gy},
                device_id_type=MESH,
            )

        y = up + down
        out = [
            copy(0, 0, up, east, me_y),
            copy(up, up, down, west, me_y),
            copy(y, y, ny, me_x, north),
            copy(y, y + ny, ny, me_x, south),
        ]
        if extra is not None:
            out.append(copy(extra[0], extra[1], CX, west, south))
        return out

    def whole(slot, rbuf):
        return pltpu.make_async_remote_copy(
            src_ref=rbuf,
            dst_ref=rbuf,
            send_sem=hs.at[slot],
            recv_sem=hr.at[slot],
            device_id={"gx": east, "gy": me_y},
            device_id_type=MESH,
        )

    for i in range(7):
        loads[i].wait()
    eye = iota((NB, NB), 0) == iota((NB, NB), 1)

    def to_col(row):
        return jnp.sum(jnp.where(eye, jnp.broadcast_to(row, (NB, NB)), 0.0), axis=1, keepdims=True)

    dof_col = to_col(dofv[...].astype(F32))
    cor_col = to_col(corv[...].astype(F32))
    own_row = ownv[...].astype(F32)
    own_col = to_col(own_row)
    same = jnp.broadcast_to(own_col, (NB, NB)) == jnp.broadcast_to(own_row, (NB, NB))
    upper = iota((NB, NB), 0) < iota((NB, NB), 1)
    lower = iota((NB, NB), 0) > iota((NB, NB), 1)
    pos_row = jnp.sum(jnp.where(same & upper, 1.0, 0.0), axis=0, keepdims=True)
    pos_col = jnp.sum(jnp.where(same & lower, 1.0, 0.0), axis=1, keepdims=True)
    mask = iota((NB, DOF), 1).astype(F32) < dof_col
    cpl = jnp.where(mask, bd[2], 0.0)
    rate0 = jnp.where(mask, bd[1], 0.0)
    drift0 = jnp.where(mask, bd[0], 0.0)

    def gather_dofs(value, lane):
        want = (iota((DOF, CY), 0) % 3 + lane) == iota((DOF, CY), 1)
        return pick_rhs(value, want.astype(F32), NN)

    lane = iota((NB, CY), 1)
    start_x = jnp.floor((cor_col + 0.5) * (1.0 / SPAN))
    start_y = cor_col - SPAN * start_x
    weights = ct[...] / jnp.sum(ct[...], axis=1, keepdims=True)
    cell, to = iota((64, CY), 0), iota((64, CY), 1)
    turned = (cell % FOOT == to // CX) & (cell // FOOT == to % CX)
    placed = pick_rhs(weights, turned.astype(F32), NN)
    shift = jnp.broadcast_to(start_x, (NB, CY)).astype(jnp.int32)
    for bit in (1, 2, 4, 8):
        placed = jnp.where((shift & bit) != 0, pltpu.roll(placed, bit, 1), placed)
    info = gather_dofs(cpl * rate0, R0) + gather_dofs(cpl, CC) + gather_dofs(DT * cpl * cpl, QQ)
    info = jnp.where(lane == YS, start_y, info)
    own_x = jnp.floor((own_row + 0.5) * (1.0 / GY))
    dest = own_row + 8.0 * own_x + 8.0 * pos_row
    route = (iota((256, NB), 0).astype(F32) == dest).astype(F32)
    send_a[:, 0:16, :] = pick_lhs(route, placed, NN).reshape(GX, 16, CY)
    send_a[:, 16:32, :] = pick_lhs(route, info, NN).reshape(GX, 16, CY)

    for i in range(7, 10):
        loads[i].wait()
    pack_x(rows_v, pairs_v, b0)
    for f in range(2):
        b0[pl.ds(288 + 32 * f, 32), :] = layer_rows(rows_m, f, 34, 0, 8)
    sources = [lambda k, f=f: vp[f, k + 2, 8:24, :] for f in range(3)]
    sources += [lambda k, f=f: mp[f, k, 8:24, :] for f in range(2)]
    for i, source in enumerate(sources):
        total = jnp.zeros((CX, CY), F32)
        for k in range(NZ):
            total = pack_layer(total, source(k), k)
        b0[pl.ds(352 + 16 * i, 16), :] = total
    halos0 = halo_set(0, b0, r0b, 128, 224, 80, (352 + 64, 352 + 160))

    pl.semaphore_wait(barrier, GX + GY)
    for c in halos0:
        c.start()

    def along(src, dst, sems, base, gx, gy):
        return pltpu.make_async_remote_copy(
            src_ref=src,
            dst_ref=dst,
            send_sem=sems.at[base],
            recv_sem=sems.at[base + 1],
            device_id={"gx": gx, "gy": gy},
            device_id_type=MESH,
        )

    def over(n, me, action):
        def one(d, carry):
            action(wrap(me + d, n))
            return carry

        lax.fori_loop(1, n, one, 0)

    def to_gx(src, dst, base):
        over(GX, me_x, lambda peer: along(src.at[peer], dst.at[me_x], xa, base, peer, me_y).start())
        dst[me_x] = src[me_x]

    def to_gy(src, dst, base):
        over(GY, me_y, lambda peer: along(src.at[peer], dst.at[me_y], xa, base, me_x, peer).start())
        dst[me_y] = src[me_y]

    def all_of(ref, sems, base):
        n = ref.shape[0] - 1
        return along(ref.at[pl.ds(0, n)], ref.at[pl.ds(0, n)], sems, base, east, me_y)

    to_gx(send_a, recv_a, 0)

    def restore(value):
        bds[...] = value.astype(BF16)

        def block(i, carry):
            mine = bds[pl.ds(pl.multiple_of(16 * i, 16), 16), :]
            row = iota((16, DOF), 0)
            total = jnp.zeros((16, DOF), F32)
            for b in range(16):
                part = mm(mine, kk[16 * i + b], NT)
                total = jnp.where(row == b, part, total)
            rest[pl.ds(pl.multiple_of(16 * i, 16), 16), :] = total
            return carry

        lax.fori_loop(0, 4, block, 0)

    for c in kloads:
        c.wait()
    restore(drift0)
    rest0 = rest[...]

    moved = rate0 - DT * rest0 - DT * cpl * rate0
    send_c[...] = pick_lhs(route, gather_dofs(cpl * moved, 0), NN).reshape(GX, 16, CY)
    to_gx(send_c, recv_c, 4)

    whole(0, r0b).wait_recv()
    unpack_x(rows_v, pairs_v, r0b)
    for f in range(2):
        put_rows(rows_m, f, 34, 0, 24, r0b[pl.ds(288 + 32 * f, 32), :])
    packed_v = [merge_y(r0b, (352 + 16 * f, 432 + 16 * f)) for f in range(3)]
    packed_b = r0b[pl.ds(432 + 48, CX), :]
    packed_m = r0b[pl.ds(432 + 64, CX), :]
    corner_m = jnp.broadcast_to(r0b[pl.ds(512, 8), :][0:1, :], (CX, CY))
    packed_e = jnp.where(row16 == CX - 1, corner_m, pltpu.roll(packed_m, CX - 1, 0))

    out_x = (row16 == CX - 1) & (me_x == GX - 1)
    out_y = (lane16 == CY - 1) & (me_y == GY - 1)
    out_xy = out_x | out_y

    def shifted(value, halo, step):
        if step > 0:
            return pltpu.roll(jnp.where(lane16 < step, halo, value), CY - step, 1)
        return pltpu.roll(jnp.where(lane16 >= CY + step, halo, value), -step, 1)

    def average(k, my):
        last = k == NZ - 1
        b, m = mp[0, k, 8:24, :], mp[1, k, 8:24, :]
        bx = jnp.where(out_x, b, mp[0, k, 9:25, :])
        by = jnp.where(out_y, b, shifted(b, halo_of(packed_b, k), 1))
        bz = jnp.where(last, b, mp[0, k + 1, 8:24, :])
        east_m = mp[1, k, 9:25, :]
        mx = jnp.where(out_x, m, east_m)
        mxy = jnp.where(out_xy, m, shifted(east_m, halo_of(packed_e, k), 1))
        mz = mp[1, k + 1, 8:24, :]
        mxz = jnp.where(out_x | last, m, mp[1, k + 1, 9:25, :])
        raw = shifted(mz, halo_of(packed_m, wrap(k + 1, NZ)), 1)
        myz = jnp.where(out_y | last, m, raw)
        mz = jnp.where(last, m, mz)
        my = jnp.where(out_y, m, my)
        av[0, k] = (b + bx) * (0.5 * DT)
        av[1, k] = (b + by) * (0.5 * DT)
        av[2, k] = (b + bz) * (0.5 * DT)
        av[3, k] = (m + mx + my + mxy) * (0.25 * DT)
        av[4, k] = (m + mx + mz + mxz) * (0.25 * DT)
        av[5, k] = (m + my + mz + myz) * (0.25 * DT)
        return raw

    def layers(action, init, first=0):
        def group(i, carry):
            for j in range(GROUP):
                carry = action(GROUP * i + j, carry)
            return carry

        return lax.fori_loop(first, NZ // GROUP, group, init)

    layers(average, shifted(mp[1, 0, 8:24, :], halo_of(packed_m, 0), 1))

    def fwd(minus, zero_, plus, plus2):
        return INNER * (plus - zero_) - OUTER * (plus2 - minus)

    def bwd(minus2, minus, zero_, plus):
        return INNER * (zero_ - minus) - OUTER * (plus - minus2)

    def dx(ref, f, k, forward):
        first = 7 if forward else 6
        parts = [ref[f, k + 2, first + i : first + i + CX, :] for i in range(4)]
        return (fwd if forward else bwd)(*parts)

    def dz(ref, f, k, forward):
        first = 1 if forward else 0
        parts = [ref[f, k + first + i, 8:24, :] for i in range(4)]
        return (fwd if forward else bwd)(*parts)

    def dy(ref, f, packed, k, forward):
        value, halo = ref[f, k + 2, 8:24, :], halo_of(packed, k)
        if forward:
            return fwd(shifted(value, halo, -1), value, shifted(value, halo, 1), shifted(value, halo, 2))
        return bwd(shifted(value, halo, -2), shifted(value, halo, -1), value, shifted(value, halo, 1))

    def stress_layer(halos, k, carry):
        sx, sy, sz = dx(vp, 0, k, False), dy(vp, 1, halos[1], k, False), dz(vp, 2, k, False)
        m2 = (2.0 * DT) * mp[1, k, 8:24, :]
        volume = (DT * lam[k]) * (sx + sy + sz)
        new = {}
        for f, s in ((0, sx), (1, sy), (2, sz)):
            new[f] = sp[f, k + 2, 8:24, :] + (volume + m2 * s)
        new[3] = sp[3, k + 2, 8:24, :] + av[3, k] * (
            dy(vp, 0, halos[0], k, True) + dx(vp, 1, k, True)
        )
        new[4] = sp[4, k + 2, 8:24, :] + av[4, k] * (dz(vp, 0, k, True) + dx(vp, 2, k, True))
        new[5] = sp[5, k + 2, 8:24, :] + av[5, k] * (
            dz(vp, 1, k, True) + dy(vp, 2, halos[2], k, True)
        )
        for f in range(6):
            sp[f, k + 2, 8:24, :] = new[f]
        return tuple(pack_layer(t, new[f], k) for t, f in zip(carry, (3, 1, 5)))

    def velocity_layer(halos, out, surface, k, carry):
        ax = dx(sp, 0, k, True) + dy(sp, 3, halos[0], k, False) + dz(sp, 4, k, False)
        ay = dx(sp, 3, k, False) + dy(sp, 1, halos[1], k, True) + dz(sp, 5, k, False)
        az = dx(sp, 4, k, False) + dy(sp, 5, halos[2], k, False) + dz(sp, 2, k, True)
        new = []
        for f, a in ((0, ax), (1, ay), (2, az)):
            value = vp[f, k + 2, 8:24, :] + av[f, k] * a
            if surface:
                value = value + forc[f]
            new.append(value)
            if out is None:
                vp[f, k + 2, 8:24, :] = value
            else:
                out[f, k] = value
        return tuple(pack_layer(t, v, k) for t, v in zip(carry, new)) if carry else carry

    def stress_step(halos, buf, at):
        blank = (jnp.zeros((CX, CY), F32),) * 3
        packed = layers(lambda k, c: stress_layer(halos, k, c), blank)
        for f in range(3):
            buf[pl.ds(at + 16 * f, 16), :] = packed[f]

    def velocity_step(halos, out, buf, at):
        carry = () if buf is None else (jnp.zeros((CX, CY), F32),) * 3
        for k in range(GROUP):
            carry = velocity_layer(halos, out, k == 0, k, carry)
        carry = layers(lambda k, c: velocity_layer(halos, out, False, k, c), carry, 1)
        if buf is not None:
            for f in range(3):
                buf[pl.ds(at + 16 * f, 16), :] = carry[f]

    loads[10].wait()
    loads[11].wait()
    stress_step(packed_v, b1, 288)
    pack_x(rows_s, pairs_s, b1)
    halos1 = halo_set(1, b1, r1b, 160, 128, 48)
    for c in halos1:
        c.start()

    all_of(recv_a, xa, 0).wait_recv()
    for j in range(GY):
        for i in range(4):
            send_b[j, pl.ds(16 * i, 16), :] = recv_a.reshape(GX * 32, CY)[
                pl.ds(8 * i + j, GX, stride=32), :
            ]
    to_gy(send_b, tab, 2)
    all_of(recv_c, xa, 4).wait_recv()
    for j in range(GY):
        for i in range(2):
            send_d[j, pl.ds(16 * i, 16), :] = recv_c.reshape(GX * 16, CY)[
                pl.ds(8 * i + j, GX, stride=16), :
            ]
    to_gy(send_d, tab_p, 6)

    all_of(tab, xa, 2).wait_recv()
    for i in range(2):
        block = tab[4 * i : 4 * i + 4, 0:32, :].reshape(128, CY)
        wxt[:, 128 * i : 128 * i + 128] = jnp.transpose(block)
    params = [jnp.transpose(tab[4 * i : 4 * i + 4, 32:64, :].reshape(128, CY))[0:32] for i in range(2)]
    params = jnp.concatenate(params, axis=1)
    r0, c0, q0, y0 = (params[8 * i : 8 * i + 8] for i in range(4))
    oyt = (iota((CY, 256), 0).astype(F32) == y0[0:1]).astype(F32).astype(BF16)

    def motion():
        total = jnp.zeros((8, 256), F32)
        row = iota((8, 256), 0)
        for f in range(3):
            value = vp[f, 2, 8:24, :]
            turns = [value] + [pltpu.roll(value, CY - c, 1) for c in range(1, FOOT)]
            hi, lo = split(jnp.concatenate(turns, axis=0))
            found = mm(hi, oyt, NN) + mm(lo, oyt, NN)
            one = jnp.sum(found * wxt[...], axis=0, keepdims=True)
            total = jnp.where(row == f, jnp.broadcast_to(one, (8, 256)), total)
        return total

    def push(reaction):
        reaction = reaction * (DT * FOOT)
        for f in range(3):
            hi, lo = split(wxt[...] * reaction[f : f + 1])
            spread = mm(hi, oyt, NT) + mm(lo, oyt, NT)
            total = spread[0:CX]
            for c in range(1, FOOT):
                total = total + pltpu.roll(spread[CX * c : CX * c + CX], c, 1)
            forc[f] = total

    def send_motion(step, value):
        bm_s[step, 0] = value[:, 0:128]
        bm_s[step, 1] = value[:, 128:256]
        over(
            GY,
            me_y,
            lambda peer: along(
                bm_s.at[step, lax.div(peer, 4)], m_r.at[step, me_y], xm, 4 * step, me_x, peer
            ).start(),
        )
        m_r[step, me_y] = bm_s[step, lax.div(me_y, 4)]

    def pass_motion(step):
        all_of(m_r.at[step], xm, 4 * step).wait_recv()
        offset = 32 * lax.rem(me_y, 4)
        total = jnp.zeros((8, CY), F32)
        for j in range(GY):
            value = pltpu.roll(m_r[step, j], lax.rem(32 * (j // 2) - offset + CY, CY), 1)
            if j % 2:
                value = pltpu.roll(value, 4, 0)
            want = (row8 // 4 == j % 2) & (lane8 // 32 == j // 2)
            total = jnp.where(want, value, total)
        m_p[step] = total
        over(
            GX,
            me_x,
            lambda peer: along(
                m_p.at[step], m_q.at[step, me_x], xm, 4 * step + 2, peer, me_y
            ).start(),
        )
        m_q[step, me_x] = total

    own_xc = jnp.floor((own_col + 0.5) * (1.0 / GY))
    own_yc = own_col - GY * own_xc
    half = jnp.floor(own_yc * 0.5)
    want_lane = half * 32.0 + pos_col * 16.0 + me_x.astype(F32)
    want_row = own_xc * 2.0 + (own_yc - 2.0 * half)

    def take_motion(step):
        all_of(m_q.at[step], xm, 4 * step + 2).wait_recv()
        where_ = (lane.astype(F32) == want_lane).astype(F32)
        found = pick_lhs(where_, m_q[step].reshape(128, CY), NT)
        found = jnp.where((lane // 4).astype(F32) == want_row, found, 0.0)
        onto = (iota((CY, DOF), 0) % 4 == iota((CY, DOF), 1) % 3).astype(F32)
        return pick_rhs(found, onto, NN)

    bm1 = motion()
    send_motion(0, bm1)
    push(r0 - c0 * bm1)

    whole(1, r1b).wait_recv()
    unpack_x(rows_s, pairs_s, r1b)
    packed_s = [merge_y(r1b, (288 + 16 * f, 336 + 16 * f)) for f in range(3)]
    velocity_step(packed_s, None, b2, 288)
    pack_x(rows_v, pairs_v, b2)
    halos2 = halo_set(2, b2, r2b, 128, 160, 48)
    for c in halos2:
        c.start()

    bm2 = motion()
    send_motion(1, bm2)
    pass_motion(0)
    all_of(tab_p, xa, 6).wait_recv()
    p0 = [jnp.transpose(tab_p[4 * i : 4 * i + 4].reshape(128, CY))[0:8] for i in range(2)]
    push(jnp.concatenate(p0, axis=1) + q0 * bm1 - c0 * bm2)

    whole(2, r2b).wait_recv()
    unpack_x(rows_v, pairs_v, r2b)
    packed_v = [merge_y(r2b, (288 + 16 * f, 336 + 16 * f)) for f in range(3)]
    stress_step(packed_v, b3, 288)
    pack_x(rows_s, pairs_s, b3)
    halos3 = halo_set(3, b3, r3b, 160, 128, 48)
    for c in halos3:
        c.start()

    pass_motion(1)

    def advance(rates, drifts, restoring, base):
        relative = jnp.where(mask, rates - base, 0.0)
        rates = jnp.where(mask, rates - DT * restoring - DT * cpl * relative, 0.0)
        return rates, jnp.where(mask, drifts + DT * rates, 0.0)

    rate1, drift1 = advance(rate0, drift0, rest0, take_motion(0))
    restore(drift1)

    whole(3, r3b).wait_recv()
    unpack_x(rows_s, pairs_s, r3b)
    packed_s = [merge_y(r3b, (288 + 16 * f, 336 + 16 * f)) for f in range(3)]
    velocity_step(packed_s, ovel, None, 0)
    rate2, drift2 = advance(rate1, drift1, rest[...], take_motion(1))
    odrift[...] = drift2
    orate[...] = rate2

    for slot, rbuf in enumerate((r0b, r1b, r2b, r3b)):
        whole(slot, rbuf).wait_send()
    for ref, base in ((recv_a, 0), (tab, 2), (recv_c, 4), (tab_p, 6)):
        all_of(ref, xa, base).wait_send()
    for step in range(2):
        all_of(m_r.at[step], xm, 4 * step).wait_send()
        all_of(m_q.at[step], xm, 4 * step + 2).wait_send()


def body(vel, stress, buoy, lame, shear, stiff, drift, rate, coup, contact, dof, owner, corner):
    anywhere = pl.BlockSpec(memory_space=pltpu.HBM)
    vmem = pltpu.VMEM
    near = pl.BlockSpec(memory_space=vmem)
    dma = pltpu.SemaphoreType.DMA
    halo = [vmem((512, CY), F32), vmem((528, CY), F32)] + [vmem((336, CY), F32), vmem((384, CY), F32)] * 3
    shapes = ((3, NZ, CX, CY), (NB, DOF), (NB, DOF))
    return pl.pallas_call(
        kernel,
        out_shape=tuple(vmem(s, F32) for s in shapes),
        in_specs=[anywhere] * 13,
        out_specs=(near,) * 3,
        scratch_shapes=[
            vmem((3, 36, 32, CY), F32),
            vmem((6, 36, 32, CY), F32),
            vmem((2, 34, 32, CY), F32),
            vmem((NZ, CX, CY), F32),
            vmem((6, NZ, CX, CY), F32),
            vmem((NB, DOF, DOF), BF16),
            vmem((3, NB, DOF), F32),
            vmem((NB, 64), F32),
            vmem((1, NB), jnp.int32),
            vmem((1, NB), jnp.int32),
            vmem((1, NB), jnp.int32),
            vmem((GX, 32, CY), F32),
            vmem((GX, 32, CY), F32),
            vmem((GY, 64, CY), F32),
            vmem((GY, 64, CY), F32),
            vmem((GX, 16, CY), F32),
            vmem((GX, 16, CY), F32),
            vmem((GY, 32, CY), F32),
            vmem((GY, 32, CY), F32),
            vmem((128, 256), F32),
            vmem((3, CX, CY), F32),
            vmem((2, 2, 8, CY), F32),
            vmem((2, GY, 8, CY), F32),
            vmem((2, 8, CY), F32),
            vmem((2, GX, 8, CY), F32),
            vmem((NB, DOF), F32),
            vmem((NB, DOF), BF16),
            *halo,
            dma((12,)),
            dma((4,)),
            dma((8,)),
            dma((8,)),
            dma((4,)),
            dma((4,)),
        ],
        compiler_params=pltpu.CompilerParams(
            collective_id=0, has_side_effects=True, vmem_limit_bytes=66_100_000
        ),
    )(
        vel, stress, buoy, lame, shear, stiff, drift, rate, coup, contact,
        dof.reshape(1, NB), owner.reshape(1, NB), corner.reshape(1, NB),
    )


def solution(mesh):
    placed = (
        P(None, None, "gx", "gy"),
        P(None, None, "gx", "gy"),
        P(None, "gx", "gy"),
        P(None, "gx", "gy"),
        P(None, "gx", "gy"),
        P(("gx", "gy"), None, None),
        P(("gx", "gy"), None),
        P(("gx", "gy"), None),
        P(("gx", "gy"), None),
        P(("gx", "gy"), None),
        P(("gx", "gy")),
        P(("gx", "gy"), None),
        P(("gx", "gy")),
    )
    return jax.shard_map(
        body,
        mesh=mesh,
        in_specs=placed,
        out_specs=(P(None, None, "gx", "gy"), P(("gx", "gy"), None), P(("gx", "gy"), None)),
        check_vma=False,
    )
```

```python
import jax
import jax.numpy as jnp
from jax import lax
from jax.experimental import pallas as pl
from jax.experimental.pallas import tpu as pltpu
from jax.sharding import PartitionSpec as P

MESH = pl.DeviceIdType.MESH
F32 = jnp.float32
BF16 = jnp.bfloat16
DT = 0.3
INNER = 9.0 / 8.0
OUTER = 1.0 / 24.0
FOOT = 8
GX, GY = 16, 8
NZ, CX, CY = 32, 16, 128
NB, DOF = 64, 256
SPAN = CY - FOOT + 1
ROWS = NZ * CX
GROUP = 4
UNIT = DT / 24.0


def iota(shape, dim):
    return lax.broadcasted_iota(jnp.int32, shape, dim)


def mm(a, b, dims):
    return lax.dot_general(a, b, (dims, ((), ())), preferred_element_type=F32)


def split(x):
    hi = x.astype(BF16)
    return hi, (x - hi.astype(F32)).astype(BF16)


NN, NT = ((1,), (0,)), ((1,), (1,))


def pick_lhs(exact, value, dims):
    hi, lo = split(value)
    exact = exact.astype(BF16)
    return mm(exact, hi, dims) + mm(exact, lo, dims)


def pick_rhs(value, exact, dims):
    hi, lo = split(value)
    exact = exact.astype(BF16)
    return mm(hi, exact, dims) + mm(lo, exact, dims)


def kernel(
    vel, stress, buoy, lame, shear, stiff, drift, rate, coup, contact, dof, owner, corner,
    ovel, odrift, orate,
    vp, sp, mp, lam, av, kk, bd, ct, dofv, ownv, corv,
    dyb, sten, shb, shm,
    send_w, recv_w, send_p, recv_p, send_b, tab, send_q, recv_q, send_d, tab_q, wxt, forc,
    bm_s, m_r, m_p, m_q, rest, bds,
    b0, r0b, b1, r1b, b2, r2b, b3, r3b,
    ld, ldk, xa, xm, hs, hr,
):
    me_x = lax.axis_index("gx")
    me_y = lax.axis_index("gy")

    def wrap(value, n):
        return lax.rem(value + n, n)

    east, west = wrap(me_x + 1, GX), wrap(me_x - 1, GX)
    north, south = wrap(me_y + 1, GY), wrap(me_y - 1, GY)

    inner = (pl.ds(2, NZ), pl.ds(8, CX), slice(None))
    loads = [
        pltpu.make_async_copy(contact, ct, ld.at[0]),
        pltpu.make_async_copy(dof, dofv, ld.at[1]),
        pltpu.make_async_copy(owner, ownv, ld.at[2]),
        pltpu.make_async_copy(corner, corv, ld.at[3]),
        pltpu.make_async_copy(drift, bd.at[0], ld.at[4]),
        pltpu.make_async_copy(rate, bd.at[1], ld.at[5]),
        pltpu.make_async_copy(coup, bd.at[2], ld.at[6]),
        pltpu.make_async_copy(vel, vp.at[(slice(None),) + inner], ld.at[7]),
        pltpu.make_async_copy(buoy, mp.at[0, pl.ds(0, NZ), pl.ds(8, CX), :], ld.at[8]),
        pltpu.make_async_copy(shear, mp.at[1, pl.ds(0, NZ), pl.ds(8, CX), :], ld.at[9]),
        pltpu.make_async_copy(lame, lam, ld.at[10]),
        pltpu.make_async_copy(stress, sp.at[(slice(None),) + inner], ld.at[11]),
    ]
    kloads = [
        pltpu.make_async_copy(stiff.at[pl.ds(16 * i, 16)], kk.at[pl.ds(16 * i, 16)], ldk.at[i])
        for i in range(4)
    ]
    for c in loads[7:10] + loads[:7] + kloads + loads[10:]:
        c.start()

    barrier = pltpu.get_barrier_semaphore()

    def greet(gx, gy):
        pl.semaphore_signal(barrier, inc=1, device_id={"gx": gx, "gy": gy}, device_id_type=MESH)

    for d in range(1, GX):
        greet(wrap(me_x + d, GX), me_y)
    for d in range(1, GY):
        greet(me_x, wrap(me_y + d, GY))
    greet(west, south)
    greet(east, north)

    zero = jnp.zeros((2, 32, CY), F32)
    for f in range(3):
        vp[f, 0:2] = zero
        vp[f, 34:36] = zero
    for f in (2, 4, 5):
        sp[f, 0:2] = zero
        sp[f, 34:36] = zero
    mp[0, NZ] = zero[0]
    mp[1, NZ] = zero[0]
    shm[NZ] = zero[0]

    rows_v = vp.reshape(3 * 36 * 32, CY)
    rows_s = sp.reshape(6 * 36 * 32, CY)
    rows_m = mp.reshape(2 * 34 * 32, CY)
    lane16, row16 = iota((CX, CY), 1), iota((CX, CY), 0)
    row8, lane8 = iota((8, CY), 0), iota((8, CY), 1)

    def layer_rows(ref, field, depth, first, row):
        return ref[pl.ds((field * depth + first) * 32 + row, NZ, stride=32), :]

    def put_rows(ref, field, depth, first, row, value):
        ref[pl.ds((field * depth + first) * 32 + row, NZ, stride=32), :] = value

    keep_w = (me_x > 0).astype(F32)
    keep_e = (me_x < GX - 1).astype(F32)
    keep_s = (me_y > 0).astype(F32)
    keep_n = (me_y < GY - 1).astype(F32)

    pairs_v = [(0, 2, 1), (1, 1, 2), (2, 1, 2)]
    pairs_s = [(0, 1, 2), (3, 2, 1), (4, 2, 1)]

    def pack_x(ref, pairs, buf):
        at = 0
        for field, before, _ in pairs:
            for i in range(before):
                buf[pl.ds(at, 32), :] = layer_rows(ref, field, 36, 2, 8 + CX - before + i)
                at += 32
        for field, _, after in pairs:
            for i in range(after):
                buf[pl.ds(at, 32), :] = layer_rows(ref, field, 36, 2, 8 + i)
                at += 32

    def unpack_x(ref, pairs, buf):
        at = 0
        for field, before, _ in pairs:
            for i in range(before):
                put_rows(ref, field, 36, 2, 8 - before + i, buf[pl.ds(at, 32), :] * keep_w)
                at += 32
        for field, _, after in pairs:
            for i in range(after):
                put_rows(ref, field, 36, 2, 8 + CX + i, buf[pl.ds(at, 32), :] * keep_e)
                at += 32

    def pack_layer(total, value, k):
        return jnp.where(lane16 // 4 == k, pltpu.roll(value, 4 * k + 2, 1), total)

    def halo_of(packed, k):
        return pltpu.roll(packed, CY - 2 - 4 * k, 1)

    def merge_y(buf, at):
        from_south = buf[pl.ds(at[0], CX), :] * keep_s
        return jnp.where(lane16 % 4 >= 2, buf[pl.ds(at[1], CX), :] * keep_n, from_south)

    def halo_set(slot, buf, rbuf, up, down, ny, extra=None):
        def copy(at, to, n, gx, gy):
            return pltpu.make_async_remote_copy(
                src_ref=buf.at[pl.ds(at, n)],
                dst_ref=rbuf.at[pl.ds(to, n)],
                send_sem=hs.at[slot],
                recv_sem=hr.at[slot],
                device_id={"gx": gx, "gy": gy},
                device_id_type=MESH,
            )

        y = up + down
        out = [
            copy(0, 0, up, east, me_y),
            copy(up, up, down, west, me_y),
            copy(y, y, ny, me_x, north),
            copy(y, y + ny, ny, me_x, south),
        ]
        if extra is not None:
            out.append(copy(extra[0], extra[1], CX, west, south))
        return out

    def whole(slot, rbuf):
        return pltpu.make_async_remote_copy(
            src_ref=rbuf,
            dst_ref=rbuf,
            send_sem=hs.at[slot],
            recv_sem=hr.at[slot],
            device_id={"gx": east, "gy": me_y},
            device_id_type=MESH,
        )

    for i in range(7, 10):
        loads[i].wait()
    pack_x(rows_v, pairs_v, b0)
    for f in range(2):
        b0[pl.ds(288 + 32 * f, 32), :] = layer_rows(rows_m, f, 34, 0, 8)
    sources = [lambda k, f=f: vp[f, k + 2, 8:24, :] for f in range(3)]
    sources += [lambda k, f=f: mp[f, k, 8:24, :] for f in range(2)]
    for i, source in enumerate(sources):
        total = jnp.zeros((CX, CY), F32)
        for k in range(NZ):
            total = pack_layer(total, source(k), k)
        b0[pl.ds(352 + 16 * i, 16), :] = total
    halos0 = halo_set(0, b0, r0b, 128, 224, 80, (352 + 64, 352 + 160))

    pl.semaphore_wait(barrier, GX + GY)
    for c in halos0:
        c.start()

    for i in range(7):
        loads[i].wait()
    eye = iota((NB, NB), 0) == iota((NB, NB), 1)

    def to_col(row):
        return jnp.sum(jnp.where(eye, jnp.broadcast_to(row, (NB, NB)), 0.0), axis=1, keepdims=True)

    dof_col = to_col(dofv[...].astype(F32))
    cor_col = to_col(corv[...].astype(F32))
    own_row = ownv[...].astype(F32)
    own_col = to_col(own_row)
    same = jnp.broadcast_to(own_col, (NB, NB)) == jnp.broadcast_to(own_row, (NB, NB))
    upper = iota((NB, NB), 0) < iota((NB, NB), 1)
    lower = iota((NB, NB), 0) > iota((NB, NB), 1)
    pos_row = jnp.sum(jnp.where(same & upper, 1.0, 0.0), axis=0, keepdims=True)
    pos_col = jnp.sum(jnp.where(same & lower, 1.0, 0.0), axis=1, keepdims=True)
    mask = iota((NB, DOF), 1).astype(F32) < dof_col
    cpl = jnp.where(mask, bd[2], 0.0)
    rate0 = jnp.where(mask, bd[1], 0.0)
    drift0 = jnp.where(mask, bd[0], 0.0)

    def gather_dofs(value, first):
        want = (iota((DOF, CY), 0) % 3 + first) == iota((DOF, CY), 1) // 16
        return pick_rhs(value, want.astype(F32), NN)

    lane = iota((NB, CY), 1)
    start_x = jnp.floor((cor_col + 0.5) * (1.0 / SPAN))
    start_y = cor_col - SPAN * start_x
    own_xc = jnp.floor((own_col + 0.5) * (1.0 / GY))
    own_yc = own_col - GY * own_xc
    own_xr = jnp.floor((own_row + 0.5) * (1.0 / GY))
    weights = ct[...] / jnp.sum(ct[...], axis=1, keepdims=True)
    twice = jnp.concatenate([weights, weights], axis=1)
    twice = jnp.where((lane // 64).astype(F32) == pos_col, twice, 0.0)
    to_tile = (iota((128, NB), 0).astype(F32) == own_row).astype(F32)
    send_w[...] = pick_lhs(to_tile, twice, NN).reshape(GX, GY, CY)
    to_column = (iota((GX, NB), 0).astype(F32) == own_xr).astype(F32)
    slot = (lane % 16).astype(F32) == pos_col * 8.0 + own_yc

    def by_column(value):
        return pick_lhs(to_column, jnp.where(slot, value, 0.0), NN).reshape(GX, 1, CY)

    info = gather_dofs(cpl * rate0, 0) + gather_dofs(cpl, 3)
    info = jnp.where(lane // 16 == 6, start_y, jnp.where(lane // 16 == 7, start_x, info))
    send_p[...] = by_column(info)

    def along(src, dst, sems, base, gx, gy):
        return pltpu.make_async_remote_copy(
            src_ref=src,
            dst_ref=dst,
            send_sem=sems.at[base],
            recv_sem=sems.at[base + 1],
            device_id={"gx": gx, "gy": gy},
            device_id_type=MESH,
        )

    def over(n, me, action):
        def one(d, carry):
            action(wrap(me + d, n))
            return carry

        lax.fori_loop(1, n, one, 0)

    def to_gx(src, dst, base):
        over(GX, me_x, lambda peer: along(src.at[peer], dst.at[me_x], xa, base, peer, me_y).start())
        dst[me_x] = src[me_x]

    def to_gy(src, dst, base):
        over(GY, me_y, lambda peer: along(src.at[peer], dst.at[me_y], xa, base, me_x, peer).start())
        dst[me_y] = src[me_y]

    def all_of(ref, sems, base):
        n = ref.shape[0] - 1
        return along(ref.at[pl.ds(0, n)], ref.at[pl.ds(0, n)], sems, base, east, me_y)

    to_gx(send_w, recv_w, 0)
    to_gx(send_p, recv_p, 2)

    def restore(value):
        bds[...] = value.astype(BF16)

        def block(i, carry):
            mine = bds[pl.ds(pl.multiple_of(16 * i, 16), 16), :]
            row = iota((16, DOF), 0)
            total = jnp.zeros((16, DOF), F32)
            for b in range(16):
                part = mm(mine, kk[16 * i + b], NT)
                total = jnp.where(row == b, part, total)
            rest[pl.ds(pl.multiple_of(16 * i, 16), 16), :] = total
            return carry

        lax.fori_loop(0, 4, block, 0)

    for c in kloads:
        c.wait()
    restore(drift0)
    rest0 = rest[...]

    moved = rate0 - DT * rest0 - DT * cpl * rate0
    send_q[...] = by_column(gather_dofs(DT * cpl * cpl, 0) + gather_dofs(cpl * moved, 3))
    to_gx(send_q, recv_q, 6)

    def stencil(points):
        row, col = iota((256, CY), 0) % CY, iota((256, CY), 1)
        total = jnp.zeros((256, CY), F32)
        for offset, weight in points.items():
            total = jnp.where(row == col + offset, weight, total)
        return total.astype(BF16)

    sten[0] = stencil({1: 27.0, 0: -27.0, 2: -1.0, -1: 1.0})
    sten[1] = stencil({0: 27.0, -1: -27.0, 1: -1.0, -2: 1.0})
    sten[2] = stencil({1: 1.0})

    def along_y(value, kind):
        hi, lo = split(value.reshape(ROWS, CY))
        return mm(jnp.concatenate([hi, lo], axis=1), sten[kind], NN).reshape(NZ, CX, CY)

    def y_parts(ref, fields, kinds):
        for i in range(3):
            dyb[i] = along_y(ref[fields[i], pl.ds(2, NZ), pl.ds(8, CX), :], kinds[i])

    y_parts(vp, (0, 1, 2), (0, 1, 0))
    shb[...] = along_y(mp[0, pl.ds(0, NZ), pl.ds(8, CX), :], 2)
    shm[pl.ds(0, NZ), pl.ds(8, CX), :] = along_y(mp[1, pl.ds(0, NZ), pl.ds(8, CX), :], 2)

    all_of(recv_w, xa, 0).wait_recv()
    all_of(recv_p, xa, 2).wait_recv()
    info = recv_p[...].reshape(GX, CY)
    for j in range(GY):
        send_b[j, 0:16, :] = recv_w.reshape(GX * GY, CY)[pl.ds(j, GX, stride=8), :]
        send_b[j, 16:32, :] = info
    to_gy(send_b, tab, 4)

    whole(0, r0b).wait_recv()
    unpack_x(rows_v, pairs_v, r0b)
    for f in range(2):
        put_rows(rows_m, f, 34, 0, 24, r0b[pl.ds(288 + 32 * f, 32), :])
    def reach(packed, forward):
        at = lane16 % 4
        up1, dn1 = pltpu.roll(packed, CY - 1, 1), pltpu.roll(packed, 1, 1)
        if forward:
            up2 = pltpu.roll(packed, CY - 2, 1)
            return jnp.where(
                at == 0, -up2, jnp.where(at == 1, 27.0 * up1 - up2, jnp.where(at == 2, dn1, 0.0))
            )
        dn2 = pltpu.roll(packed, 2, 1)
        return jnp.where(
            at == 0, 0.0, jnp.where(at == 1, -up1, jnp.where(at == 2, dn2 - 27.0 * dn1, dn2))
        )

    reach_v = [
        reach(merge_y(r0b, (352 + 16 * f, 432 + 16 * f)), forward)
        for f, forward in enumerate((True, False, True))
    ]
    packed_b = r0b[pl.ds(432 + 48, CX), :]
    packed_m = r0b[pl.ds(432 + 64, CX), :]

    out_x = (row16 == CX - 1) & (me_x == GX - 1)
    out_y = (lane16 == CY - 1) & (me_y == GY - 1)
    out_xy = out_x | out_y
    last_lane = lane16 == CY - 1
    edge = (lane16 < 2) | (lane16 >= CY - 2)

    def to_last(packed, k):
        return pltpu.roll(packed, lax.rem(2 * CY - 3 - 4 * k, CY), 1)

    def average(k, carry):
        last = k == NZ - 1
        b, m = mp[0, k, 8:24, :], mp[1, k, 8:24, :]
        bx = jnp.where(out_x, b, mp[0, k, 9:25, :])
        by = jnp.where(out_y, b, jnp.where(last_lane, to_last(packed_b, k), shb[k]))
        bz = jnp.where(last, b, mp[0, k + 1, 8:24, :])
        mx = jnp.where(out_x, m, mp[1, k, 9:25, :])
        my = jnp.where(out_y, m, shm[k, 8:24, :])
        mxy = jnp.where(out_xy, m, shm[k, 9:25, :])
        mz = jnp.where(last, m, mp[1, k + 1, 8:24, :])
        mxz = jnp.where(out_x | last, m, mp[1, k + 1, 9:25, :])
        myz = jnp.where(out_y | last, m, shm[k + 1, 8:24, :])
        av[0, k] = (b + bx) * (0.5 * UNIT)
        av[1, k] = (b + by) * (0.5 * UNIT)
        av[2, k] = (b + bz) * (0.5 * UNIT)
        av[3, k] = (m + mx + my + mxy) * (0.25 * UNIT)
        av[4, k] = (m + mx + mz + mxz) * (0.25 * UNIT)
        av[5, k] = (m + my + mz + myz) * (0.25 * UNIT)
        return carry

    def join(k, carry):
        shm[k, 8:24, :] = jnp.where(last_lane, to_last(packed_m, k), shm[k, 8:24, :])
        return carry

    def layers(action, init, first=0):
        def group(i, carry):
            for j in range(GROUP):
                carry = action(GROUP * i + j, carry)
            return carry

        return lax.fori_loop(first, NZ // GROUP, group, init)

    layers(join, 0)
    lane32, row32 = iota((NZ, CY), 1), iota((NZ, CY), 0)
    corners = jnp.broadcast_to(r0b[pl.ds(512, 8), :][0:1, :], (NZ, CY))
    corners = jnp.sum(jnp.where(lane32 == 4 * row32 + 2, corners, 0.0), axis=1, keepdims=True)
    eastern = pltpu.roll(r0b[pl.ds(320, NZ), :], CY - 1, 1)
    eastern = jnp.where(lane32 == CY - 1, corners, eastern)
    put_rows(shm.reshape(33 * 32, CY), 0, 33, 0, 24, eastern)
    layers(average, 0)

    def fwd(minus, zero_, plus, plus2):
        return 27.0 * (plus - zero_) - (plus2 - minus)

    def bwd(minus2, minus, zero_, plus):
        return 27.0 * (zero_ - minus) - (plus - minus2)

    def dx(ref, f, k, forward):
        first = 7 if forward else 6
        parts = [ref[f, k + 2, first + i : first + i + CX, :] for i in range(4)]
        return (fwd if forward else bwd)(*parts)

    def dz(ref, f, k, forward):
        first = 1 if forward else 0
        parts = [ref[f, k + first + i, 8:24, :] for i in range(4)]
        return (fwd if forward else bwd)(*parts)

    def dy(reaches, i, k):
        return dyb[i, k] + jnp.where(edge, halo_of(reaches[i], k), 0.0)

    def stress_layer(reaches, k, carry):
        sx, sy, sz = dx(vp, 0, k, False), dy(reaches, 1, k), dz(vp, 2, k, False)
        m2 = (2.0 * UNIT) * mp[1, k, 8:24, :]
        volume = (UNIT * lam[k]) * (sx + sy + sz)
        new = {}
        for f, s in ((0, sx), (1, sy), (2, sz)):
            new[f] = sp[f, k + 2, 8:24, :] + (volume + m2 * s)
        shear_xy = dy(reaches, 0, k) + dx(vp, 1, k, True)
        shear_xz = dz(vp, 0, k, True) + dx(vp, 2, k, True)
        shear_yz = dz(vp, 1, k, True) + dy(reaches, 2, k)
        for f, s in ((3, shear_xy), (4, shear_xz), (5, shear_yz)):
            new[f] = sp[f, k + 2, 8:24, :] + av[f, k] * s
        for f in range(6):
            sp[f, k + 2, 8:24, :] = new[f]
        return tuple(pack_layer(t, new[f], k) for t, f in zip(carry, (3, 1, 5)))

    def velocity_layer(reaches, out, surface, k, carry):
        ax = dx(sp, 0, k, True) + dy(reaches, 0, k) + dz(sp, 4, k, False)
        ay = dx(sp, 3, k, False) + dy(reaches, 1, k) + dz(sp, 5, k, False)
        az = dx(sp, 4, k, False) + dy(reaches, 2, k) + dz(sp, 2, k, True)
        new = []
        for f, a in ((0, ax), (1, ay), (2, az)):
            value = vp[f, k + 2, 8:24, :] + av[f, k] * a
            if surface:
                value = value + forc[f]
            new.append(value)
            if out is None:
                vp[f, k + 2, 8:24, :] = value
            else:
                out[f, k] = value
        return tuple(pack_layer(t, v, k) for t, v in zip(carry, new)) if carry else carry

    def stress_step(halos, buf, at):
        blank = (jnp.zeros((CX, CY), F32),) * 3
        packed = layers(lambda k, c: stress_layer(halos, k, c), blank)
        for f in range(3):
            buf[pl.ds(at + 16 * f, 16), :] = packed[f]

    def velocity_step(halos, out, buf, at):
        carry = () if buf is None else (jnp.zeros((CX, CY), F32),) * 3
        for k in range(GROUP):
            carry = velocity_layer(halos, out, k == 0, k, carry)
        carry = layers(lambda k, c: velocity_layer(halos, out, False, k, c), carry, 1)
        if buf is not None:
            for f in range(3):
                buf[pl.ds(at + 16 * f, 16), :] = carry[f]

    loads[10].wait()
    loads[11].wait()
    stress_step(reach_v, b1, 288)
    pack_x(rows_s, pairs_s, b1)
    halos1 = halo_set(1, b1, r1b, 160, 128, 48)
    for c in halos1:
        c.start()
    y_parts(sp, (3, 1, 5), (1, 0, 1))

    all_of(tab, xa, 4).wait_recv()
    row128, lane128 = iota((128, CY), 0), iota((128, CY), 1)
    sel = iota((16, CY), 1) == (iota((16, CY), 0) % 8) * 16 + (iota((16, CY), 0) // 8) * 8 + me_y

    def by_slot(value):
        both = pick_lhs(sel.astype(F32), value, NT)
        return jnp.concatenate([both[0:8], both[8:16]], axis=1)

    params = by_slot(tab[:, 16:32, :].reshape(128, CY))
    r0, c0 = params, pltpu.roll(params, 5, 0)
    sent = tab[:, 0:16, :].reshape(128, CY)
    for p in range(2):
        want = (row128 % CX < FOOT) & (lane128 == 64 * p + (row128 % CX) * FOOT + row128 // CX)
        placed = pick_lhs(want.astype(F32), sent, NT)
        shift = jnp.broadcast_to(params[7:8, 128 * p : 128 * p + 128], (128, CY)).astype(jnp.int32)
        for bit in (1, 2, 4, 8):
            placed = jnp.where((shift & bit) != 0, pltpu.roll(placed, bit, 0), placed)
        wxt[:, 128 * p : 128 * p + 128] = placed
    oyt = (iota((CY, 256), 0).astype(F32) == params[6:7]).astype(F32).astype(BF16)

    def motion():
        total = jnp.zeros((8, 256), F32)
        row = iota((8, 256), 0)
        for f in range(3):
            value = vp[f, 2, 8:24, :]
            turns = [value] + [pltpu.roll(value, CY - c, 1) for c in range(1, FOOT)]
            hi, lo = split(jnp.concatenate(turns, axis=0))
            found = mm(hi, oyt, NN) + mm(lo, oyt, NN)
            one = jnp.sum(found * wxt[...], axis=0, keepdims=True)
            total = jnp.where(row == f, jnp.broadcast_to(one, (8, 256)), total)
        return total

    def push(reaction):
        reaction = reaction * (DT * FOOT)
        for f in range(3):
            hi, lo = split(wxt[...] * reaction[f : f + 1])
            spread = mm(hi, oyt, NT) + mm(lo, oyt, NT)
            total = spread[0:CX]
            for c in range(1, FOOT):
                total = total + pltpu.roll(spread[CX * c : CX * c + CX], c, 1)
            forc[f] = total

    def send_motion(step, value):
        bm_s[step] = jnp.where(row8 < 4, value[:, 0:128], pltpu.roll(value[:, 128:256], 4, 0))
        over(
            GY,
            me_y,
            lambda peer: along(
                bm_s.at[step], m_r.at[step, me_y], xm, 4 * step, me_x, peer
            ).start(),
        )
        m_r[step, me_y] = bm_s[step]

    def pass_motion(step):
        all_of(m_r.at[step], xm, 4 * step).wait_recv()
        total = jnp.zeros((8, CY), F32)
        for j in range(GY):
            value = pltpu.roll(m_r[step, j], lax.rem(16 * (j - me_y) + CY, CY), 1)
            total = jnp.where(lane8 // 16 == j, value, total)
        m_p[step] = total
        over(
            GX,
            me_x,
            lambda peer: along(
                m_p.at[step], m_q.at[step, me_x], xm, 4 * step + 2, peer, me_y
            ).start(),
        )
        m_q[step, me_x] = total

    want_lane = own_yc * 16.0 + me_x.astype(F32)
    want_row = own_xc * 2.0 + pos_col

    def take_motion(step):
        all_of(m_q.at[step], xm, 4 * step + 2).wait_recv()
        where_ = (lane.astype(F32) == want_lane).astype(F32)
        found = pick_lhs(where_, m_q[step].reshape(128, CY), NT)
        found = jnp.where((lane // 4).astype(F32) == want_row, found, 0.0)
        onto = (iota((CY, DOF), 0) % 4 == iota((CY, DOF), 1) % 3).astype(F32)
        return pick_rhs(found, onto, NN)

    bm1 = motion()
    send_motion(0, bm1)
    push(r0 - c0 * bm1)

    all_of(recv_q, xa, 6).wait_recv()
    send_d[...] = recv_q[...].reshape(GX, CY)
    over(GY, me_y, lambda peer: along(send_d, tab_q.at[me_y], xa, 8, me_x, peer).start())
    tab_q[me_y] = send_d[...]

    whole(1, r1b).wait_recv()
    unpack_x(rows_s, pairs_s, r1b)
    kinds_s = (False, True, False)
    reach_s = [reach(merge_y(r1b, (288 + 16 * f, 336 + 16 * f)), kinds_s[f]) for f in range(3)]
    velocity_step(reach_s, None, b2, 288)
    pack_x(rows_v, pairs_v, b2)
    halos2 = halo_set(2, b2, r2b, 128, 160, 48)
    for c in halos2:
        c.start()
    y_parts(vp, (0, 1, 2), (0, 1, 0))

    bm2 = motion()
    send_motion(1, bm2)
    pass_motion(0)
    all_of(tab_q, xa, 8).wait_recv()
    params = by_slot(tab_q[...].reshape(128, CY))
    push(pltpu.roll(params, 5, 0) + params * bm1 - c0 * bm2)

    whole(2, r2b).wait_recv()
    unpack_x(rows_v, pairs_v, r2b)
    reach_v = [
        reach(merge_y(r2b, (288 + 16 * f, 336 + 16 * f)), f != 1)
        for f in range(3)
    ]
    stress_step(reach_v, b3, 288)
    pack_x(rows_s, pairs_s, b3)
    halos3 = halo_set(3, b3, r3b, 160, 128, 48)
    for c in halos3:
        c.start()
    y_parts(sp, (3, 1, 5), (1, 0, 1))

    pass_motion(1)

    def advance(rates, drifts, restoring, base):
        relative = jnp.where(mask, rates - base, 0.0)
        rates = jnp.where(mask, rates - DT * restoring - DT * cpl * relative, 0.0)
        return rates, jnp.where(mask, drifts + DT * rates, 0.0)

    rate1, drift1 = advance(rate0, drift0, rest0, take_motion(0))
    restore(drift1)

    whole(3, r3b).wait_recv()
    unpack_x(rows_s, pairs_s, r3b)
    reach_s = [reach(merge_y(r3b, (288 + 16 * f, 336 + 16 * f)), kinds_s[f]) for f in range(3)]
    velocity_step(reach_s, ovel, None, 0)
    rate2, drift2 = advance(rate1, drift1, rest[...], take_motion(1))
    odrift[...] = drift2
    orate[...] = rate2

    for slot, rbuf in enumerate((r0b, r1b, r2b, r3b)):
        whole(slot, rbuf).wait_send()
    for ref, base in ((recv_w, 0), (recv_p, 2), (tab, 4), (recv_q, 6), (tab_q, 8)):
        all_of(ref, xa, base).wait_send()
    for step in range(2):
        all_of(m_r.at[step], xm, 4 * step).wait_send()
        all_of(m_q.at[step], xm, 4 * step + 2).wait_send()


def body(vel, stress, buoy, lame, shear, stiff, drift, rate, coup, contact, dof, owner, corner):
    anywhere = pl.BlockSpec(memory_space=pltpu.HBM)
    vmem = pltpu.VMEM
    near = pl.BlockSpec(memory_space=vmem)
    dma = pltpu.SemaphoreType.DMA
    halo = [vmem((512, CY), F32), vmem((528, CY), F32)] + [vmem((336, CY), F32), vmem((384, CY), F32)] * 3
    shapes = ((3, NZ, CX, CY), (NB, DOF), (NB, DOF))
    return pl.pallas_call(
        kernel,
        out_shape=tuple(vmem(s, F32) for s in shapes),
        in_specs=[anywhere] * 13,
        out_specs=(near,) * 3,
        scratch_shapes=[
            vmem((3, 36, 32, CY), F32),
            vmem((6, 36, 32, CY), F32),
            vmem((2, 34, 32, CY), F32),
            vmem((NZ, CX, CY), F32),
            vmem((6, NZ, CX, CY), F32),
            vmem((NB, DOF, DOF), BF16),
            vmem((3, NB, DOF), F32),
            vmem((NB, 64), F32),
            vmem((1, NB), jnp.int32),
            vmem((1, NB), jnp.int32),
            vmem((1, NB), jnp.int32),
            vmem((3, NZ, CX, CY), F32),
            vmem((3, 256, CY), BF16),
            vmem((NZ, CX, CY), F32),
            vmem((33, 32, CY), F32),
            vmem((GX, GY, CY), F32),
            vmem((GX, GY, CY), F32),
            vmem((GX, 1, CY), F32),
            vmem((GX, 1, CY), F32),
            vmem((GY, 32, CY), F32),
            vmem((GY, 32, CY), F32),
            vmem((GX, 1, CY), F32),
            vmem((GX, 1, CY), F32),
            vmem((GX, CY), F32),
            vmem((GY, GX, CY), F32),
            vmem((128, 256), F32),
            vmem((3, CX, CY), F32),
            vmem((2, 8, CY), F32),
            vmem((2, GY, 8, CY), F32),
            vmem((2, 8, CY), F32),
            vmem((2, GX, 8, CY), F32),
            vmem((NB, DOF), F32),
            vmem((NB, DOF), BF16),
            *halo,
            dma((12,)),
            dma((4,)),
            dma((10,)),
            dma((8,)),
            dma((4,)),
            dma((4,)),
        ],
        compiler_params=pltpu.CompilerParams(
            collective_id=0, has_side_effects=True, vmem_limit_bytes=66_100_000
        ),
    )(
        vel, stress, buoy, lame, shear, stiff, drift, rate, coup, contact,
        dof.reshape(1, NB), owner.reshape(1, NB), corner.reshape(1, NB),
    )


def solution(mesh):
    placed = (
        P(None, None, "gx", "gy"),
        P(None, None, "gx", "gy"),
        P(None, "gx", "gy"),
        P(None, "gx", "gy"),
        P(None, "gx", "gy"),
        P(("gx", "gy"), None, None),
        P(("gx", "gy"), None),
        P(("gx", "gy"), None),
        P(("gx", "gy"), None),
        P(("gx", "gy"), None),
        P(("gx", "gy")),
        P(("gx", "gy"), None),
        P(("gx", "gy")),
    )
    return jax.shard_map(
        body,
        mesh=mesh,
        in_specs=placed,
        out_specs=(P(None, None, "gx", "gy"), P(("gx", "gy"), None), P(("gx", "gy"), None)),
        check_vma=False,
    )
```

```python
import jax
import jax.numpy as jnp
from jax import lax
from jax.experimental import pallas as pl
from jax.experimental.pallas import tpu as pltpu
from jax.sharding import PartitionSpec as P

MESH = pl.DeviceIdType.MESH
F32 = jnp.float32
BF16 = jnp.bfloat16
DT = 0.3
INNER = 9.0 / 8.0
OUTER = 1.0 / 24.0
FOOT = 8
GX, GY = 16, 8
NZ, CX, CY = 32, 16, 128
NB, DOF = 64, 256
SPAN = CY - FOOT + 1
ROWS = NZ * CX
GROUP, PARTS = 4, 4
PART = NZ // PARTS
UNIT = DT / 24.0


def iota(shape, dim):
    return lax.broadcasted_iota(jnp.int32, shape, dim)


def mm(a, b, dims):
    return lax.dot_general(a, b, (dims, ((), ())), preferred_element_type=F32)


def split(x):
    hi = x.astype(BF16)
    return hi, (x - hi.astype(F32)).astype(BF16)


NN, NT = ((1,), (0,)), ((1,), (1,))


def pick_lhs(exact, value, dims):
    hi, lo = split(value)
    exact = exact.astype(BF16)
    return mm(exact, hi, dims) + mm(exact, lo, dims)


def pick_rhs(value, exact, dims):
    hi, lo = split(value)
    exact = exact.astype(BF16)
    return mm(hi, exact, dims) + mm(lo, exact, dims)


def kernel(
    vel, stress, buoy, lame, shear, stiff, drift, rate, coup, contact, dof, owner, corner,
    ovel, odrift, orate,
    vp, sp, mp, lam, av, kk, bd, ct, dofv, ownv, corv,
    dyb, sten, shb, shm,
    send_w, recv_w, send_p, recv_p, send_b, tab, send_q, recv_q, send_d, tab_q, wxt, forc,
    bm_s, m_r, m_p, m_q, rest, bds,
    b0, r0b, b1, r1b, b2, r2b, b3, r3b,
    ld, ldk, xa, xm, hs, hr,
):
    me_x = lax.axis_index("gx")
    me_y = lax.axis_index("gy")

    def wrap(value, n):
        return lax.rem(value + n, n)

    east, west = wrap(me_x + 1, GX), wrap(me_x - 1, GX)
    north, south = wrap(me_y + 1, GY), wrap(me_y - 1, GY)

    inner = (pl.ds(2, NZ), pl.ds(8, CX), slice(None))
    loads = [
        pltpu.make_async_copy(contact, ct, ld.at[0]),
        pltpu.make_async_copy(dof, dofv, ld.at[1]),
        pltpu.make_async_copy(owner, ownv, ld.at[2]),
        pltpu.make_async_copy(corner, corv, ld.at[3]),
        pltpu.make_async_copy(drift, bd.at[0], ld.at[4]),
        pltpu.make_async_copy(rate, bd.at[1], ld.at[5]),
        pltpu.make_async_copy(coup, bd.at[2], ld.at[6]),
        pltpu.make_async_copy(vel, vp.at[(slice(None),) + inner], ld.at[7]),
        pltpu.make_async_copy(buoy, mp.at[0, pl.ds(0, NZ), pl.ds(8, CX), :], ld.at[8]),
        pltpu.make_async_copy(shear, mp.at[1, pl.ds(0, NZ), pl.ds(8, CX), :], ld.at[9]),
        pltpu.make_async_copy(lame, lam, ld.at[10]),
        pltpu.make_async_copy(stress, sp.at[(slice(None),) + inner], ld.at[11]),
    ]
    kloads = [
        pltpu.make_async_copy(stiff.at[pl.ds(16 * i, 16)], kk.at[pl.ds(16 * i, 16)], ldk.at[i])
        for i in range(4)
    ]
    for c in loads[7:10] + loads[:7] + kloads + loads[10:]:
        c.start()

    barrier = pltpu.get_barrier_semaphore()

    def greet(gx, gy):
        pl.semaphore_signal(barrier, inc=1, device_id={"gx": gx, "gy": gy}, device_id_type=MESH)

    for d in range(1, GX):
        greet(wrap(me_x + d, GX), me_y)
    for d in range(1, GY):
        greet(me_x, wrap(me_y + d, GY))
    greet(west, south)
    greet(east, north)

    zero = jnp.zeros((2, 32, CY), F32)
    for f in range(3):
        vp[f, 0:2] = zero
        vp[f, 34:36] = zero
    for f in (2, 4, 5):
        sp[f, 0:2] = zero
        sp[f, 34:36] = zero
    mp[0, NZ] = zero[0]
    mp[1, NZ] = zero[0]
    shm[NZ] = zero[0]

    rows_v = vp.reshape(3 * 36 * 32, CY)
    rows_s = sp.reshape(6 * 36 * 32, CY)
    rows_m = mp.reshape(2 * 34 * 32, CY)
    lane16, row16 = iota((CX, CY), 1), iota((CX, CY), 0)
    row8, lane8 = iota((8, CY), 0), iota((8, CY), 1)

    def layer_rows(ref, field, depth, first, row):
        return ref[pl.ds((field * depth + first) * 32 + row, NZ, stride=32), :]

    def put_rows(ref, field, depth, first, row, value):
        ref[pl.ds((field * depth + first) * 32 + row, NZ, stride=32), :] = value

    keep_w = (me_x > 0).astype(F32)
    keep_e = (me_x < GX - 1).astype(F32)
    keep_s = (me_y > 0).astype(F32)
    keep_n = (me_y < GY - 1).astype(F32)

    pairs_v = [(0, 2, 1), (1, 1, 2), (2, 1, 2)]
    pairs_s = [(0, 1, 2), (3, 2, 1), (4, 2, 1)]

    def x_rows(pairs, part, inside):
        ups, downs = sum(p[1] for p in pairs), sum(p[2] for p in pairs)
        at = PART * ups * part
        for field, before, _ in pairs:
            for i in range(before):
                yield field, 8 - before + i + (CX if inside else 0), at, keep_w
                at += PART
        at = PART * (ups * PARTS + downs * part)
        for field, _, after in pairs:
            for i in range(after):
                yield field, 8 + i + (0 if inside else CX), at, keep_e
                at += PART

    def pack_x(ref, pairs, buf, part):
        for field, row, at, _ in x_rows(pairs, part, True):
            first = (field * 36 + 2 + PART * part) * 32 + row
            buf[pl.ds(at, PART), :] = ref[pl.ds(first, PART, stride=32), :]

    def unpack_x(ref, pairs, buf):
        for part in range(PARTS):
            for field, row, at, keep in x_rows(pairs, part, False):
                first = (field * 36 + 2 + PART * part) * 32 + row
                ref[pl.ds(first, PART, stride=32), :] = buf[pl.ds(at, PART), :] * keep

    def pack_layer(total, value, k):
        return jnp.where(lane16 // 4 == k, pltpu.roll(value, 4 * k + 2, 1), total)

    def halo_of(packed, k):
        return pltpu.roll(packed, CY - 2 - 4 * k, 1)

    def merge_y(buf, at):
        from_south = buf[pl.ds(at[0], CX), :] * keep_s
        return jnp.where(lane16 % 4 >= 2, buf[pl.ds(at[1], CX), :] * keep_n, from_south)

    def halo_set(slot, buf, rbuf, up, down, ny, extra=None):
        def copy(at, to, n, gx, gy):
            return pltpu.make_async_remote_copy(
                src_ref=buf.at[pl.ds(at, n)],
                dst_ref=rbuf.at[pl.ds(to, n)],
                send_sem=hs.at[slot],
                recv_sem=hr.at[slot],
                device_id={"gx": gx, "gy": gy},
                device_id_type=MESH,
            )

        def x_part(part, parts):
            a, b = up // parts, down // parts
            return [
                copy(a * part, a * part, a, east, me_y),
                copy(up + b * part, up + b * part, b, west, me_y),
            ]

        y = up + down
        ends = [copy(y, y, ny, me_x, north), copy(y, y + ny, ny, me_x, south)]
        if extra is not None:
            ends.append(copy(extra[0], extra[1], CX, west, south))
        return x_part, ends

    def start(copies):
        for c in copies:
            c.start()

    def whole(slot, rbuf):
        return pltpu.make_async_remote_copy(
            src_ref=rbuf,
            dst_ref=rbuf,
            send_sem=hs.at[slot],
            recv_sem=hr.at[slot],
            device_id={"gx": east, "gy": me_y},
            device_id_type=MESH,
        )

    for i in range(7, 10):
        loads[i].wait()
    for part in range(PARTS):
        pack_x(rows_v, pairs_v, b0, part)
    for f in range(2):
        b0[pl.ds(288 + 32 * f, 32), :] = layer_rows(rows_m, f, 34, 0, 8)
    sources = [lambda k, f=f: vp[f, k + 2, 8:24, :] for f in range(3)]
    sources += [lambda k, f=f: mp[f, k, 8:24, :] for f in range(2)]
    for i, source in enumerate(sources):
        total = jnp.zeros((CX, CY), F32)
        for k in range(NZ):
            total = pack_layer(total, source(k), k)
        b0[pl.ds(352 + 16 * i, 16), :] = total
    halos0 = halo_set(0, b0, r0b, 128, 224, 80, (352 + 64, 352 + 160))

    pl.semaphore_wait(barrier, GX + GY)
    start(halos0[0](0, 1) + halos0[1])

    for i in range(7):
        loads[i].wait()
    eye = iota((NB, NB), 0) == iota((NB, NB), 1)

    def to_col(row):
        return jnp.sum(jnp.where(eye, jnp.broadcast_to(row, (NB, NB)), 0.0), axis=1, keepdims=True)

    dof_col = to_col(dofv[...].astype(F32))
    cor_col = to_col(corv[...].astype(F32))
    own_row = ownv[...].astype(F32)
    own_col = to_col(own_row)
    same = jnp.broadcast_to(own_col, (NB, NB)) == jnp.broadcast_to(own_row, (NB, NB))
    upper = iota((NB, NB), 0) < iota((NB, NB), 1)
    lower = iota((NB, NB), 0) > iota((NB, NB), 1)
    pos_row = jnp.sum(jnp.where(same & upper, 1.0, 0.0), axis=0, keepdims=True)
    pos_col = jnp.sum(jnp.where(same & lower, 1.0, 0.0), axis=1, keepdims=True)
    mask = iota((NB, DOF), 1).astype(F32) < dof_col
    cpl = jnp.where(mask, bd[2], 0.0)
    rate0 = jnp.where(mask, bd[1], 0.0)
    drift0 = jnp.where(mask, bd[0], 0.0)

    def gather_dofs(value, first):
        want = (iota((DOF, CY), 0) % 3 + first) == iota((DOF, CY), 1) // 16
        return pick_rhs(value, want.astype(F32), NN)

    lane = iota((NB, CY), 1)
    start_x = jnp.floor((cor_col + 0.5) * (1.0 / SPAN))
    start_y = cor_col - SPAN * start_x
    own_xc = jnp.floor((own_col + 0.5) * (1.0 / GY))
    own_yc = own_col - GY * own_xc
    own_xr = jnp.floor((own_row + 0.5) * (1.0 / GY))
    weights = ct[...] / jnp.sum(ct[...], axis=1, keepdims=True)
    twice = jnp.concatenate([weights, weights], axis=1)
    twice = jnp.where((lane // 64).astype(F32) == pos_col, twice, 0.0)
    to_tile = (iota((128, NB), 0).astype(F32) == own_row).astype(F32)
    send_w[...] = pick_lhs(to_tile, twice, NN).reshape(GX, GY, CY)
    to_column = (iota((GX, NB), 0).astype(F32) == own_xr).astype(F32)
    slot = (lane % 16).astype(F32) == pos_col * 8.0 + own_yc

    def by_column(value):
        return pick_lhs(to_column, jnp.where(slot, value, 0.0), NN).reshape(GX, 1, CY)

    info = gather_dofs(cpl * rate0, 0) + gather_dofs(cpl, 3)
    info = jnp.where(lane // 16 == 6, start_y, jnp.where(lane // 16 == 7, start_x, info))
    send_p[...] = by_column(info)

    def along(src, dst, sems, base, gx, gy):
        return pltpu.make_async_remote_copy(
            src_ref=src,
            dst_ref=dst,
            send_sem=sems.at[base],
            recv_sem=sems.at[base + 1],
            device_id={"gx": gx, "gy": gy},
            device_id_type=MESH,
        )

    def over(n, me, action):
        def one(d, carry):
            action(wrap(me + d, n))
            return carry

        lax.fori_loop(1, n, one, 0)

    def to_gx(src, dst, base):
        over(GX, me_x, lambda peer: along(src.at[peer], dst.at[me_x], xa, base, peer, me_y).start())
        dst[me_x] = src[me_x]

    def to_gy(src, dst, base):
        over(GY, me_y, lambda peer: along(src.at[peer], dst.at[me_y], xa, base, me_x, peer).start())
        dst[me_y] = src[me_y]

    def all_of(ref, sems, base):
        n = ref.shape[0] - 1
        return along(ref.at[pl.ds(0, n)], ref.at[pl.ds(0, n)], sems, base, east, me_y)

    to_gx(send_w, recv_w, 0)
    to_gx(send_p, recv_p, 2)

    def restore(value):
        bds[...] = value.astype(BF16)

        def block(i, carry):
            mine = bds[pl.ds(pl.multiple_of(16 * i, 16), 16), :]
            row = iota((16, DOF), 0)
            total = jnp.zeros((16, DOF), F32)
            for b in range(16):
                part = mm(mine, kk[16 * i + b], NT)
                total = jnp.where(row == b, part, total)
            rest[pl.ds(pl.multiple_of(16 * i, 16), 16), :] = total
            return carry

        lax.fori_loop(0, 4, block, 0)

    for c in kloads:
        c.wait()
    restore(drift0)
    rest0 = rest[...]

    moved = rate0 - DT * rest0 - DT * cpl * rate0
    send_q[...] = by_column(gather_dofs(DT * cpl * cpl, 0) + gather_dofs(cpl * moved, 3))
    to_gx(send_q, recv_q, 6)

    def stencil(points):
        row, col = iota((256, CY), 0) % CY, iota((256, CY), 1)
        total = jnp.zeros((256, CY), F32)
        for offset, weight in points.items():
            total = jnp.where(row == col + offset, weight, total)
        return total.astype(BF16)

    sten[0] = stencil({1: 27.0, 0: -27.0, 2: -1.0, -1: 1.0})
    sten[1] = stencil({0: 27.0, -1: -27.0, 1: -1.0, -2: 1.0})
    sten[2] = stencil({1: 1.0})

    def along_y(value, kind):
        hi, lo = split(value.reshape(ROWS, CY))
        return mm(jnp.concatenate([hi, lo], axis=1), sten[kind], NN).reshape(NZ, CX, CY)

    def y_parts(ref, fields, kinds):
        for i in range(3):
            dyb[i] = along_y(ref[fields[i], pl.ds(2, NZ), pl.ds(8, CX), :], kinds[i])

    y_parts(vp, (0, 1, 2), (0, 1, 0))
    shb[...] = along_y(mp[0, pl.ds(0, NZ), pl.ds(8, CX), :], 2)
    shm[pl.ds(0, NZ), pl.ds(8, CX), :] = along_y(mp[1, pl.ds(0, NZ), pl.ds(8, CX), :], 2)

    whole(0, r0b).wait_recv()
    unpack_x(rows_v, pairs_v, r0b)
    for f in range(2):
        put_rows(rows_m, f, 34, 0, 24, r0b[pl.ds(288 + 32 * f, 32), :])
    def reach(packed, forward):
        at = lane16 % 4
        up1, dn1 = pltpu.roll(packed, CY - 1, 1), pltpu.roll(packed, 1, 1)
        if forward:
            up2 = pltpu.roll(packed, CY - 2, 1)
            return jnp.where(
                at == 0, -up2, jnp.where(at == 1, 27.0 * up1 - up2, jnp.where(at == 2, dn1, 0.0))
            )
        dn2 = pltpu.roll(packed, 2, 1)
        return jnp.where(
            at == 0, 0.0, jnp.where(at == 1, -up1, jnp.where(at == 2, dn2 - 27.0 * dn1, dn2))
        )

    reach_v = [
        reach(merge_y(r0b, (352 + 16 * f, 432 + 16 * f)), forward)
        for f, forward in enumerate((True, False, True))
    ]
    packed_b = r0b[pl.ds(432 + 48, CX), :]
    packed_m = r0b[pl.ds(432 + 64, CX), :]

    out_x = (row16 == CX - 1) & (me_x == GX - 1)
    out_y = (lane16 == CY - 1) & (me_y == GY - 1)
    out_xy = out_x | out_y
    last_lane = lane16 == CY - 1
    edge = (lane16 < 2) | (lane16 >= CY - 2)

    def to_last(packed, k):
        return pltpu.roll(packed, lax.rem(2 * CY - 3 - 4 * k, CY), 1)

    def average_b(k, carry):
        b = mp[0, k, 8:24, :]
        bx = jnp.where(out_x, b, mp[0, k, 9:25, :])
        by = jnp.where(out_y, b, jnp.where(last_lane, to_last(packed_b, k), shb[k]))
        bz = jnp.where(k == NZ - 1, b, mp[0, k + 1, 8:24, :])
        av[0, k] = (b + bx) * (0.5 * UNIT)
        av[1, k] = (b + by) * (0.5 * UNIT)
        av[2, k] = (b + bz) * (0.5 * UNIT)
        return carry

    def average_m(k, carry):
        last = k == NZ - 1
        m = mp[1, k, 8:24, :]
        mx = jnp.where(out_x, m, mp[1, k, 9:25, :])
        my = jnp.where(out_y, m, shm[k, 8:24, :])
        mxy = jnp.where(out_xy, m, shm[k, 9:25, :])
        mz = jnp.where(last, m, mp[1, k + 1, 8:24, :])
        mxz = jnp.where(out_x | last, m, mp[1, k + 1, 9:25, :])
        myz = jnp.where(out_y | last, m, shm[k + 1, 8:24, :])
        av[3, k] = (m + mx + my + mxy) * (0.25 * UNIT)
        av[4, k] = (m + mx + mz + mxz) * (0.25 * UNIT)
        av[5, k] = (m + my + mz + myz) * (0.25 * UNIT)
        return carry

    def join(k, carry):
        shm[k, 8:24, :] = jnp.where(last_lane, to_last(packed_m, k), shm[k, 8:24, :])
        return carry

    def layers(action, init, first=0, last=NZ // GROUP):
        def group(i, carry):
            for j in range(GROUP):
                carry = action(GROUP * i + j, carry)
            return carry

        return lax.fori_loop(first, last, group, init)

    layers(join, 0)
    lane32, row32 = iota((NZ, CY), 1), iota((NZ, CY), 0)
    corners = jnp.broadcast_to(r0b[pl.ds(512, 8), :][0:1, :], (NZ, CY))
    corners = jnp.sum(jnp.where(lane32 == 4 * row32 + 2, corners, 0.0), axis=1, keepdims=True)
    eastern = pltpu.roll(r0b[pl.ds(320, NZ), :], CY - 1, 1)
    eastern = jnp.where(lane32 == CY - 1, corners, eastern)
    put_rows(shm.reshape(33 * 32, CY), 0, 33, 0, 24, eastern)
    layers(average_m, 0)

    all_of(recv_w, xa, 0).wait_recv()
    all_of(recv_p, xa, 2).wait_recv()
    info = recv_p[...].reshape(GX, CY)
    for j in range(GY):
        send_b[j, 0:16, :] = recv_w.reshape(GX * GY, CY)[pl.ds(j, GX, stride=8), :]
        send_b[j, 16:32, :] = info
    to_gy(send_b, tab, 4)

    def fwd(minus, zero_, plus, plus2):
        return 27.0 * (plus - zero_) - (plus2 - minus)

    def bwd(minus2, minus, zero_, plus):
        return 27.0 * (zero_ - minus) - (plus - minus2)

    def dx(ref, f, k, forward):
        first = 7 if forward else 6
        parts = [ref[f, k + 2, first + i : first + i + CX, :] for i in range(4)]
        return (fwd if forward else bwd)(*parts)

    def dz(ref, f, k, forward):
        first = 1 if forward else 0
        parts = [ref[f, k + first + i, 8:24, :] for i in range(4)]
        return (fwd if forward else bwd)(*parts)

    def dy(reaches, i, k):
        return dyb[i, k] + jnp.where(edge, halo_of(reaches[i], k), 0.0)

    def stress_layer(reaches, k, carry):
        sx, sy, sz = dx(vp, 0, k, False), dy(reaches, 1, k), dz(vp, 2, k, False)
        m2 = (2.0 * UNIT) * mp[1, k, 8:24, :]
        volume = (UNIT * lam[k]) * (sx + sy + sz)
        new = {}
        for f, s in ((0, sx), (1, sy), (2, sz)):
            new[f] = sp[f, k + 2, 8:24, :] + (volume + m2 * s)
        shear_xy = dy(reaches, 0, k) + dx(vp, 1, k, True)
        shear_xz = dz(vp, 0, k, True) + dx(vp, 2, k, True)
        shear_yz = dz(vp, 1, k, True) + dy(reaches, 2, k)
        for f, s in ((3, shear_xy), (4, shear_xz), (5, shear_yz)):
            new[f] = sp[f, k + 2, 8:24, :] + av[f, k] * s
        for f in range(6):
            sp[f, k + 2, 8:24, :] = new[f]
        return tuple(pack_layer(t, new[f], k) for t, f in zip(carry, (3, 1, 5)))

    def velocity_layer(reaches, out, surface, k, carry):
        ax = dx(sp, 0, k, True) + dy(reaches, 0, k) + dz(sp, 4, k, False)
        ay = dx(sp, 3, k, False) + dy(reaches, 1, k) + dz(sp, 5, k, False)
        az = dx(sp, 4, k, False) + dy(reaches, 2, k) + dz(sp, 2, k, True)
        new = []
        for f, a in ((0, ax), (1, ay), (2, az)):
            value = vp[f, k + 2, 8:24, :] + av[f, k] * a
            if surface:
                value = value + forc[f]
            new.append(value)
            if out is None:
                vp[f, k + 2, 8:24, :] = value
            else:
                out[f, k] = value
        return tuple(pack_layer(t, v, k) for t, v in zip(carry, new)) if carry else carry

    def stress_step(reaches, buf, halos):
        carry = (jnp.zeros((CX, CY), F32),) * 3
        count = PART // GROUP
        for part in range(PARTS):
            carry = layers(
                lambda k, c: stress_layer(reaches, k, c), carry, count * part, count * part + count
            )
            pack_x(rows_s, pairs_s, buf, part)
            start(halos[0](part, PARTS))
        for f in range(3):
            buf[pl.ds(288 + 16 * f, 16), :] = carry[f]
        start(halos[1])

    def velocity_step(reaches, buf, halos):
        carry = (jnp.zeros((CX, CY), F32),) * 3
        count = PART // GROUP
        for part in range(PARTS):
            first = count * part
            if part == 0:
                for k in range(GROUP):
                    carry = velocity_layer(reaches, None, k == 0, k, carry)
                first = 1
            carry = layers(
                lambda k, c: velocity_layer(reaches, None, False, k, c), carry, first, count * part + count
            )
            pack_x(rows_v, pairs_v, buf, part)
            start(halos[0](part, PARTS))
        for f in range(3):
            buf[pl.ds(288 + 16 * f, 16), :] = carry[f]
        start(halos[1])

    def last_velocity(reaches, out):
        for k in range(GROUP):
            velocity_layer(reaches, out, k == 0, k, ())
        layers(lambda k, c: velocity_layer(reaches, out, False, k, c), (), 1)

    loads[10].wait()
    loads[11].wait()
    halos1 = halo_set(1, b1, r1b, 160, 128, 48)
    stress_step(reach_v, b1, halos1)
    y_parts(sp, (3, 1, 5), (1, 0, 1))
    layers(average_b, 0)

    all_of(tab, xa, 4).wait_recv()
    row128, lane128 = iota((128, CY), 0), iota((128, CY), 1)
    sel = iota((16, CY), 1) == (iota((16, CY), 0) % 8) * 16 + (iota((16, CY), 0) // 8) * 8 + me_y

    def by_slot(value):
        both = pick_lhs(sel.astype(F32), value, NT)
        return jnp.concatenate([both[0:8], both[8:16]], axis=1)

    params = by_slot(tab[:, 16:32, :].reshape(128, CY))
    r0, c0 = params, pltpu.roll(params, 5, 0)
    sent = tab[:, 0:16, :].reshape(128, CY)
    for p in range(2):
        want = (row128 % CX < FOOT) & (lane128 == 64 * p + (row128 % CX) * FOOT + row128 // CX)
        placed = pick_lhs(want.astype(F32), sent, NT)
        shift = jnp.broadcast_to(params[7:8, 128 * p : 128 * p + 128], (128, CY)).astype(jnp.int32)
        for bit in (1, 2, 4, 8):
            placed = jnp.where((shift & bit) != 0, pltpu.roll(placed, bit, 0), placed)
        wxt[:, 128 * p : 128 * p + 128] = placed
    oyt = (iota((CY, 256), 0).astype(F32) == params[6:7]).astype(F32).astype(BF16)

    def motion():
        total = jnp.zeros((8, 256), F32)
        row = iota((8, 256), 0)
        for f in range(3):
            value = vp[f, 2, 8:24, :]
            turns = [value] + [pltpu.roll(value, CY - c, 1) for c in range(1, FOOT)]
            hi, lo = split(jnp.concatenate(turns, axis=0))
            found = mm(hi, oyt, NN) + mm(lo, oyt, NN)
            one = jnp.sum(found * wxt[...], axis=0, keepdims=True)
            total = jnp.where(row == f, jnp.broadcast_to(one, (8, 256)), total)
        return total

    def push(reaction):
        reaction = reaction * (DT * FOOT)
        for f in range(3):
            hi, lo = split(wxt[...] * reaction[f : f + 1])
            spread = mm(hi, oyt, NT) + mm(lo, oyt, NT)
            total = spread[0:CX]
            for c in range(1, FOOT):
                total = total + pltpu.roll(spread[CX * c : CX * c + CX], c, 1)
            forc[f] = total

    def send_motion(step, value):
        bm_s[step] = jnp.where(row8 < 4, value[:, 0:128], pltpu.roll(value[:, 128:256], 4, 0))
        over(
            GY,
            me_y,
            lambda peer: along(
                bm_s.at[step], m_r.at[step, me_y], xm, 4 * step, me_x, peer
            ).start(),
        )
        m_r[step, me_y] = bm_s[step]

    def pass_motion(step):
        all_of(m_r.at[step], xm, 4 * step).wait_recv()
        total = jnp.zeros((8, CY), F32)
        for j in range(GY):
            value = pltpu.roll(m_r[step, j], lax.rem(16 * (j - me_y) + CY, CY), 1)
            total = jnp.where(lane8 // 16 == j, value, total)
        m_p[step] = total
        over(
            GX,
            me_x,
            lambda peer: along(
                m_p.at[step], m_q.at[step, me_x], xm, 4 * step + 2, peer, me_y
            ).start(),
        )
        m_q[step, me_x] = total

    want_lane = own_yc * 16.0 + me_x.astype(F32)
    want_row = own_xc * 2.0 + pos_col

    def take_motion(step):
        all_of(m_q.at[step], xm, 4 * step + 2).wait_recv()
        where_ = (lane.astype(F32) == want_lane).astype(F32)
        found = pick_lhs(where_, m_q[step].reshape(128, CY), NT)
        found = jnp.where((lane // 4).astype(F32) == want_row, found, 0.0)
        onto = (iota((CY, DOF), 0) % 4 == iota((CY, DOF), 1) % 3).astype(F32)
        return pick_rhs(found, onto, NN)

    bm1 = motion()
    send_motion(0, bm1)
    push(r0 - c0 * bm1)

    all_of(recv_q, xa, 6).wait_recv()
    send_d[...] = recv_q[...].reshape(GX, CY)
    over(GY, me_y, lambda peer: along(send_d, tab_q.at[me_y], xa, 8, me_x, peer).start())
    tab_q[me_y] = send_d[...]

    whole(1, r1b).wait_recv()
    unpack_x(rows_s, pairs_s, r1b)
    kinds_s = (False, True, False)
    reach_s = [reach(merge_y(r1b, (288 + 16 * f, 336 + 16 * f)), kinds_s[f]) for f in range(3)]
    halos2 = halo_set(2, b2, r2b, 128, 160, 48)
    velocity_step(reach_s, b2, halos2)

    bm2 = motion()
    send_motion(1, bm2)
    y_parts(vp, (0, 1, 2), (0, 1, 0))
    pass_motion(0)
    all_of(tab_q, xa, 8).wait_recv()
    params = by_slot(tab_q[...].reshape(128, CY))
    push(pltpu.roll(params, 5, 0) + params * bm1 - c0 * bm2)

    whole(2, r2b).wait_recv()
    unpack_x(rows_v, pairs_v, r2b)
    reach_v = [
        reach(merge_y(r2b, (288 + 16 * f, 336 + 16 * f)), f != 1)
        for f in range(3)
    ]
    halos3 = halo_set(3, b3, r3b, 160, 128, 48)
    stress_step(reach_v, b3, halos3)
    y_parts(sp, (3, 1, 5), (1, 0, 1))

    pass_motion(1)

    def advance(rates, drifts, restoring, base):
        relative = jnp.where(mask, rates - base, 0.0)
        rates = jnp.where(mask, rates - DT * restoring - DT * cpl * relative, 0.0)
        return rates, jnp.where(mask, drifts + DT * rates, 0.0)

    rate1, drift1 = advance(rate0, drift0, rest0, take_motion(0))
    restore(drift1)

    whole(3, r3b).wait_recv()
    unpack_x(rows_s, pairs_s, r3b)
    reach_s = [reach(merge_y(r3b, (288 + 16 * f, 336 + 16 * f)), kinds_s[f]) for f in range(3)]
    last_velocity(reach_s, ovel)
    rate2, drift2 = advance(rate1, drift1, rest[...], take_motion(1))
    odrift[...] = drift2
    orate[...] = rate2

    for slot, rbuf in enumerate((r0b, r1b, r2b, r3b)):
        whole(slot, rbuf).wait_send()
    for ref, base in ((recv_w, 0), (recv_p, 2), (tab, 4), (recv_q, 6), (tab_q, 8)):
        all_of(ref, xa, base).wait_send()
    for step in range(2):
        all_of(m_r.at[step], xm, 4 * step).wait_send()
        all_of(m_q.at[step], xm, 4 * step + 2).wait_send()


def finish(vel, drift, rate, ovel, odrift, orate, sem):
    copies = [
        pltpu.make_async_copy(vel, ovel, sem.at[0]),
        pltpu.make_async_copy(drift, odrift, sem.at[1]),
        pltpu.make_async_copy(rate, orate, sem.at[2]),
    ]
    for c in copies:
        c.start()
    for c in copies:
        c.wait()


def body(vel, stress, buoy, lame, shear, stiff, drift, rate, coup, contact, dof, owner, corner):
    anywhere = pl.BlockSpec(memory_space=pltpu.HBM)
    vmem = pltpu.VMEM
    near = pl.BlockSpec(memory_space=vmem)
    dma = pltpu.SemaphoreType.DMA
    halo = [vmem((512, CY), F32), vmem((528, CY), F32)] + [vmem((336, CY), F32), vmem((384, CY), F32)] * 3
    shapes = ((3, NZ, CX, CY), (NB, DOF), (NB, DOF))
    outs = pl.pallas_call(
        kernel,
        out_shape=tuple(vmem(s, F32) for s in shapes),
        in_specs=[anywhere] * 13,
        out_specs=(near,) * 3,
        scratch_shapes=[
            vmem((3, 36, 32, CY), F32),
            vmem((6, 36, 32, CY), F32),
            vmem((2, 34, 32, CY), F32),
            vmem((NZ, CX, CY), F32),
            vmem((6, NZ, CX, CY), F32),
            vmem((NB, DOF, DOF), BF16),
            vmem((3, NB, DOF), F32),
            vmem((NB, 64), F32),
            vmem((1, NB), jnp.int32),
            vmem((1, NB), jnp.int32),
            vmem((1, NB), jnp.int32),
            vmem((3, NZ, CX, CY), F32),
            vmem((3, 256, CY), BF16),
            vmem((NZ, CX, CY), F32),
            vmem((33, 32, CY), F32),
            vmem((GX, GY, CY), F32),
            vmem((GX, GY, CY), F32),
            vmem((GX, 1, CY), F32),
            vmem((GX, 1, CY), F32),
            vmem((GY, 32, CY), F32),
            vmem((GY, 32, CY), F32),
            vmem((GX, 1, CY), F32),
            vmem((GX, 1, CY), F32),
            vmem((GX, CY), F32),
            vmem((GY, GX, CY), F32),
            vmem((128, 256), F32),
            vmem((3, CX, CY), F32),
            vmem((2, 8, CY), F32),
            vmem((2, GY, 8, CY), F32),
            vmem((2, 8, CY), F32),
            vmem((2, GX, 8, CY), F32),
            vmem((NB, DOF), F32),
            vmem((NB, DOF), BF16),
            *halo,
            dma((12,)),
            dma((4,)),
            dma((10,)),
            dma((8,)),
            dma((4,)),
            dma((4,)),
        ],
        compiler_params=pltpu.CompilerParams(
            collective_id=0, has_side_effects=True, vmem_limit_bytes=66_100_000
        ),
    )(
        vel, stress, buoy, lame, shear, stiff, drift, rate, coup, contact,
        dof.reshape(1, NB), owner.reshape(1, NB), corner.reshape(1, NB),
    )
    return pl.pallas_call(
        finish,
        out_shape=tuple(jax.ShapeDtypeStruct(s, F32) for s in shapes),
        in_specs=[near] * 3,
        out_specs=(anywhere,) * 3,
        scratch_shapes=[dma((3,))],
        compiler_params=pltpu.CompilerParams(vmem_limit_bytes=1024 * 1024),
    )(*outs)


def solution(mesh):
    placed = (
        P(None, None, "gx", "gy"),
        P(None, None, "gx", "gy"),
        P(None, "gx", "gy"),
        P(None, "gx", "gy"),
        P(None, "gx", "gy"),
        P(("gx", "gy"), None, None),
        P(("gx", "gy"), None),
        P(("gx", "gy"), None),
        P(("gx", "gy"), None),
        P(("gx", "gy"), None),
        P(("gx", "gy")),
        P(("gx", "gy"), None),
        P(("gx", "gy")),
    )
    return jax.shard_map(
        body,
        mesh=mesh,
        in_specs=placed,
        out_specs=(P(None, None, "gx", "gy"), P(("gx", "gy"), None), P(("gx", "gy"), None)),
        check_vma=False,
    )
```

```python
import jax
import jax.numpy as jnp
from jax import lax
from jax.experimental import pallas as pl
from jax.experimental.pallas import tpu as pltpu
from jax.sharding import PartitionSpec as P

MESH = pl.DeviceIdType.MESH
F32 = jnp.float32
BF16 = jnp.bfloat16
DT = 0.3
INNER = 9.0 / 8.0
OUTER = 1.0 / 24.0
FOOT = 8
GX, GY = 16, 8
NZ, CX, CY = 32, 16, 128
NB, DOF = 64, 256
SPAN = CY - FOOT + 1
ROWS = NZ * CX
GROUP, PARTS = 4, 4
PART = NZ // PARTS
HALF = NZ // 2
UNIT = DT / 24.0


def iota(shape, dim):
    return lax.broadcasted_iota(jnp.int32, shape, dim)


def mm(a, b, dims):
    return lax.dot_general(a, b, (dims, ((), ())), preferred_element_type=F32)


def split(x):
    hi = x.astype(BF16)
    return hi, (x - hi.astype(F32)).astype(BF16)


NN, NT = ((1,), (0,)), ((1,), (1,))


def pick_lhs(exact, value, dims):
    hi, lo = split(value)
    exact = exact.astype(BF16)
    return mm(exact, hi, dims) + mm(exact, lo, dims)


def pick_rhs(value, exact, dims):
    hi, lo = split(value)
    exact = exact.astype(BF16)
    return mm(hi, exact, dims) + mm(lo, exact, dims)


def kernel(
    vel, stress, buoy, lame, shear, stiff, drift, rate, coup, contact, dof, owner, corner,
    ovel, odrift, orate,
    vp, sp, mp, lam, av, kk, bd, ct, dofv, ownv, corv,
    dyb, sten, shb, shm,
    send_w, recv_w, send_p, recv_p, send_b, tab, send_q, recv_q, send_d, tab_q, wxt, forc,
    bm_s, m_r, m_p, m_q, rest, bds,
    b0, r0b, b1, r1b, b2, r2b, b3, r3b,
    ld, ldk, xa, xm, hs, hr,
):
    me_x = lax.axis_index("gx")
    me_y = lax.axis_index("gy")

    def wrap(value, n):
        return lax.rem(value + n, n)

    east, west = wrap(me_x + 1, GX), wrap(me_x - 1, GX)
    north, south = wrap(me_y + 1, GY), wrap(me_y - 1, GY)

    inner = (pl.ds(2, NZ), pl.ds(8, CX), slice(None))
    loads = [
        pltpu.make_async_copy(contact, ct, ld.at[0]),
        pltpu.make_async_copy(dof, dofv, ld.at[1]),
        pltpu.make_async_copy(owner, ownv, ld.at[2]),
        pltpu.make_async_copy(corner, corv, ld.at[3]),
        pltpu.make_async_copy(drift, bd.at[0], ld.at[4]),
        pltpu.make_async_copy(rate, bd.at[1], ld.at[5]),
        pltpu.make_async_copy(coup, bd.at[2], ld.at[6]),
        pltpu.make_async_copy(vel, vp.at[(slice(None),) + inner], ld.at[7]),
        pltpu.make_async_copy(buoy, mp.at[0, pl.ds(0, NZ), pl.ds(8, CX), :], ld.at[8]),
        pltpu.make_async_copy(shear, mp.at[1, pl.ds(0, NZ), pl.ds(8, CX), :], ld.at[9]),
        pltpu.make_async_copy(lame, lam, ld.at[10]),
        pltpu.make_async_copy(stress, sp.at[(slice(None),) + inner], ld.at[11]),
    ]
    kloads = [
        pltpu.make_async_copy(stiff.at[pl.ds(16 * i, 16)], kk.at[pl.ds(16 * i, 16)], ldk.at[i])
        for i in range(4)
    ]
    for c in loads[7:10] + loads[:7] + kloads + loads[10:]:
        c.start()

    barrier = pltpu.get_barrier_semaphore()

    def greet(gx, gy):
        pl.semaphore_signal(barrier, inc=1, device_id={"gx": gx, "gy": gy}, device_id_type=MESH)

    for d in range(1, GX):
        greet(wrap(me_x + d, GX), me_y)
    for d in range(1, GY):
        greet(me_x, wrap(me_y + d, GY))
    greet(west, south)
    greet(east, north)

    zero = jnp.zeros((2, 32, CY), F32)
    for f in range(3):
        vp[f, 0:2] = zero
        vp[f, 34:36] = zero
    for f in (2, 4, 5):
        sp[f, 0:2] = zero
        sp[f, 34:36] = zero
    mp[0, NZ] = zero[0]
    mp[1, NZ] = zero[0]
    shm[NZ] = zero[0]

    rows_v = vp.reshape(3 * 36 * 32, CY)
    rows_s = sp.reshape(6 * 36 * 32, CY)
    rows_m = mp.reshape(2 * 34 * 32, CY)
    lane16, row16 = iota((CX, CY), 1), iota((CX, CY), 0)
    row8, lane8 = iota((8, CY), 0), iota((8, CY), 1)

    def layer_rows(ref, field, depth, first, row):
        return ref[pl.ds((field * depth + first) * 32 + row, NZ, stride=32), :]

    def put_rows(ref, field, depth, first, row, value):
        ref[pl.ds((field * depth + first) * 32 + row, NZ, stride=32), :] = value

    keep_w = (me_x > 0).astype(F32)
    keep_e = (me_x < GX - 1).astype(F32)
    keep_s = (me_y > 0).astype(F32)
    keep_n = (me_y < GY - 1).astype(F32)

    pairs_v = [(0, 2, 1), (1, 1, 2), (2, 1, 2)]
    pairs_s = [(0, 1, 2), (3, 2, 1), (4, 2, 1)]

    def x_rows(pairs, part, inside):
        ups, downs = sum(p[1] for p in pairs), sum(p[2] for p in pairs)
        at = PART * ups * part
        for field, before, _ in pairs:
            for i in range(before):
                yield field, 8 - before + i + (CX if inside else 0), at, keep_w
                at += PART
        at = PART * (ups * PARTS + downs * part)
        for field, _, after in pairs:
            for i in range(after):
                yield field, 8 + i + (0 if inside else CX), at, keep_e
                at += PART

    def pack_x(ref, pairs, buf, part):
        for field, row, at, _ in x_rows(pairs, part, True):
            first = (field * 36 + 2 + PART * part) * 32 + row
            buf[pl.ds(at, PART), :] = ref[pl.ds(first, PART, stride=32), :]

    def unpack_x(ref, pairs, buf, parts=range(PARTS)):
        for part in parts:
            for field, row, at, keep in x_rows(pairs, part, False):
                first = (field * 36 + 2 + PART * part) * 32 + row
                ref[pl.ds(first, PART, stride=32), :] = buf[pl.ds(at, PART), :] * keep

    def pack_layer(total, value, k):
        return jnp.where(lane16 // 4 == k, pltpu.roll(value, 4 * k + 2, 1), total)

    def halo_of(packed, k):
        return pltpu.roll(packed, CY - 2 - 4 * k, 1)

    def merge_y(buf, at):
        from_south = buf[pl.ds(at[0], CX), :] * keep_s
        return jnp.where(lane16 % 4 >= 2, buf[pl.ds(at[1], CX), :] * keep_n, from_south)

    def halo_copies(buf, rbuf):
        def copy(slot, at, to, n, gx, gy):
            return pltpu.make_async_remote_copy(
                src_ref=buf.at[pl.ds(at, n)],
                dst_ref=rbuf.at[pl.ds(to, n)],
                send_sem=hs.at[slot],
                recv_sem=hr.at[slot],
                device_id={"gx": gx, "gy": gy},
                device_id_type=MESH,
            )

        return copy

    def halo_set(slot, buf, rbuf, up, down):
        copy = halo_copies(buf, rbuf)

        def x_part(part):
            a, b = up // PARTS, down // PARTS
            return [
                copy(slot + part // 2, a * part, a * part, a, east, me_y),
                copy(slot + part // 2, up + b * part, up + b * part, b, west, me_y),
            ]

        def y_half(h):
            y = up + down + 32 * h
            return [
                copy(slot + h, y, y, 32, me_x, north),
                copy(slot + h, y, y + 64, 32, me_x, south),
            ]

        return x_part, y_half

    def start(copies):
        for c in copies:
            c.start()

    def whole(slot, rbuf):
        return pltpu.make_async_remote_copy(
            src_ref=rbuf,
            dst_ref=rbuf,
            send_sem=hs.at[slot],
            recv_sem=hr.at[slot],
            device_id={"gx": east, "gy": me_y},
            device_id_type=MESH,
        )

    for i in range(7, 10):
        loads[i].wait()
    for part in range(PARTS):
        pack_x(rows_v, pairs_v, b0, part)
    b0[pl.ds(288, 32), :] = layer_rows(rows_m, 1, 34, 0, 8)

    def pack_columns(source, at):
        total = jnp.zeros((CX, CY), F32)
        for k in range(NZ):
            total = pack_layer(total, source(k), k)
        b0[pl.ds(at, 16), :] = total

    for f in range(3):
        pack_columns(lambda k, f=f: vp[f, k + 2, 8:24, :], 352 + 16 * f)
    pack_columns(lambda k: mp[1, k, 8:24, :], 400)
    copy0 = halo_copies(b0, r0b)
    halos0 = [
        copy0(0, 0, 0, 64, east, me_y),
        copy0(0, 128, 128, 80, west, me_y),
        copy0(0, 288, 288, 32, west, me_y),
        copy0(0, 352, 352, 48, me_x, north),
        copy0(0, 352, 416, 64, me_x, south),
        copy0(0, 400, 496, CX, west, south),
    ]
    late0 = [
        copy0(1, 64, 64, 64, east, me_y),
        copy0(1, 208, 208, 80, west, me_y),
        copy0(2, 320, 320, 32, west, me_y),
        copy0(2, 416, 480, CX, me_x, south),
    ]

    for i in range(7):
        loads[i].wait()
    eye = iota((NB, NB), 0) == iota((NB, NB), 1)

    def to_col(row):
        return jnp.sum(jnp.where(eye, jnp.broadcast_to(row, (NB, NB)), 0.0), axis=1, keepdims=True)

    dof_col = to_col(dofv[...].astype(F32))
    cor_col = to_col(corv[...].astype(F32))
    own_row = ownv[...].astype(F32)
    own_col = to_col(own_row)
    same = jnp.broadcast_to(own_col, (NB, NB)) == jnp.broadcast_to(own_row, (NB, NB))
    upper = iota((NB, NB), 0) < iota((NB, NB), 1)
    lower = iota((NB, NB), 0) > iota((NB, NB), 1)
    pos_row = jnp.sum(jnp.where(same & upper, 1.0, 0.0), axis=0, keepdims=True)
    pos_col = jnp.sum(jnp.where(same & lower, 1.0, 0.0), axis=1, keepdims=True)
    mask = iota((NB, DOF), 1).astype(F32) < dof_col
    cpl = jnp.where(mask, bd[2], 0.0)
    rate0 = jnp.where(mask, bd[1], 0.0)
    drift0 = jnp.where(mask, bd[0], 0.0)

    def gather_dofs(value, first):
        want = (iota((DOF, CY), 0) % 3 + first) == iota((DOF, CY), 1) // 16
        return pick_rhs(value, want.astype(F32), NN)

    lane = iota((NB, CY), 1)
    start_x = jnp.floor((cor_col + 0.5) * (1.0 / SPAN))
    start_y = cor_col - SPAN * start_x
    own_xc = jnp.floor((own_col + 0.5) * (1.0 / GY))
    own_yc = own_col - GY * own_xc
    own_xr = jnp.floor((own_row + 0.5) * (1.0 / GY))
    weights = ct[...] / jnp.sum(ct[...], axis=1, keepdims=True)
    twice = jnp.concatenate([weights, weights], axis=1)
    twice = jnp.where((lane // 64).astype(F32) == pos_col, twice, 0.0)
    to_tile = (iota((128, NB), 0).astype(F32) == own_row).astype(F32)
    send_w[...] = pick_lhs(to_tile, twice, NN).reshape(GX, GY, CY)
    to_column = (iota((GX, NB), 0).astype(F32) == own_xr).astype(F32)
    slot = (lane % 16).astype(F32) == pos_col * 8.0 + own_yc

    def by_column(value):
        return pick_lhs(to_column, jnp.where(slot, value, 0.0), NN).reshape(GX, 1, CY)

    info = gather_dofs(cpl * rate0, 0) + gather_dofs(cpl, 3)
    info = jnp.where(lane // 16 == 6, start_y, jnp.where(lane // 16 == 7, start_x, info))
    send_p[...] = by_column(info)

    pl.semaphore_wait(barrier, GX + GY)
    start(halos0)

    def along(src, dst, sems, base, gx, gy):
        return pltpu.make_async_remote_copy(
            src_ref=src,
            dst_ref=dst,
            send_sem=sems.at[base],
            recv_sem=sems.at[base + 1],
            device_id={"gx": gx, "gy": gy},
            device_id_type=MESH,
        )

    def over(n, me, action):
        def one(d, carry):
            action(wrap(me + d, n))
            return carry

        lax.fori_loop(1, n, one, 0)

    def to_gx(src, dst, base):
        over(GX, me_x, lambda peer: along(src.at[peer], dst.at[me_x], xa, base, peer, me_y).start())
        dst[me_x] = src[me_x]

    def to_gy(src, dst, base):
        over(GY, me_y, lambda peer: along(src.at[peer], dst.at[me_y], xa, base, me_x, peer).start())
        dst[me_y] = src[me_y]

    def all_of(ref, sems, base):
        n = ref.shape[0] - 1
        return along(ref.at[pl.ds(0, n)], ref.at[pl.ds(0, n)], sems, base, east, me_y)

    to_gx(send_w, recv_w, 0)
    to_gx(send_p, recv_p, 2)
    start(late0[:2])
    b0[pl.ds(320, 32), :] = layer_rows(rows_m, 0, 34, 0, 8)
    pack_columns(lambda k: mp[0, k, 8:24, :], 416)
    start(late0[2:])

    def restore(value):
        bds[...] = value.astype(BF16)

        def block(i, carry):
            mine = bds[pl.ds(pl.multiple_of(16 * i, 16), 16), :]
            row = iota((16, DOF), 0)
            total = jnp.zeros((16, DOF), F32)
            for b in range(16):
                part = mm(mine, kk[16 * i + b], NT)
                total = jnp.where(row == b, part, total)
            rest[pl.ds(pl.multiple_of(16 * i, 16), 16), :] = total
            return carry

        lax.fori_loop(0, 4, block, 0)

    for c in kloads:
        c.wait()
    restore(drift0)
    rest0 = rest[...]

    moved = rate0 - DT * rest0 - DT * cpl * rate0
    send_q[...] = by_column(gather_dofs(DT * cpl * cpl, 0) + gather_dofs(cpl * moved, 3))
    to_gx(send_q, recv_q, 6)

    def stencil(points):
        row, col = iota((256, CY), 0) % CY, iota((256, CY), 1)
        total = jnp.zeros((256, CY), F32)
        for offset, weight in points.items():
            total = jnp.where(row == col + offset, weight, total)
        return total.astype(BF16)

    sten[0] = stencil({1: 27.0, 0: -27.0, 2: -1.0, -1: 1.0})
    sten[1] = stencil({0: 27.0, -1: -27.0, 1: -1.0, -2: 1.0})
    sten[2] = stencil({1: 1.0})

    def along_y(value, kind):
        hi, lo = split(value.reshape(ROWS, CY))
        return mm(jnp.concatenate([hi, lo], axis=1), sten[kind], NN).reshape(NZ, CX, CY)

    def y_parts(ref, fields, kinds):
        for i in range(3):
            dyb[i] = along_y(ref[fields[i], pl.ds(2, NZ), pl.ds(8, CX), :], kinds[i])

    y_parts(vp, (0, 1, 2), (0, 1, 0))
    shb[...] = along_y(mp[0, pl.ds(0, NZ), pl.ds(8, CX), :], 2)
    shm[pl.ds(0, NZ), pl.ds(8, CX), :] = along_y(mp[1, pl.ds(0, NZ), pl.ds(8, CX), :], 2)

    whole(0, r0b.at[pl.ds(0, 304)]).wait_recv()
    all_of(recv_w, xa, 0).wait_recv()
    all_of(recv_p, xa, 2).wait_recv()
    info = recv_p[...].reshape(GX, CY)
    for j in range(GY):
        send_b[j, 0:16, :] = recv_w.reshape(GX * GY, CY)[pl.ds(j, GX, stride=8), :]
        send_b[j, 16:32, :] = info
    to_gy(send_b, tab, 4)
    unpack_x(rows_v, pairs_v, r0b, (0, 1))
    put_rows(rows_m, 1, 34, 0, 24, r0b[pl.ds(288, 32), :])
    def reach(packed, forward):
        at = lane16 % 4
        up1, dn1 = pltpu.roll(packed, CY - 1, 1), pltpu.roll(packed, 1, 1)
        if forward:
            up2 = pltpu.roll(packed, CY - 2, 1)
            return jnp.where(
                at == 0, -up2, jnp.where(at == 1, 27.0 * up1 - up2, jnp.where(at == 2, dn1, 0.0))
            )
        dn2 = pltpu.roll(packed, 2, 1)
        return jnp.where(
            at == 0, 0.0, jnp.where(at == 1, -up1, jnp.where(at == 2, dn2 - 27.0 * dn1, dn2))
        )

    reach_v = [
        reach(merge_y(r0b, (352 + 16 * f, 416 + 16 * f)), forward)
        for f, forward in enumerate((True, False, True))
    ]
    packed_m = r0b[pl.ds(464, CX), :]

    out_x = (row16 == CX - 1) & (me_x == GX - 1)
    out_y = (lane16 == CY - 1) & (me_y == GY - 1)
    out_xy = out_x | out_y
    last_lane = lane16 == CY - 1
    edge = (lane16 < 2) | (lane16 >= CY - 2)

    def to_last(packed, k):
        return pltpu.roll(packed, lax.rem(2 * CY - 3 - 4 * k, CY), 1)

    def average_b(k, carry):
        b = mp[0, k, 8:24, :]
        bx = jnp.where(out_x, b, mp[0, k, 9:25, :])
        by = jnp.where(out_y, b, jnp.where(last_lane, to_last(packed_b, k), shb[k]))
        bz = jnp.where(k == NZ - 1, b, mp[0, k + 1, 8:24, :])
        av[0, k] = (b + bx) * (0.5 * UNIT)
        av[1, k] = (b + by) * (0.5 * UNIT)
        av[2, k] = (b + bz) * (0.5 * UNIT)
        return carry

    def average_m(k, carry):
        last = k == NZ - 1
        m = mp[1, k, 8:24, :]
        mx = jnp.where(out_x, m, mp[1, k, 9:25, :])
        my = jnp.where(out_y, m, shm[k, 8:24, :])
        mxy = jnp.where(out_xy, m, shm[k, 9:25, :])
        mz = jnp.where(last, m, mp[1, k + 1, 8:24, :])
        mxz = jnp.where(out_x | last, m, mp[1, k + 1, 9:25, :])
        myz = jnp.where(out_y | last, m, shm[k + 1, 8:24, :])
        av[3, k] = (m + mx + my + mxy) * (0.25 * UNIT)
        av[4, k] = (m + mx + mz + mxz) * (0.25 * UNIT)
        av[5, k] = (m + my + mz + myz) * (0.25 * UNIT)
        return carry

    def join(k, carry):
        shm[k, 8:24, :] = jnp.where(last_lane, to_last(packed_m, k), shm[k, 8:24, :])
        return carry

    def layers(action, init, first=0, last=NZ // GROUP):
        def group(i, carry):
            for j in range(GROUP):
                carry = action(GROUP * i + j, carry)
            return carry

        return lax.fori_loop(first, last, group, init)

    layers(join, 0)
    lane32, row32 = iota((NZ, CY), 1), iota((NZ, CY), 0)
    corners = jnp.broadcast_to(r0b[pl.ds(496, 8), :][0:1, :], (NZ, CY))
    corners = jnp.sum(jnp.where(lane32 == 4 * row32 + 2, corners, 0.0), axis=1, keepdims=True)
    eastern = pltpu.roll(r0b[pl.ds(288, NZ), :], CY - 1, 1)
    eastern = jnp.where(lane32 == CY - 1, corners, eastern)
    put_rows(shm.reshape(33 * 32, CY), 0, 33, 0, 24, eastern)
    layers(average_m, 0)

    def fwd(minus, zero_, plus, plus2):
        return 27.0 * (plus - zero_) - (plus2 - minus)

    def bwd(minus2, minus, zero_, plus):
        return 27.0 * (zero_ - minus) - (plus - minus2)

    def dx(ref, f, k, forward):
        first = 7 if forward else 6
        parts = [ref[f, k + 2, first + i : first + i + CX, :] for i in range(4)]
        return (fwd if forward else bwd)(*parts)

    def dz(ref, f, k, forward):
        first = 1 if forward else 0
        parts = [ref[f, k + first + i, 8:24, :] for i in range(4)]
        return (fwd if forward else bwd)(*parts)

    def dy(reaches, i, k):
        return dyb[i, k] + jnp.where(edge, reaches(i, k), 0.0)

    def pack_half(carry, values, k):
        first = pack_layer(pack_layer(carry[0], values[0], k), values[1], k + HALF)
        return first, pack_layer(carry[1], values[2], k)

    def stress_layer(reaches, h, k, carry):
        sx, sy, sz = dx(vp, 0, k, False), dy(reaches, 1, k), dz(vp, 2, k, False)
        m2 = (2.0 * UNIT) * mp[1, k, 8:24, :]
        volume = (UNIT * lam[k]) * (sx + sy + sz)
        new = {}
        for f, s in ((0, sx), (1, sy), (2, sz)):
            new[f] = sp[f, k + 2, 8:24, :] + (volume + m2 * s)
        shear_xy = dy(reaches, 0, k) + dx(vp, 1, k, True)
        shear_xz = dz(vp, 0, k, True) + dx(vp, 2, k, True)
        shear_yz = dz(vp, 1, k, True) + dy(reaches, 2, k)
        for f, s in ((3, shear_xy), (4, shear_xz), (5, shear_yz)):
            new[f] = sp[f, k + 2, 8:24, :] + av[f, k] * s
        for f in range(6):
            sp[f, k + 2, 8:24, :] = new[f]
        return pack_half(carry, (new[3], new[1], new[5]), k - HALF * h)

    def velocity_layer(reaches, out, surface, h, k, carry):
        ax = dx(sp, 0, k, True) + dy(reaches, 0, k) + dz(sp, 4, k, False)
        ay = dx(sp, 3, k, False) + dy(reaches, 1, k) + dz(sp, 5, k, False)
        az = dx(sp, 4, k, False) + dy(reaches, 2, k) + dz(sp, 2, k, True)
        new = []
        for f, a in ((0, ax), (1, ay), (2, az)):
            value = vp[f, k + 2, 8:24, :] + av[f, k] * a
            if surface:
                value = value + forc[f]
            new.append(value)
            if out is None:
                vp[f, k + 2, 8:24, :] = value
            else:
                out[f, k] = value
        return pack_half(carry, new, k - HALF * h) if carry else carry

    def received(slot, ref, pairs, rbuf, kinds):
        def begin(h):
            whole(slot + h, rbuf.at[pl.ds(0, 208)]).wait_recv()
            unpack_x(ref, pairs, rbuf, (2 * h, 2 * h + 1))
            south_at, north_at = 288 + 32 * h, 352 + 32 * h
            merged = [merge_y(rbuf, (south_at + 16 * i, north_at + 16 * i)) for i in range(2)]
            fields = [reach(merged[i // 2], kinds[i]) for i in range(3)]
            return lambda i, k: halo_of(fields[i], k - HALF * h + (HALF if i == 1 else 0))

        return begin

    count = PART // GROUP
    blank = (jnp.zeros((CX, CY), F32),) * 2

    def send_half(buf, halos, carry, h):
        for i in range(2):
            buf[pl.ds(288 + 32 * h + 16 * i, 16), :] = carry[i]
        start(halos[1](h))

    def stress_step(begin, buf, halos):
        for h in range(2):
            reaches, carry = begin(h), blank
            for part in (2 * h, 2 * h + 1):
                carry = layers(
                    lambda k, c: stress_layer(reaches, h, k, c), carry, count * part, count * part + count
                )
                pack_x(rows_s, pairs_s, buf, part)
                start(halos[0](part))
            send_half(buf, halos, carry, h)

    def velocity_step(begin, out, buf, halos):
        for h in range(2):
            reaches, carry = begin(h), () if buf is None else blank
            for part in (2 * h, 2 * h + 1):
                first = count * part
                if part == 0:
                    for k in range(GROUP):
                        carry = velocity_layer(reaches, out, k == 0, h, k, carry)
                    first = 1
                carry = layers(
                    lambda k, c: velocity_layer(reaches, out, False, h, k, c),
                    carry,
                    first,
                    count * part + count,
                )
                if buf is not None:
                    pack_x(rows_v, pairs_v, buf, part)
                    start(halos[0](part))
            if buf is not None:
                send_half(buf, halos, carry, h)

    loads[10].wait()
    loads[11].wait()
    halos1 = halo_set(3, b1, r1b, 160, 128)

    def begin_first(h):
        if h == 1:
            whole(1, r0b.at[pl.ds(0, 144)]).wait_recv()
            unpack_x(rows_v, pairs_v, r0b, (2, 3))
        return lambda i, k: halo_of(reach_v[i], k)

    stress_step(begin_first, b1, halos1)
    y_parts(sp, (3, 1, 5), (1, 0, 1))
    whole(2, r0b.at[pl.ds(0, 48)]).wait_recv()
    put_rows(rows_m, 0, 34, 0, 24, r0b[pl.ds(320, 32), :])
    packed_b = r0b[pl.ds(480, CX), :]
    layers(average_b, 0)

    all_of(tab, xa, 4).wait_recv()
    row128, lane128 = iota((128, CY), 0), iota((128, CY), 1)
    sel = iota((16, CY), 1) == (iota((16, CY), 0) % 8) * 16 + (iota((16, CY), 0) // 8) * 8 + me_y

    def by_slot(value):
        both = pick_lhs(sel.astype(F32), value, NT)
        return jnp.concatenate([both[0:8], both[8:16]], axis=1)

    params = by_slot(tab[:, 16:32, :].reshape(128, CY))
    r0, c0 = params, pltpu.roll(params, 5, 0)
    sent = tab[:, 0:16, :].reshape(128, CY)
    for p in range(2):
        want = (row128 % CX < FOOT) & (lane128 == 64 * p + (row128 % CX) * FOOT + row128 // CX)
        placed = pick_lhs(want.astype(F32), sent, NT)
        shift = jnp.broadcast_to(params[7:8, 128 * p : 128 * p + 128], (128, CY)).astype(jnp.int32)
        for bit in (1, 2, 4, 8):
            placed = jnp.where((shift & bit) != 0, pltpu.roll(placed, bit, 0), placed)
        wxt[:, 128 * p : 128 * p + 128] = placed
    oyt = (iota((CY, 256), 0).astype(F32) == params[6:7]).astype(F32).astype(BF16)

    def motion():
        total = jnp.zeros((8, 256), F32)
        row = iota((8, 256), 0)
        for f in range(3):
            value = vp[f, 2, 8:24, :]
            turns = [value] + [pltpu.roll(value, CY - c, 1) for c in range(1, FOOT)]
            hi, lo = split(jnp.concatenate(turns, axis=0))
            found = mm(hi, oyt, NN) + mm(lo, oyt, NN)
            one = jnp.sum(found * wxt[...], axis=0, keepdims=True)
            total = jnp.where(row == f, jnp.broadcast_to(one, (8, 256)), total)
        return total

    def push(reaction):
        reaction = reaction * (DT * FOOT)
        for f in range(3):
            hi, lo = split(wxt[...] * reaction[f : f + 1])
            spread = mm(hi, oyt, NT) + mm(lo, oyt, NT)
            total = spread[0:CX]
            for c in range(1, FOOT):
                total = total + pltpu.roll(spread[CX * c : CX * c + CX], c, 1)
            forc[f] = total

    def send_motion(step, value):
        bm_s[step] = jnp.where(row8 < 4, value[:, 0:128], pltpu.roll(value[:, 128:256], 4, 0))
        over(
            GY,
            me_y,
            lambda peer: along(
                bm_s.at[step], m_r.at[step, me_y], xm, 4 * step, me_x, peer
            ).start(),
        )
        m_r[step, me_y] = bm_s[step]

    def pass_motion(step):
        all_of(m_r.at[step], xm, 4 * step).wait_recv()
        want = (iota((GX, CY), 1) == iota((GX, CY), 0) + GX * me_y).astype(F32)
        rows = pick_lhs(want, m_r[step].reshape(GY * 8, CY), NT)
        rows = jnp.concatenate([rows, jnp.zeros((GX, CY - GY * 8), F32)], axis=1)
        m_p[step] = rows.reshape(GX, 1, CY)
        over(
            GX,
            me_x,
            lambda peer: along(
                m_p.at[step, peer], m_q.at[step, me_x], xm, 4 * step + 2, peer, me_y
            ).start(),
        )
        m_q[step, me_x] = m_p[step, me_x]

    want_lane = own_yc * 2.0 + pos_col
    own_gx = (iota((NB, GX), 1).astype(F32) == own_xc).astype(F32)

    def take_motion(step):
        all_of(m_q.at[step], xm, 4 * step + 2).wait_recv()
        found = pick_lhs(own_gx, m_q[step].reshape(GX, CY), NN)
        found = jnp.where((lane // 4).astype(F32) == want_lane, found, 0.0)
        onto = (iota((CY, DOF), 0) % 4 == iota((CY, DOF), 1) % 3).astype(F32)
        return pick_rhs(found, onto, NN)

    bm1 = motion()
    send_motion(0, bm1)
    push(r0 - c0 * bm1)

    all_of(recv_q, xa, 6).wait_recv()
    send_d[...] = recv_q[...].reshape(GX, CY)
    over(GY, me_y, lambda peer: along(send_d, tab_q.at[me_y], xa, 8, me_x, peer).start())
    tab_q[me_y] = send_d[...]

    kinds_s, kinds_v = (False, True, False), (True, False, True)
    halos2 = halo_set(5, b2, r2b, 128, 160)
    velocity_step(received(3, rows_s, pairs_s, r1b, kinds_s), None, b2, halos2)

    bm2 = motion()
    send_motion(1, bm2)
    y_parts(vp, (0, 1, 2), (0, 1, 0))
    pass_motion(0)
    all_of(tab_q, xa, 8).wait_recv()
    params = by_slot(tab_q[...].reshape(128, CY))
    push(pltpu.roll(params, 5, 0) + params * bm1 - c0 * bm2)

    halos3 = halo_set(7, b3, r3b, 160, 128)
    stress_step(received(5, rows_v, pairs_v, r2b, kinds_v), b3, halos3)
    y_parts(sp, (3, 1, 5), (1, 0, 1))

    pass_motion(1)

    def advance(rates, drifts, restoring, base):
        relative = jnp.where(mask, rates - base, 0.0)
        rates = jnp.where(mask, rates - DT * restoring - DT * cpl * relative, 0.0)
        return rates, jnp.where(mask, drifts + DT * rates, 0.0)

    rate1, drift1 = advance(rate0, drift0, rest0, take_motion(0))
    restore(drift1)

    velocity_step(received(7, rows_s, pairs_s, r3b, kinds_s), ovel, None, None)
    rate2, drift2 = advance(rate1, drift1, rest[...], take_motion(1))
    odrift[...] = drift2
    orate[...] = rate2

    for slot, n in enumerate((304, 144, 48)):
        whole(slot, r0b.at[pl.ds(0, n)]).wait_send()
    for slot in range(3, 9):
        whole(slot, r1b.at[pl.ds(0, 208)]).wait_send()
    for ref, base in ((recv_w, 0), (recv_p, 2), (tab, 4), (recv_q, 6), (tab_q, 8)):
        all_of(ref, xa, base).wait_send()
    for step in range(2):
        all_of(m_r.at[step], xm, 4 * step).wait_send()
        all_of(m_q.at[step], xm, 4 * step + 2).wait_send()


def finish(vel, drift, rate, ovel, odrift, orate, sem):
    copies = [
        pltpu.make_async_copy(vel, ovel, sem.at[0]),
        pltpu.make_async_copy(drift, odrift, sem.at[1]),
        pltpu.make_async_copy(rate, orate, sem.at[2]),
    ]
    for c in copies:
        c.start()
    for c in copies:
        c.wait()


def body(vel, stress, buoy, lame, shear, stiff, drift, rate, coup, contact, dof, owner, corner):
    anywhere = pl.BlockSpec(memory_space=pltpu.HBM)
    vmem = pltpu.VMEM
    near = pl.BlockSpec(memory_space=vmem)
    dma = pltpu.SemaphoreType.DMA
    halo = [vmem((512, CY), F32), vmem((528, CY), F32)] + [vmem((352, CY), F32), vmem((416, CY), F32)] * 3
    shapes = ((3, NZ, CX, CY), (NB, DOF), (NB, DOF))
    outs = pl.pallas_call(
        kernel,
        out_shape=tuple(vmem(s, F32) for s in shapes),
        in_specs=[anywhere] * 13,
        out_specs=(near,) * 3,
        scratch_shapes=[
            vmem((3, 36, 32, CY), F32),
            vmem((6, 36, 32, CY), F32),
            vmem((2, 34, 32, CY), F32),
            vmem((NZ, CX, CY), F32),
            vmem((6, NZ, CX, CY), F32),
            vmem((NB, DOF, DOF), BF16),
            vmem((3, NB, DOF), F32),
            vmem((NB, 64), F32),
            vmem((1, NB), jnp.int32),
            vmem((1, NB), jnp.int32),
            vmem((1, NB), jnp.int32),
            vmem((3, NZ, CX, CY), F32),
            vmem((3, 256, CY), BF16),
            vmem((NZ, CX, CY), F32),
            vmem((33, 32, CY), F32),
            vmem((GX, GY, CY), F32),
            vmem((GX, GY, CY), F32),
            vmem((GX, 1, CY), F32),
            vmem((GX, 1, CY), F32),
            vmem((GY, 32, CY), F32),
            vmem((GY, 32, CY), F32),
            vmem((GX, 1, CY), F32),
            vmem((GX, 1, CY), F32),
            vmem((GX, CY), F32),
            vmem((GY, GX, CY), F32),
            vmem((128, 256), F32),
            vmem((3, CX, CY), F32),
            vmem((2, 8, CY), F32),
            vmem((2, GY, 8, CY), F32),
            vmem((2, GX, 1, CY), F32),
            vmem((2, GX, 1, CY), F32),
            vmem((NB, DOF), F32),
            vmem((NB, DOF), BF16),
            *halo,
            dma((12,)),
            dma((4,)),
            dma((10,)),
            dma((8,)),
            dma((9,)),
            dma((9,)),
        ],
        compiler_params=pltpu.CompilerParams(
            collective_id=0, has_side_effects=True, vmem_limit_bytes=66_100_000
        ),
    )(
        vel, stress, buoy, lame, shear, stiff, drift, rate, coup, contact,
        dof.reshape(1, NB), owner.reshape(1, NB), corner.reshape(1, NB),
    )
    return pl.pallas_call(
        finish,
        out_shape=tuple(jax.ShapeDtypeStruct(s, F32) for s in shapes),
        in_specs=[near] * 3,
        out_specs=(anywhere,) * 3,
        scratch_shapes=[dma((3,))],
        compiler_params=pltpu.CompilerParams(vmem_limit_bytes=1024 * 1024),
    )(*outs)


def solution(mesh):
    placed = (
        P(None, None, "gx", "gy"),
        P(None, None, "gx", "gy"),
        P(None, "gx", "gy"),
        P(None, "gx", "gy"),
        P(None, "gx", "gy"),
        P(("gx", "gy"), None, None),
        P(("gx", "gy"), None),
        P(("gx", "gy"), None),
        P(("gx", "gy"), None),
        P(("gx", "gy"), None),
        P(("gx", "gy")),
        P(("gx", "gy"), None),
        P(("gx", "gy")),
    )
    return jax.shard_map(
        body,
        mesh=mesh,
        in_specs=placed,
        out_specs=(P(None, None, "gx", "gy"), P(("gx", "gy"), None), P(("gx", "gy"), None)),
        check_vma=False,
    )
```

```python
import jax
import jax.numpy as jnp
from jax import lax
from jax.experimental import pallas as pl
from jax.experimental.pallas import tpu as pltpu
from jax.sharding import PartitionSpec as P

MESH = pl.DeviceIdType.MESH
F32 = jnp.float32
BF16 = jnp.bfloat16
DT = 0.3
INNER = 9.0 / 8.0
OUTER = 1.0 / 24.0
FOOT = 8
GX, GY = 16, 8
NZ, CX, CY = 32, 16, 128
NB, DOF = 64, 256
SPAN = CY - FOOT + 1
ROWS = NZ * CX
GROUP, PARTS = 4, 4
PART = NZ // PARTS
HALF = NZ // 2
UNIT = DT / 24.0


def iota(shape, dim):
    return lax.broadcasted_iota(jnp.int32, shape, dim)


def mm(a, b, dims):
    return lax.dot_general(a, b, (dims, ((), ())), preferred_element_type=F32)


def split(x):
    hi = x.astype(BF16)
    return hi, (x - hi.astype(F32)).astype(BF16)


NN, NT = ((1,), (0,)), ((1,), (1,))


def pick_lhs(exact, value, dims):
    hi, lo = split(value)
    exact = exact.astype(BF16)
    return mm(exact, hi, dims) + mm(exact, lo, dims)


def pick_rhs(value, exact, dims):
    hi, lo = split(value)
    exact = exact.astype(BF16)
    return mm(hi, exact, dims) + mm(lo, exact, dims)


def kernel(
    vel, stress, buoy, lame, shear, stiff, drift, rate, coup, contact, dof, owner, corner,
    ovel, odrift, orate,
    vp, sp, mp, lam, av, kk, bd, ct, dofv, ownv, corv,
    dyb, sten, shb, shm,
    send_w, recv_w, send_p, recv_p, send_b, tab, send_q, recv_q, send_d, tab_q, wxt, forc,
    bm_s, m_r, m_p, m_q, rest, bds,
    b0, r0b, b1, r1b, b2, r2b, b3, r3b,
    ld, ldk, xa, xm, hs, hr,
):
    me_x = lax.axis_index("gx")
    me_y = lax.axis_index("gy")

    def wrap(value, n):
        return lax.rem(value + n, n)

    east, west = wrap(me_x + 1, GX), wrap(me_x - 1, GX)
    north, south = wrap(me_y + 1, GY), wrap(me_y - 1, GY)

    inner = (pl.ds(2, NZ), pl.ds(8, CX), slice(None))
    loads = [
        pltpu.make_async_copy(contact, ct, ld.at[0]),
        pltpu.make_async_copy(dof, dofv, ld.at[1]),
        pltpu.make_async_copy(owner, ownv, ld.at[2]),
        pltpu.make_async_copy(corner, corv, ld.at[3]),
        pltpu.make_async_copy(drift, bd.at[0], ld.at[4]),
        pltpu.make_async_copy(rate, bd.at[1], ld.at[5]),
        pltpu.make_async_copy(coup, bd.at[2], ld.at[6]),
        pltpu.make_async_copy(vel, vp.at[(slice(None),) + inner], ld.at[7]),
        pltpu.make_async_copy(buoy, mp.at[0, pl.ds(0, NZ), pl.ds(8, CX), :], ld.at[8]),
        pltpu.make_async_copy(shear, mp.at[1, pl.ds(0, NZ), pl.ds(8, CX), :], ld.at[9]),
        pltpu.make_async_copy(lame, lam, ld.at[10]),
        pltpu.make_async_copy(stress, sp.at[(slice(None),) + inner], ld.at[11]),
    ]

    def kload(i):
        at = pl.ds(16 * i, 16)
        return pltpu.make_async_copy(stiff.at[at], kk.at[at], ldk.at[i])

    kloads = [kload(i) for i in range(4)]
    for c in loads[7:10] + loads[:7]:
        c.start()

    barrier = pltpu.get_barrier_semaphore()

    def greet(gx, gy):
        pl.semaphore_signal(barrier, inc=1, device_id={"gx": gx, "gy": gy}, device_id_type=MESH)

    for d in range(1, GX):
        greet(wrap(me_x + d, GX), me_y)
    for d in range(1, GY):
        greet(me_x, wrap(me_y + d, GY))
    greet(west, south)
    greet(east, north)

    zero = jnp.zeros((2, 32, CY), F32)
    for f in range(3):
        vp[f, 0:2] = zero
        vp[f, 34:36] = zero
    for f in (2, 4, 5):
        sp[f, 0:2] = zero
        sp[f, 34:36] = zero
    mp[0, NZ] = zero[0]
    mp[1, NZ] = zero[0]
    shm[NZ] = zero[0]

    rows_v = vp.reshape(3 * 36 * 32, CY)
    rows_s = sp.reshape(6 * 36 * 32, CY)
    rows_m = mp.reshape(2 * 34 * 32, CY)
    lane16, row16 = iota((CX, CY), 1), iota((CX, CY), 0)
    row8, lane8 = iota((8, CY), 0), iota((8, CY), 1)

    def layer_rows(ref, field, depth, first, row):
        return ref[pl.ds((field * depth + first) * 32 + row, NZ, stride=32), :]

    def put_rows(ref, field, depth, first, row, value):
        ref[pl.ds((field * depth + first) * 32 + row, NZ, stride=32), :] = value

    keep_w = (me_x > 0).astype(F32)
    keep_e = (me_x < GX - 1).astype(F32)
    keep_s = (me_y > 0).astype(F32)
    keep_n = (me_y < GY - 1).astype(F32)

    pairs_v = [(0, 2, 1), (1, 1, 2), (2, 1, 2)]
    pairs_s = [(0, 1, 2), (3, 2, 1), (4, 2, 1)]

    def x_rows(pairs, part, inside):
        ups, downs = sum(p[1] for p in pairs), sum(p[2] for p in pairs)
        at = PART * ups * part
        for field, before, _ in pairs:
            for i in range(before):
                yield field, 8 - before + i + (CX if inside else 0), at, keep_w
                at += PART
        at = PART * (ups * PARTS + downs * part)
        for field, _, after in pairs:
            for i in range(after):
                yield field, 8 + i + (0 if inside else CX), at, keep_e
                at += PART

    def pack_x(ref, pairs, buf, part):
        for field, row, at, _ in x_rows(pairs, part, True):
            first = (field * 36 + 2 + PART * part) * 32 + row
            buf[pl.ds(at, PART), :] = ref[pl.ds(first, PART, stride=32), :]

    def unpack_x(ref, pairs, buf, parts=range(PARTS)):
        for part in parts:
            for field, row, at, keep in x_rows(pairs, part, False):
                first = (field * 36 + 2 + PART * part) * 32 + row
                ref[pl.ds(first, PART, stride=32), :] = buf[pl.ds(at, PART), :] * keep

    def pack_layer(total, value, k):
        return jnp.where(lane16 // 4 == k, pltpu.roll(value, 4 * k + 2, 1), total)

    def halo_of(packed, k):
        return pltpu.roll(packed, CY - 2 - 4 * k, 1)

    def merge_y(buf, at):
        from_south = buf[pl.ds(at[0], CX), :] * keep_s
        return jnp.where(lane16 % 4 >= 2, buf[pl.ds(at[1], CX), :] * keep_n, from_south)

    def halo_copies(buf, rbuf):
        def copy(slot, at, to, n, gx, gy):
            return pltpu.make_async_remote_copy(
                src_ref=buf.at[pl.ds(at, n)],
                dst_ref=rbuf.at[pl.ds(to, n)],
                send_sem=hs.at[slot],
                recv_sem=hr.at[slot],
                device_id={"gx": gx, "gy": gy},
                device_id_type=MESH,
            )

        return copy

    def halo_set(slot, buf, rbuf, up, down):
        copy = halo_copies(buf, rbuf)

        def x_part(part):
            a, b = up // PARTS, down // PARTS
            return [
                copy(slot + part // 2, a * part, a * part, a, east, me_y),
                copy(slot + part // 2, up + b * part, up + b * part, b, west, me_y),
            ]

        def y_half(h):
            y = up + down + 32 * h
            return [
                copy(slot + h, y, y, 32, me_x, north),
                copy(slot + h, y, y + 64, 32, me_x, south),
            ]

        return x_part, y_half

    def start(copies):
        for c in copies:
            c.start()

    def whole(slot, rbuf):
        return pltpu.make_async_remote_copy(
            src_ref=rbuf,
            dst_ref=rbuf,
            send_sem=hs.at[slot],
            recv_sem=hr.at[slot],
            device_id={"gx": east, "gy": me_y},
            device_id_type=MESH,
        )

    for i in range(7, 10):
        loads[i].wait()
    for c in kloads:
        c.start()
    for part in range(PARTS):
        pack_x(rows_v, pairs_v, b0, part)
    b0[pl.ds(288, 32), :] = layer_rows(rows_m, 1, 34, 0, 8)

    def pack_columns(source, at):
        total = jnp.zeros((CX, CY), F32)
        for k in range(NZ):
            total = pack_layer(total, source(k), k)
        b0[pl.ds(at, 16), :] = total

    for f in range(3):
        pack_columns(lambda k, f=f: vp[f, k + 2, 8:24, :], 352 + 16 * f)
    pack_columns(lambda k: mp[1, k, 8:24, :], 400)
    copy0 = halo_copies(b0, r0b)
    halos0 = [
        copy0(0, 0, 0, 64, east, me_y),
        copy0(0, 128, 128, 80, west, me_y),
        copy0(0, 288, 288, 32, west, me_y),
        copy0(0, 352, 352, 48, me_x, north),
        copy0(0, 352, 416, 64, me_x, south),
        copy0(0, 400, 496, CX, west, south),
    ]
    late0 = [
        copy0(1, 64, 64, 64, east, me_y),
        copy0(1, 208, 208, 80, west, me_y),
        copy0(2, 320, 320, 32, west, me_y),
        copy0(2, 416, 480, CX, me_x, south),
    ]

    for i in range(7):
        loads[i].wait()
    for c in loads[10:]:
        c.start()
    eye = iota((NB, NB), 0) == iota((NB, NB), 1)

    def to_col(row):
        return jnp.sum(jnp.where(eye, jnp.broadcast_to(row, (NB, NB)), 0.0), axis=1, keepdims=True)

    dof_col = to_col(dofv[...].astype(F32))
    cor_col = to_col(corv[...].astype(F32))
    own_row = ownv[...].astype(F32)
    own_col = to_col(own_row)
    same = jnp.broadcast_to(own_col, (NB, NB)) == jnp.broadcast_to(own_row, (NB, NB))
    upper = iota((NB, NB), 0) < iota((NB, NB), 1)
    lower = iota((NB, NB), 0) > iota((NB, NB), 1)
    pos_row = jnp.sum(jnp.where(same & upper, 1.0, 0.0), axis=0, keepdims=True)
    pos_col = jnp.sum(jnp.where(same & lower, 1.0, 0.0), axis=1, keepdims=True)
    mask = iota((NB, DOF), 1).astype(F32) < dof_col
    cpl = jnp.where(mask, bd[2], 0.0)
    rate0 = jnp.where(mask, bd[1], 0.0)
    drift0 = jnp.where(mask, bd[0], 0.0)

    def gather_dofs(value, first):
        want = (iota((DOF, CY), 0) % 3 + first) == iota((DOF, CY), 1) // 16
        return pick_rhs(value, want.astype(F32), NN)

    lane = iota((NB, CY), 1)
    start_x = jnp.floor((cor_col + 0.5) * (1.0 / SPAN))
    start_y = cor_col - SPAN * start_x
    own_xc = jnp.floor((own_col + 0.5) * (1.0 / GY))
    own_yc = own_col - GY * own_xc
    own_xr = jnp.floor((own_row + 0.5) * (1.0 / GY))
    weights = ct[...] / jnp.sum(ct[...], axis=1, keepdims=True)
    twice = jnp.concatenate([weights, weights], axis=1)
    twice = jnp.where((lane // 64).astype(F32) == pos_col, twice, 0.0)
    to_tile = (iota((128, NB), 0).astype(F32) == own_row).astype(F32)
    send_w[...] = pick_lhs(to_tile, twice, NN).reshape(GX, GY, CY)
    to_column = (iota((GX, NB), 0).astype(F32) == own_xr).astype(F32)
    slot = (lane % 16).astype(F32) == pos_col * 8.0 + own_yc

    def by_column(value):
        return pick_lhs(to_column, jnp.where(slot, value, 0.0), NN).reshape(GX, 1, CY)

    info = gather_dofs(cpl * rate0, 0) + gather_dofs(cpl, 3)
    info = jnp.where(lane // 16 == 6, start_y, jnp.where(lane // 16 == 7, start_x, info))
    send_p[...] = by_column(info)

    pl.semaphore_wait(barrier, GX + GY)
    start(halos0)

    def along(src, dst, sems, base, gx, gy):
        return pltpu.make_async_remote_copy(
            src_ref=src,
            dst_ref=dst,
            send_sem=sems.at[base],
            recv_sem=sems.at[base + 1],
            device_id={"gx": gx, "gy": gy},
            device_id_type=MESH,
        )

    def over(n, me, action):
        def one(d, carry):
            action(wrap(me + d, n))
            return carry

        lax.fori_loop(1, n, one, 0)

    def to_gx(src, dst, base):
        over(GX, me_x, lambda peer: along(src.at[peer], dst.at[me_x], xa, base, peer, me_y).start())
        dst[me_x] = src[me_x]

    def to_gy(src, dst, base):
        over(GY, me_y, lambda peer: along(src.at[peer], dst.at[me_y], xa, base, me_x, peer).start())
        dst[me_y] = src[me_y]

    def all_of(ref, sems, base):
        n = ref.shape[0] - 1
        return along(ref.at[pl.ds(0, n)], ref.at[pl.ds(0, n)], sems, base, east, me_y)

    to_gx(send_w, recv_w, 0)
    to_gx(send_p, recv_p, 2)

    def restore(value, loading=False):
        bds[...] = value.astype(BF16)

        def block(i, carry):
            if loading:
                kload(i).wait()
            mine = bds[pl.ds(pl.multiple_of(16 * i, 16), 16), :]
            row = iota((16, DOF), 0)
            total = jnp.zeros((16, DOF), F32)
            for b in range(16):
                part = mm(mine, kk[16 * i + b], NT)
                total = jnp.where(row == b, part, total)
            rest[pl.ds(pl.multiple_of(16 * i, 16), 16), :] = total
            return carry

        lax.fori_loop(0, 4, block, 0)

    restore(drift0, True)
    rest0 = rest[...]
    start(late0[:2])
    b0[pl.ds(320, 32), :] = layer_rows(rows_m, 0, 34, 0, 8)
    pack_columns(lambda k: mp[0, k, 8:24, :], 416)
    start(late0[2:])

    moved = rate0 - DT * rest0 - DT * cpl * rate0
    send_q[...] = by_column(gather_dofs(DT * cpl * cpl, 0) + gather_dofs(cpl * moved, 3))
    to_gx(send_q, recv_q, 6)

    def stencil(points):
        row, col = iota((256, CY), 0) % CY, iota((256, CY), 1)
        total = jnp.zeros((256, CY), F32)
        for offset, weight in points.items():
            total = jnp.where(row == col + offset, weight, total)
        return total.astype(BF16)

    sten[0] = stencil({1: 27.0, 0: -27.0, 2: -1.0, -1: 1.0})
    sten[1] = stencil({0: 27.0, -1: -27.0, 1: -1.0, -2: 1.0})
    sten[2] = stencil({1: 1.0})

    def along_y(value, kind):
        hi, lo = split(value.reshape(ROWS, CY))
        return mm(jnp.concatenate([hi, lo], axis=1), sten[kind], NN).reshape(NZ, CX, CY)

    def y_parts(ref, fields, kinds):
        for i in range(3):
            dyb[i] = along_y(ref[fields[i], pl.ds(2, NZ), pl.ds(8, CX), :], kinds[i])

    y_parts(vp, (0, 1, 2), (0, 1, 0))
    shb[...] = along_y(mp[0, pl.ds(0, NZ), pl.ds(8, CX), :], 2)
    shm[pl.ds(0, NZ), pl.ds(8, CX), :] = along_y(mp[1, pl.ds(0, NZ), pl.ds(8, CX), :], 2)

    whole(0, r0b.at[pl.ds(0, 304)]).wait_recv()
    all_of(recv_w, xa, 0).wait_recv()
    all_of(recv_p, xa, 2).wait_recv()
    info = recv_p[...].reshape(GX, CY)
    for j in range(GY):
        send_b[j, 0:16, :] = recv_w.reshape(GX * GY, CY)[pl.ds(j, GX, stride=8), :]
        send_b[j, 16:32, :] = info
    to_gy(send_b, tab, 4)
    unpack_x(rows_v, pairs_v, r0b, (0, 1))
    put_rows(rows_m, 1, 34, 0, 24, r0b[pl.ds(288, 32), :])
    def reach(packed, forward):
        at = lane16 % 4
        up1, dn1 = pltpu.roll(packed, CY - 1, 1), pltpu.roll(packed, 1, 1)
        if forward:
            up2 = pltpu.roll(packed, CY - 2, 1)
            return jnp.where(
                at == 0, -up2, jnp.where(at == 1, 27.0 * up1 - up2, jnp.where(at == 2, dn1, 0.0))
            )
        dn2 = pltpu.roll(packed, 2, 1)
        return jnp.where(
            at == 0, 0.0, jnp.where(at == 1, -up1, jnp.where(at == 2, dn2 - 27.0 * dn1, dn2))
        )

    reach_v = [
        reach(merge_y(r0b, (352 + 16 * f, 416 + 16 * f)), forward)
        for f, forward in enumerate((True, False, True))
    ]
    packed_m = r0b[pl.ds(464, CX), :]

    out_x = (row16 == CX - 1) & (me_x == GX - 1)
    out_y = (lane16 == CY - 1) & (me_y == GY - 1)
    out_xy = out_x | out_y
    last_lane = lane16 == CY - 1
    edge = (lane16 < 2) | (lane16 >= CY - 2)

    def to_last(packed, k):
        return pltpu.roll(packed, lax.rem(2 * CY - 3 - 4 * k, CY), 1)

    def average_b(k, carry):
        b = mp[0, k, 8:24, :]
        bx = jnp.where(out_x, b, mp[0, k, 9:25, :])
        by = jnp.where(out_y, b, jnp.where(last_lane, to_last(packed_b, k), shb[k]))
        bz = jnp.where(k == NZ - 1, b, mp[0, k + 1, 8:24, :])
        av[0, k] = (b + bx) * (0.5 * UNIT)
        av[1, k] = (b + by) * (0.5 * UNIT)
        av[2, k] = (b + bz) * (0.5 * UNIT)
        return carry

    def average_m(k, carry):
        last = k == NZ - 1
        m = mp[1, k, 8:24, :]
        mx = jnp.where(out_x, m, mp[1, k, 9:25, :])
        my = jnp.where(out_y, m, shm[k, 8:24, :])
        mxy = jnp.where(out_xy, m, shm[k, 9:25, :])
        mz = jnp.where(last, m, mp[1, k + 1, 8:24, :])
        mxz = jnp.where(out_x | last, m, mp[1, k + 1, 9:25, :])
        myz = jnp.where(out_y | last, m, shm[k + 1, 8:24, :])
        av[3, k] = (m + mx + my + mxy) * (0.25 * UNIT)
        av[4, k] = (m + mx + mz + mxz) * (0.25 * UNIT)
        av[5, k] = (m + my + mz + myz) * (0.25 * UNIT)
        return carry

    def join(k, carry):
        shm[k, 8:24, :] = jnp.where(last_lane, to_last(packed_m, k), shm[k, 8:24, :])
        return carry

    def layers(action, init, first=0, last=NZ // GROUP):
        def group(i, carry):
            for j in range(GROUP):
                carry = action(GROUP * i + j, carry)
            return carry

        return lax.fori_loop(first, last, group, init)

    layers(join, 0)
    lane32, row32 = iota((NZ, CY), 1), iota((NZ, CY), 0)
    corners = jnp.broadcast_to(r0b[pl.ds(496, 8), :][0:1, :], (NZ, CY))
    corners = jnp.sum(jnp.where(lane32 == 4 * row32 + 2, corners, 0.0), axis=1, keepdims=True)
    eastern = pltpu.roll(r0b[pl.ds(288, NZ), :], CY - 1, 1)
    eastern = jnp.where(lane32 == CY - 1, corners, eastern)
    put_rows(shm.reshape(33 * 32, CY), 0, 33, 0, 24, eastern)
    layers(average_m, 0)

    def fwd(minus, zero_, plus, plus2):
        return 27.0 * (plus - zero_) - (plus2 - minus)

    def bwd(minus2, minus, zero_, plus):
        return 27.0 * (zero_ - minus) - (plus - minus2)

    def dx(ref, f, k, forward):
        first = 7 if forward else 6
        parts = [ref[f, k + 2, first + i : first + i + CX, :] for i in range(4)]
        return (fwd if forward else bwd)(*parts)

    def dz(ref, f, k, forward):
        first = 1 if forward else 0
        parts = [ref[f, k + first + i, 8:24, :] for i in range(4)]
        return (fwd if forward else bwd)(*parts)

    def dy(reaches, i, k):
        return dyb[i, k] + jnp.where(edge, reaches(i, k), 0.0)

    def pack_half(carry, values, k):
        first = pack_layer(pack_layer(carry[0], values[0], k), values[1], k + HALF)
        return first, pack_layer(carry[1], values[2], k)

    def stress_layer(reaches, h, k, carry):
        sx, sy, sz = dx(vp, 0, k, False), dy(reaches, 1, k), dz(vp, 2, k, False)
        m2 = (2.0 * UNIT) * mp[1, k, 8:24, :]
        volume = (UNIT * lam[k]) * (sx + sy + sz)
        new = {}
        for f, s in ((0, sx), (1, sy), (2, sz)):
            new[f] = sp[f, k + 2, 8:24, :] + (volume + m2 * s)
        shear_xy = dy(reaches, 0, k) + dx(vp, 1, k, True)
        shear_xz = dz(vp, 0, k, True) + dx(vp, 2, k, True)
        shear_yz = dz(vp, 1, k, True) + dy(reaches, 2, k)
        for f, s in ((3, shear_xy), (4, shear_xz), (5, shear_yz)):
            new[f] = sp[f, k + 2, 8:24, :] + av[f, k] * s
        for f in range(6):
            sp[f, k + 2, 8:24, :] = new[f]
        return pack_half(carry, (new[3], new[1], new[5]), k - HALF * h)

    def velocity_layer(reaches, out, surface, h, k, carry):
        ax = dx(sp, 0, k, True) + dy(reaches, 0, k) + dz(sp, 4, k, False)
        ay = dx(sp, 3, k, False) + dy(reaches, 1, k) + dz(sp, 5, k, False)
        az = dx(sp, 4, k, False) + dy(reaches, 2, k) + dz(sp, 2, k, True)
        new = []
        for f, a in ((0, ax), (1, ay), (2, az)):
            value = vp[f, k + 2, 8:24, :] + av[f, k] * a
            if surface:
                value = value + forc[f]
            new.append(value)
            if out is None:
                vp[f, k + 2, 8:24, :] = value
            else:
                out[f, k] = value
        return pack_half(carry, new, k - HALF * h) if carry else carry

    def received(slot, ref, pairs, rbuf, kinds):
        def begin(h):
            whole(slot + h, rbuf.at[pl.ds(0, 208)]).wait_recv()
            unpack_x(ref, pairs, rbuf, (2 * h, 2 * h + 1))
            south_at, north_at = 288 + 32 * h, 352 + 32 * h
            merged = [merge_y(rbuf, (south_at + 16 * i, north_at + 16 * i)) for i in range(2)]
            fields = [reach(merged[i // 2], kinds[i]) for i in range(3)]
            return lambda i, k: halo_of(fields[i], k - HALF * h + (HALF if i == 1 else 0))

        return begin

    count = PART // GROUP
    blank = (jnp.zeros((CX, CY), F32),) * 2

    def send_half(buf, halos, carry, h):
        for i in range(2):
            buf[pl.ds(288 + 32 * h + 16 * i, 16), :] = carry[i]
        start(halos[1](h))

    def stress_step(begin, buf, halos):
        for h in range(2):
            reaches, carry = begin(h), blank
            for part in (2 * h, 2 * h + 1):
                carry = layers(
                    lambda k, c: stress_layer(reaches, h, k, c), carry, count * part, count * part + count
                )
                pack_x(rows_s, pairs_s, buf, part)
                start(halos[0](part))
            send_half(buf, halos, carry, h)

    def velocity_step(begin, out, buf, halos):
        for h in range(2):
            reaches, carry = begin(h), () if buf is None else blank
            for part in (2 * h, 2 * h + 1):
                first = count * part
                if part == 0:
                    for k in range(GROUP):
                        carry = velocity_layer(reaches, out, k == 0, h, k, carry)
                    first = 1
                carry = layers(
                    lambda k, c: velocity_layer(reaches, out, False, h, k, c),
                    carry,
                    first,
                    count * part + count,
                )
                if buf is not None:
                    pack_x(rows_v, pairs_v, buf, part)
                    start(halos[0](part))
            if buf is not None:
                send_half(buf, halos, carry, h)

    loads[10].wait()
    loads[11].wait()
    halos1 = halo_set(3, b1, r1b, 160, 128)

    def begin_first(h):
        if h == 1:
            whole(1, r0b.at[pl.ds(0, 144)]).wait_recv()
            unpack_x(rows_v, pairs_v, r0b, (2, 3))
        return lambda i, k: halo_of(reach_v[i], k)

    stress_step(begin_first, b1, halos1)
    y_parts(sp, (3, 1, 5), (1, 0, 1))
    whole(2, r0b.at[pl.ds(0, 48)]).wait_recv()
    put_rows(rows_m, 0, 34, 0, 24, r0b[pl.ds(320, 32), :])
    packed_b = r0b[pl.ds(480, CX), :]
    layers(average_b, 0)

    all_of(tab, xa, 4).wait_recv()
    row128, lane128 = iota((128, CY), 0), iota((128, CY), 1)
    sel = iota((16, CY), 1) == (iota((16, CY), 0) % 8) * 16 + (iota((16, CY), 0) // 8) * 8 + me_y

    def by_slot(value):
        both = pick_lhs(sel.astype(F32), value, NT)
        return jnp.concatenate([both[0:8], both[8:16]], axis=1)

    params = by_slot(tab[:, 16:32, :].reshape(128, CY))
    r0, c0 = params, pltpu.roll(params, 5, 0)
    sent = tab[:, 0:16, :].reshape(128, CY)
    for p in range(2):
        want = (row128 % CX < FOOT) & (lane128 == 64 * p + (row128 % CX) * FOOT + row128 // CX)
        placed = pick_lhs(want.astype(F32), sent, NT)
        shift = jnp.broadcast_to(params[7:8, 128 * p : 128 * p + 128], (128, CY)).astype(jnp.int32)
        for bit in (1, 2, 4, 8):
            placed = jnp.where((shift & bit) != 0, pltpu.roll(placed, bit, 0), placed)
        wxt[:, 128 * p : 128 * p + 128] = placed
    oyt = (iota((CY, 256), 0).astype(F32) == params[6:7]).astype(F32).astype(BF16)

    def motion():
        total = jnp.zeros((8, 256), F32)
        row = iota((8, 256), 0)
        for f in range(3):
            value = vp[f, 2, 8:24, :]
            turns = [value] + [pltpu.roll(value, CY - c, 1) for c in range(1, FOOT)]
            hi, lo = split(jnp.concatenate(turns, axis=0))
            found = mm(hi, oyt, NN) + mm(lo, oyt, NN)
            one = jnp.sum(found * wxt[...], axis=0, keepdims=True)
            total = jnp.where(row == f, jnp.broadcast_to(one, (8, 256)), total)
        return total

    def push(reaction):
        reaction = reaction * (DT * FOOT)
        for f in range(3):
            hi, lo = split(wxt[...] * reaction[f : f + 1])
            spread = mm(hi, oyt, NT) + mm(lo, oyt, NT)
            total = spread[0:CX]
            for c in range(1, FOOT):
                total = total + pltpu.roll(spread[CX * c : CX * c + CX], c, 1)
            forc[f] = total

    def send_motion(step, value):
        bm_s[step] = jnp.where(row8 < 4, value[:, 0:128], pltpu.roll(value[:, 128:256], 4, 0))
        over(
            GY,
            me_y,
            lambda peer: along(
                bm_s.at[step], m_r.at[step, me_y], xm, 4 * step, me_x, peer
            ).start(),
        )
        m_r[step, me_y] = bm_s[step]

    def pass_motion(step):
        all_of(m_r.at[step], xm, 4 * step).wait_recv()
        want = (iota((GX, CY), 1) == iota((GX, CY), 0) + GX * me_y).astype(F32)
        rows = pick_lhs(want, m_r[step].reshape(GY * 8, CY), NT)
        rows = jnp.concatenate([rows, jnp.zeros((GX, CY - GY * 8), F32)], axis=1)
        m_p[step] = rows.reshape(GX, 1, CY)
        over(
            GX,
            me_x,
            lambda peer: along(
                m_p.at[step, peer], m_q.at[step, me_x], xm, 4 * step + 2, peer, me_y
            ).start(),
        )
        m_q[step, me_x] = m_p[step, me_x]

    want_lane = own_yc * 2.0 + pos_col
    own_gx = (iota((NB, GX), 1).astype(F32) == own_xc).astype(F32)

    def take_motion(step):
        all_of(m_q.at[step], xm, 4 * step + 2).wait_recv()
        found = pick_lhs(own_gx, m_q[step].reshape(GX, CY), NN)
        found = jnp.where((lane // 4).astype(F32) == want_lane, found, 0.0)
        onto = (iota((CY, DOF), 0) % 4 == iota((CY, DOF), 1) % 3).astype(F32)
        return pick_rhs(found, onto, NN)

    bm1 = motion()
    send_motion(0, bm1)
    push(r0 - c0 * bm1)

    all_of(recv_q, xa, 6).wait_recv()
    send_d[...] = recv_q[...].reshape(GX, CY)
    over(GY, me_y, lambda peer: along(send_d, tab_q.at[me_y], xa, 8, me_x, peer).start())
    tab_q[me_y] = send_d[...]

    kinds_s, kinds_v = (False, True, False), (True, False, True)
    halos2 = halo_set(5, b2, r2b, 128, 160)
    velocity_step(received(3, rows_s, pairs_s, r1b, kinds_s), None, b2, halos2)

    bm2 = motion()
    send_motion(1, bm2)
    y_parts(vp, (0, 1, 2), (0, 1, 0))
    pass_motion(0)
    all_of(tab_q, xa, 8).wait_recv()
    params = by_slot(tab_q[...].reshape(128, CY))
    push(pltpu.roll(params, 5, 0) + params * bm1 - c0 * bm2)

    halos3 = halo_set(7, b3, r3b, 160, 128)
    stress_step(received(5, rows_v, pairs_v, r2b, kinds_v), b3, halos3)
    y_parts(sp, (3, 1, 5), (1, 0, 1))

    pass_motion(1)

    def advance(rates, drifts, restoring, base):
        relative = jnp.where(mask, rates - base, 0.0)
        rates = jnp.where(mask, rates - DT * restoring - DT * cpl * relative, 0.0)
        return rates, jnp.where(mask, drifts + DT * rates, 0.0)

    rate1, drift1 = advance(rate0, drift0, rest0, take_motion(0))
    restore(drift1)

    velocity_step(received(7, rows_s, pairs_s, r3b, kinds_s), ovel, None, None)
    rate2, drift2 = advance(rate1, drift1, rest[...], take_motion(1))
    odrift[...] = drift2
    orate[...] = rate2

    for slot, n in enumerate((304, 144, 48)):
        whole(slot, r0b.at[pl.ds(0, n)]).wait_send()
    for slot in range(3, 9):
        whole(slot, r1b.at[pl.ds(0, 208)]).wait_send()
    for ref, base in ((recv_w, 0), (recv_p, 2), (tab, 4), (recv_q, 6), (tab_q, 8)):
        all_of(ref, xa, base).wait_send()
    for step in range(2):
        all_of(m_r.at[step], xm, 4 * step).wait_send()
        all_of(m_q.at[step], xm, 4 * step + 2).wait_send()


def finish(vel, drift, rate, ovel, odrift, orate, sem):
    copies = [
        pltpu.make_async_copy(vel, ovel, sem.at[0]),
        pltpu.make_async_copy(drift, odrift, sem.at[1]),
        pltpu.make_async_copy(rate, orate, sem.at[2]),
    ]
    for c in copies:
        c.start()
    for c in copies:
        c.wait()


def body(vel, stress, buoy, lame, shear, stiff, drift, rate, coup, contact, dof, owner, corner):
    anywhere = pl.BlockSpec(memory_space=pltpu.HBM)
    vmem = pltpu.VMEM
    near = pl.BlockSpec(memory_space=vmem)
    dma = pltpu.SemaphoreType.DMA
    halo = [vmem((512, CY), F32), vmem((528, CY), F32)] + [vmem((352, CY), F32), vmem((416, CY), F32)] * 3
    shapes = ((3, NZ, CX, CY), (NB, DOF), (NB, DOF))
    outs = pl.pallas_call(
        kernel,
        out_shape=tuple(vmem(s, F32) for s in shapes),
        in_specs=[anywhere] * 13,
        out_specs=(near,) * 3,
        scratch_shapes=[
            vmem((3, 36, 32, CY), F32),
            vmem((6, 36, 32, CY), F32),
            vmem((2, 34, 32, CY), F32),
            vmem((NZ, CX, CY), F32),
            vmem((6, NZ, CX, CY), F32),
            vmem((NB, DOF, DOF), BF16),
            vmem((3, NB, DOF), F32),
            vmem((NB, 64), F32),
            vmem((1, NB), jnp.int32),
            vmem((1, NB), jnp.int32),
            vmem((1, NB), jnp.int32),
            vmem((3, NZ, CX, CY), F32),
            vmem((3, 256, CY), BF16),
            vmem((NZ, CX, CY), F32),
            vmem((33, 32, CY), F32),
            vmem((GX, GY, CY), F32),
            vmem((GX, GY, CY), F32),
            vmem((GX, 1, CY), F32),
            vmem((GX, 1, CY), F32),
            vmem((GY, 32, CY), F32),
            vmem((GY, 32, CY), F32),
            vmem((GX, 1, CY), F32),
            vmem((GX, 1, CY), F32),
            vmem((GX, CY), F32),
            vmem((GY, GX, CY), F32),
            vmem((128, 256), F32),
            vmem((3, CX, CY), F32),
            vmem((2, 8, CY), F32),
            vmem((2, GY, 8, CY), F32),
            vmem((2, GX, 1, CY), F32),
            vmem((2, GX, 1, CY), F32),
            vmem((NB, DOF), F32),
            vmem((NB, DOF), BF16),
            *halo,
            dma((12,)),
            dma((4,)),
            dma((10,)),
            dma((8,)),
            dma((9,)),
            dma((9,)),
        ],
        compiler_params=pltpu.CompilerParams(
            collective_id=0, has_side_effects=True, vmem_limit_bytes=66_100_000
        ),
    )(
        vel, stress, buoy, lame, shear, stiff, drift, rate, coup, contact,
        dof.reshape(1, NB), owner.reshape(1, NB), corner.reshape(1, NB),
    )
    return pl.pallas_call(
        finish,
        out_shape=tuple(jax.ShapeDtypeStruct(s, F32) for s in shapes),
        in_specs=[near] * 3,
        out_specs=(anywhere,) * 3,
        scratch_shapes=[dma((3,))],
        compiler_params=pltpu.CompilerParams(vmem_limit_bytes=1024 * 1024),
    )(*outs)


def solution(mesh):
    placed = (
        P(None, None, "gx", "gy"),
        P(None, None, "gx", "gy"),
        P(None, "gx", "gy"),
        P(None, "gx", "gy"),
        P(None, "gx", "gy"),
        P(("gx", "gy"), None, None),
        P(("gx", "gy"), None),
        P(("gx", "gy"), None),
        P(("gx", "gy"), None),
        P(("gx", "gy"), None),
        P(("gx", "gy")),
        P(("gx", "gy"), None),
        P(("gx", "gy")),
    )
    return jax.shard_map(
        body,
        mesh=mesh,
        in_specs=placed,
        out_specs=(P(None, None, "gx", "gy"), P(("gx", "gy"), None), P(("gx", "gy"), None)),
        check_vma=False,
    )
```

```python
import jax
import jax.numpy as jnp
from jax import lax
from jax.experimental import pallas as pl
from jax.experimental.pallas import tpu as pltpu
from jax.sharding import PartitionSpec as P

MESH = pl.DeviceIdType.MESH
F32 = jnp.float32
BF16 = jnp.bfloat16
DT = 0.3
INNER = 9.0 / 8.0
OUTER = 1.0 / 24.0
FOOT = 8
GX, GY = 16, 8
NZ, CX, CY = 32, 16, 128
NB, DOF = 64, 256
SPAN = CY - FOOT + 1
ROWS = NZ * CX
GROUP, PARTS = 8, 4
PART = NZ // PARTS
HALF = NZ // 2
UNIT = DT / 24.0


def iota(shape, dim):
    return lax.broadcasted_iota(jnp.int32, shape, dim)


def mm(a, b, dims):
    return lax.dot_general(a, b, (dims, ((), ())), preferred_element_type=F32)


def split(x):
    hi = x.astype(BF16)
    return hi, (x - hi.astype(F32)).astype(BF16)


NN, NT = ((1,), (0,)), ((1,), (1,))


def pick_lhs(exact, value, dims):
    hi, lo = split(value)
    exact = exact.astype(BF16)
    return mm(exact, hi, dims) + mm(exact, lo, dims)


def pick_rhs(value, exact, dims):
    hi, lo = split(value)
    exact = exact.astype(BF16)
    return mm(hi, exact, dims) + mm(lo, exact, dims)


def kernel(
    vel, stress, buoy, lame, shear, stiff, drift, rate, coup, contact, dof, owner, corner,
    ovel, odrift, orate,
    vp, sp, mp, lam, av, kk, bd, ct, dofv, ownv, corv,
    dyb, sten, shb, shm,
    send_w, recv_w, send_p, recv_p, send_b, tab, send_q, recv_q, send_d, tab_q, wxt, forc,
    bm_s, m_r, m_p, m_q, rest, bds,
    b0, r0b, b1, r1b, b2, r2b, b3, r3b,
    ld, ldk, xa, xm, hs, hr,
):
    me_x = lax.axis_index("gx")
    me_y = lax.axis_index("gy")

    def wrap(value, n):
        return lax.rem(value + n, n)

    east, west = wrap(me_x + 1, GX), wrap(me_x - 1, GX)
    north, south = wrap(me_y + 1, GY), wrap(me_y - 1, GY)

    inner = (pl.ds(2, NZ), pl.ds(8, CX), slice(None))
    loads = [
        pltpu.make_async_copy(contact, ct, ld.at[0]),
        pltpu.make_async_copy(dof, dofv, ld.at[1]),
        pltpu.make_async_copy(owner, ownv, ld.at[2]),
        pltpu.make_async_copy(corner, corv, ld.at[3]),
        pltpu.make_async_copy(drift, bd.at[0], ld.at[4]),
        pltpu.make_async_copy(rate, bd.at[1], ld.at[5]),
        pltpu.make_async_copy(coup, bd.at[2], ld.at[6]),
        pltpu.make_async_copy(vel, vp.at[(slice(None),) + inner], ld.at[7]),
        pltpu.make_async_copy(buoy, mp.at[0, pl.ds(0, NZ), pl.ds(8, CX), :], ld.at[8]),
        pltpu.make_async_copy(shear, mp.at[1, pl.ds(0, NZ), pl.ds(8, CX), :], ld.at[9]),
        pltpu.make_async_copy(lame, lam, ld.at[10]),
        pltpu.make_async_copy(stress, sp.at[(slice(None),) + inner], ld.at[11]),
    ]

    def kload(i):
        at = pl.ds(16 * i, 16)
        return pltpu.make_async_copy(stiff.at[at], kk.at[at], ldk.at[i])

    kloads = [kload(i) for i in range(4)]
    for c in loads[7:10] + loads[:7]:
        c.start()

    barrier = pltpu.get_barrier_semaphore()

    def greet(gx, gy):
        pl.semaphore_signal(barrier, inc=1, device_id={"gx": gx, "gy": gy}, device_id_type=MESH)

    for d in range(1, GX):
        greet(wrap(me_x + d, GX), me_y)
    for d in range(1, GY):
        greet(me_x, wrap(me_y + d, GY))
    greet(west, south)
    greet(east, north)

    zero = jnp.zeros((2, 32, CY), F32)
    for f in range(3):
        vp[f, 0:2] = zero
        vp[f, 34:36] = zero
    for f in (2, 4, 5):
        sp[f, 0:2] = zero
        sp[f, 34:36] = zero
    mp[0, NZ] = zero[0]
    mp[1, NZ] = zero[0]
    shm[NZ] = zero[0]

    rows_v = vp.reshape(3 * 36 * 32, CY)
    rows_s = sp.reshape(6 * 36 * 32, CY)
    rows_m = mp.reshape(2 * 34 * 32, CY)
    lane16, row16 = iota((CX, CY), 1), iota((CX, CY), 0)
    row8, lane8 = iota((8, CY), 0), iota((8, CY), 1)

    def layer_rows(ref, field, depth, first, row):
        return ref[pl.ds((field * depth + first) * 32 + row, NZ, stride=32), :]

    def put_rows(ref, field, depth, first, row, value):
        ref[pl.ds((field * depth + first) * 32 + row, NZ, stride=32), :] = value

    keep_w = (me_x > 0).astype(F32)
    keep_e = (me_x < GX - 1).astype(F32)
    keep_s = (me_y > 0).astype(F32)
    keep_n = (me_y < GY - 1).astype(F32)

    pairs_v = [(0, 2, 1), (1, 1, 2), (2, 1, 2)]
    pairs_s = [(0, 1, 2), (3, 2, 1), (4, 2, 1)]

    def x_rows(pairs, part, inside):
        ups, downs = sum(p[1] for p in pairs), sum(p[2] for p in pairs)
        at = PART * ups * part
        for field, before, _ in pairs:
            for i in range(before):
                yield field, 8 - before + i + (CX if inside else 0), at, keep_w
                at += PART
        at = PART * (ups * PARTS + downs * part)
        for field, _, after in pairs:
            for i in range(after):
                yield field, 8 + i + (0 if inside else CX), at, keep_e
                at += PART

    def pack_x(ref, pairs, buf, part):
        for field, row, at, _ in x_rows(pairs, part, True):
            first = (field * 36 + 2 + PART * part) * 32 + row
            buf[pl.ds(at, PART), :] = ref[pl.ds(first, PART, stride=32), :]

    def unpack_x(ref, pairs, buf, parts=range(PARTS)):
        for part in parts:
            for field, row, at, keep in x_rows(pairs, part, False):
                first = (field * 36 + 2 + PART * part) * 32 + row
                ref[pl.ds(first, PART, stride=32), :] = buf[pl.ds(at, PART), :] * keep

    def pack_layer(total, value, k):
        return jnp.where(lane16 // 4 == k, pltpu.roll(value, 4 * k + 2, 1), total)

    def halo_of(packed, k):
        return pltpu.roll(packed, CY - 2 - 4 * k, 1)

    def merge_y(buf, at):
        from_south = buf[pl.ds(at[0], CX), :] * keep_s
        return jnp.where(lane16 % 4 >= 2, buf[pl.ds(at[1], CX), :] * keep_n, from_south)

    def halo_copies(buf, rbuf):
        def copy(slot, at, to, n, gx, gy):
            return pltpu.make_async_remote_copy(
                src_ref=buf.at[pl.ds(at, n)],
                dst_ref=rbuf.at[pl.ds(to, n)],
                send_sem=hs.at[slot],
                recv_sem=hr.at[slot],
                device_id={"gx": gx, "gy": gy},
                device_id_type=MESH,
            )

        return copy

    def halo_set(slot, buf, rbuf, up, down):
        copy = halo_copies(buf, rbuf)

        def x_part(part):
            a, b = up // PARTS, down // PARTS
            return [
                copy(slot + part // 2, a * part, a * part, a, east, me_y),
                copy(slot + part // 2, up + b * part, up + b * part, b, west, me_y),
            ]

        def y_half(h):
            y = up + down + 32 * h
            return [
                copy(slot + h, y, y, 32, me_x, north),
                copy(slot + h, y, y + 64, 32, me_x, south),
            ]

        return x_part, y_half

    def start(copies):
        for c in copies:
            c.start()

    def whole(slot, rbuf):
        return pltpu.make_async_remote_copy(
            src_ref=rbuf,
            dst_ref=rbuf,
            send_sem=hs.at[slot],
            recv_sem=hr.at[slot],
            device_id={"gx": east, "gy": me_y},
            device_id_type=MESH,
        )

    for i in range(7, 10):
        loads[i].wait()
    for c in kloads:
        c.start()
    for part in range(PARTS):
        pack_x(rows_v, pairs_v, b0, part)
    b0[pl.ds(288, 32), :] = layer_rows(rows_m, 1, 34, 0, 8)

    def pack_columns(source, at):
        total = jnp.zeros((CX, CY), F32)
        for k in range(NZ):
            total = pack_layer(total, source(k), k)
        b0[pl.ds(at, 16), :] = total

    for f in range(3):
        pack_columns(lambda k, f=f: vp[f, k + 2, 8:24, :], 352 + 16 * f)
    pack_columns(lambda k: mp[1, k, 8:24, :], 400)
    copy0 = halo_copies(b0, r0b)
    halos0 = [
        copy0(0, 0, 0, 64, east, me_y),
        copy0(0, 128, 128, 80, west, me_y),
        copy0(0, 288, 288, 32, west, me_y),
        copy0(0, 352, 352, 48, me_x, north),
        copy0(0, 352, 416, 64, me_x, south),
        copy0(0, 400, 496, CX, west, south),
    ]
    late0 = [
        copy0(1, 64, 64, 64, east, me_y),
        copy0(1, 208, 208, 80, west, me_y),
        copy0(2, 320, 320, 32, west, me_y),
        copy0(2, 416, 480, CX, me_x, south),
    ]

    for i in range(7):
        loads[i].wait()
    for c in loads[10:]:
        c.start()
    eye = iota((NB, NB), 0) == iota((NB, NB), 1)

    def to_col(row):
        return jnp.sum(jnp.where(eye, jnp.broadcast_to(row, (NB, NB)), 0.0), axis=1, keepdims=True)

    dof_col = to_col(dofv[...].astype(F32))
    cor_col = to_col(corv[...].astype(F32))
    own_row = ownv[...].astype(F32)
    own_col = to_col(own_row)
    same = jnp.broadcast_to(own_col, (NB, NB)) == jnp.broadcast_to(own_row, (NB, NB))
    upper = iota((NB, NB), 0) < iota((NB, NB), 1)
    lower = iota((NB, NB), 0) > iota((NB, NB), 1)
    pos_row = jnp.sum(jnp.where(same & upper, 1.0, 0.0), axis=0, keepdims=True)
    pos_col = jnp.sum(jnp.where(same & lower, 1.0, 0.0), axis=1, keepdims=True)
    mask = iota((NB, DOF), 1).astype(F32) < dof_col
    cpl = jnp.where(mask, bd[2], 0.0)
    rate0 = jnp.where(mask, bd[1], 0.0)
    drift0 = jnp.where(mask, bd[0], 0.0)

    def gather_dofs(value, first):
        want = (iota((DOF, CY), 0) % 3 + first) == iota((DOF, CY), 1) // 16
        return pick_rhs(value, want.astype(F32), NN)

    lane = iota((NB, CY), 1)
    start_x = jnp.floor((cor_col + 0.5) * (1.0 / SPAN))
    start_y = cor_col - SPAN * start_x
    own_xc = jnp.floor((own_col + 0.5) * (1.0 / GY))
    own_yc = own_col - GY * own_xc
    own_xr = jnp.floor((own_row + 0.5) * (1.0 / GY))
    weights = ct[...] / jnp.sum(ct[...], axis=1, keepdims=True)
    twice = jnp.concatenate([weights, weights], axis=1)
    twice = jnp.where((lane // 64).astype(F32) == pos_col, twice, 0.0)
    to_tile = (iota((128, NB), 0).astype(F32) == own_row).astype(F32)
    send_w[...] = pick_lhs(to_tile, twice, NN).reshape(GX, GY, CY)
    to_column = (iota((GX, NB), 0).astype(F32) == own_xr).astype(F32)
    slot = (lane % 16).astype(F32) == pos_col * 8.0 + own_yc

    def by_column(value):
        return pick_lhs(to_column, jnp.where(slot, value, 0.0), NN).reshape(GX, 1, CY)

    info = gather_dofs(cpl * rate0, 0) + gather_dofs(cpl, 3)
    info = jnp.where(lane // 16 == 6, start_y, jnp.where(lane // 16 == 7, start_x, info))
    send_p[...] = by_column(info)

    pl.semaphore_wait(barrier, GX + GY)
    start(halos0)

    def along(src, dst, sems, base, gx, gy):
        return pltpu.make_async_remote_copy(
            src_ref=src,
            dst_ref=dst,
            send_sem=sems.at[base],
            recv_sem=sems.at[base + 1],
            device_id={"gx": gx, "gy": gy},
            device_id_type=MESH,
        )

    def over(n, me, action):
        def one(d, carry):
            action(wrap(me + d, n))
            return carry

        lax.fori_loop(1, n, one, 0)

    def to_gx(src, dst, base):
        over(GX, me_x, lambda peer: along(src.at[peer], dst.at[me_x], xa, base, peer, me_y).start())
        dst[me_x] = src[me_x]

    def to_gy(src, dst, base):
        over(GY, me_y, lambda peer: along(src.at[peer], dst.at[me_y], xa, base, me_x, peer).start())
        dst[me_y] = src[me_y]

    def all_of(ref, sems, base):
        n = ref.shape[0] - 1
        return along(ref.at[pl.ds(0, n)], ref.at[pl.ds(0, n)], sems, base, east, me_y)

    to_gx(send_w, recv_w, 0)
    to_gx(send_p, recv_p, 2)

    def restore(value, loading=False):
        bds[...] = value.astype(BF16)

        def block(i, carry):
            row = iota((16, DOF), 0)
            for n in (2 * i, 2 * i + 1):
                if loading:
                    kload(n).wait()
                at = pl.ds(pl.multiple_of(16 * n, 16), 16)
                mine = bds[at, :]
                total = jnp.zeros((16, DOF), F32)
                for b in range(16):
                    part = mm(mine, kk[16 * n + b], NT)
                    total = jnp.where(row == b, part, total)
                rest[at, :] = total
            return carry

        lax.fori_loop(0, 2, block, 0)

    restore(drift0, True)
    rest0 = rest[...]
    start(late0[:2])
    b0[pl.ds(320, 32), :] = layer_rows(rows_m, 0, 34, 0, 8)
    pack_columns(lambda k: mp[0, k, 8:24, :], 416)
    start(late0[2:])

    moved = rate0 - DT * rest0 - DT * cpl * rate0
    send_q[...] = by_column(gather_dofs(DT * cpl * cpl, 0) + gather_dofs(cpl * moved, 3))
    to_gx(send_q, recv_q, 6)

    def stencil(points):
        row, col = iota((256, CY), 0) % CY, iota((256, CY), 1)
        total = jnp.zeros((256, CY), F32)
        for offset, weight in points.items():
            total = jnp.where(row == col + offset, weight, total)
        return total.astype(BF16)

    sten[0] = stencil({1: 27.0, 0: -27.0, 2: -1.0, -1: 1.0})
    sten[1] = stencil({0: 27.0, -1: -27.0, 1: -1.0, -2: 1.0})
    sten[2] = stencil({1: 1.0})

    def along_y(value, kind):
        hi, lo = split(value.reshape(ROWS, CY))
        return mm(jnp.concatenate([hi, lo], axis=1), sten[kind], NN).reshape(NZ, CX, CY)

    def y_parts(ref, fields, kinds):
        for i in range(3):
            dyb[i] = along_y(ref[fields[i], pl.ds(2, NZ), pl.ds(8, CX), :], kinds[i])

    y_parts(vp, (0, 1, 2), (0, 1, 0))
    shb[...] = along_y(mp[0, pl.ds(0, NZ), pl.ds(8, CX), :], 2)
    shm[pl.ds(0, NZ), pl.ds(8, CX), :] = along_y(mp[1, pl.ds(0, NZ), pl.ds(8, CX), :], 2)

    whole(0, r0b.at[pl.ds(0, 304)]).wait_recv()
    all_of(recv_w, xa, 0).wait_recv()
    all_of(recv_p, xa, 2).wait_recv()
    info = recv_p[...].reshape(GX, CY)
    for j in range(GY):
        send_b[j, 0:16, :] = recv_w.reshape(GX * GY, CY)[pl.ds(j, GX, stride=8), :]
        send_b[j, 16:32, :] = info
    to_gy(send_b, tab, 4)
    unpack_x(rows_v, pairs_v, r0b, (0, 1))
    put_rows(rows_m, 1, 34, 0, 24, r0b[pl.ds(288, 32), :])
    def reach(packed, forward):
        at = lane16 % 4
        up1, dn1 = pltpu.roll(packed, CY - 1, 1), pltpu.roll(packed, 1, 1)
        if forward:
            up2 = pltpu.roll(packed, CY - 2, 1)
            return jnp.where(
                at == 0, -up2, jnp.where(at == 1, 27.0 * up1 - up2, jnp.where(at == 2, dn1, 0.0))
            )
        dn2 = pltpu.roll(packed, 2, 1)
        return jnp.where(
            at == 0, 0.0, jnp.where(at == 1, -up1, jnp.where(at == 2, dn2 - 27.0 * dn1, dn2))
        )

    reach_v = [
        reach(merge_y(r0b, (352 + 16 * f, 416 + 16 * f)), forward)
        for f, forward in enumerate((True, False, True))
    ]
    packed_m = r0b[pl.ds(464, CX), :]

    out_x = (row16 == CX - 1) & (me_x == GX - 1)
    out_y = (lane16 == CY - 1) & (me_y == GY - 1)
    out_xy = out_x | out_y
    last_lane = lane16 == CY - 1
    edge = (lane16 < 2) | (lane16 >= CY - 2)

    def to_last(packed, k):
        return pltpu.roll(packed, lax.rem(2 * CY - 3 - 4 * k, CY), 1)

    def average_b(k, carry):
        b = mp[0, k, 8:24, :]
        bx = jnp.where(out_x, b, mp[0, k, 9:25, :])
        by = jnp.where(out_y, b, jnp.where(last_lane, to_last(packed_b, k), shb[k]))
        bz = jnp.where(k == NZ - 1, b, mp[0, k + 1, 8:24, :])
        av[0, k] = (b + bx) * (0.5 * UNIT)
        av[1, k] = (b + by) * (0.5 * UNIT)
        av[2, k] = (b + bz) * (0.5 * UNIT)
        return carry

    def average_m(k, carry):
        last = k == NZ - 1
        m = mp[1, k, 8:24, :]
        mx = jnp.where(out_x, m, mp[1, k, 9:25, :])
        my = jnp.where(out_y, m, shm[k, 8:24, :])
        mxy = jnp.where(out_xy, m, shm[k, 9:25, :])
        mz = jnp.where(last, m, mp[1, k + 1, 8:24, :])
        mxz = jnp.where(out_x | last, m, mp[1, k + 1, 9:25, :])
        myz = jnp.where(out_y | last, m, shm[k + 1, 8:24, :])
        av[3, k] = (m + mx + my + mxy) * (0.25 * UNIT)
        av[4, k] = (m + mx + mz + mxz) * (0.25 * UNIT)
        av[5, k] = (m + my + mz + myz) * (0.25 * UNIT)
        return carry

    def join(k, carry):
        shm[k, 8:24, :] = jnp.where(last_lane, to_last(packed_m, k), shm[k, 8:24, :])
        return carry

    def layers(action, init, first=0, last=NZ // GROUP):
        def group(i, carry):
            for j in range(GROUP):
                carry = action(GROUP * i + j, carry)
            return carry

        return lax.fori_loop(first, last, group, init)

    layers(join, 0)
    lane32, row32 = iota((NZ, CY), 1), iota((NZ, CY), 0)
    corners = jnp.broadcast_to(r0b[pl.ds(496, 8), :][0:1, :], (NZ, CY))
    corners = jnp.sum(jnp.where(lane32 == 4 * row32 + 2, corners, 0.0), axis=1, keepdims=True)
    eastern = pltpu.roll(r0b[pl.ds(288, NZ), :], CY - 1, 1)
    eastern = jnp.where(lane32 == CY - 1, corners, eastern)
    put_rows(shm.reshape(33 * 32, CY), 0, 33, 0, 24, eastern)
    layers(average_m, 0)

    def fwd(minus, zero_, plus, plus2):
        return 27.0 * (plus - zero_) - (plus2 - minus)

    def bwd(minus2, minus, zero_, plus):
        return 27.0 * (zero_ - minus) - (plus - minus2)

    def dx(ref, f, k, forward):
        first = 7 if forward else 6
        parts = [ref[f, k + 2, first + i : first + i + CX, :] for i in range(4)]
        return (fwd if forward else bwd)(*parts)

    def dz(ref, f, k, forward):
        first = 1 if forward else 0
        parts = [ref[f, k + first + i, 8:24, :] for i in range(4)]
        return (fwd if forward else bwd)(*parts)

    def dy(reaches, i, k):
        return dyb[i, k] + jnp.where(edge, reaches(i, k), 0.0)

    def pack_half(carry, values, k):
        first = pack_layer(pack_layer(carry[0], values[0], k), values[1], k + HALF)
        return first, pack_layer(carry[1], values[2], k)

    def stress_layer(reaches, h, k, carry):
        sx, sy, sz = dx(vp, 0, k, False), dy(reaches, 1, k), dz(vp, 2, k, False)
        m2 = (2.0 * UNIT) * mp[1, k, 8:24, :]
        volume = (UNIT * lam[k]) * (sx + sy + sz)
        new = {}
        for f, s in ((0, sx), (1, sy), (2, sz)):
            new[f] = sp[f, k + 2, 8:24, :] + (volume + m2 * s)
        shear_xy = dy(reaches, 0, k) + dx(vp, 1, k, True)
        shear_xz = dz(vp, 0, k, True) + dx(vp, 2, k, True)
        shear_yz = dz(vp, 1, k, True) + dy(reaches, 2, k)
        for f, s in ((3, shear_xy), (4, shear_xz), (5, shear_yz)):
            new[f] = sp[f, k + 2, 8:24, :] + av[f, k] * s
        for f in range(6):
            sp[f, k + 2, 8:24, :] = new[f]
        return pack_half(carry, (new[3], new[1], new[5]), k - HALF * h)

    def velocity_layer(reaches, out, surface, h, k, carry):
        ax = dx(sp, 0, k, True) + dy(reaches, 0, k) + dz(sp, 4, k, False)
        ay = dx(sp, 3, k, False) + dy(reaches, 1, k) + dz(sp, 5, k, False)
        az = dx(sp, 4, k, False) + dy(reaches, 2, k) + dz(sp, 2, k, True)
        new = []
        for f, a in ((0, ax), (1, ay), (2, az)):
            value = vp[f, k + 2, 8:24, :] + av[f, k] * a
            if surface:
                value = value + forc[f]
            new.append(value)
            if out is None:
                vp[f, k + 2, 8:24, :] = value
            else:
                out[f, k] = value
        return pack_half(carry, new, k - HALF * h) if carry else carry

    def received(slot, ref, pairs, rbuf, kinds):
        def begin(h):
            whole(slot + h, rbuf.at[pl.ds(0, 208)]).wait_recv()
            unpack_x(ref, pairs, rbuf, (2 * h, 2 * h + 1))
            south_at, north_at = 288 + 32 * h, 352 + 32 * h
            merged = [merge_y(rbuf, (south_at + 16 * i, north_at + 16 * i)) for i in range(2)]
            fields = [reach(merged[i // 2], kinds[i]) for i in range(3)]
            return lambda i, k: halo_of(fields[i], k - HALF * h + (HALF if i == 1 else 0))

        return begin

    count = PART // GROUP
    blank = (jnp.zeros((CX, CY), F32),) * 2

    def send_half(buf, halos, carry, h):
        for i in range(2):
            buf[pl.ds(288 + 32 * h + 16 * i, 16), :] = carry[i]
        start(halos[1](h))

    def stress_step(begin, buf, halos, between=None):
        for h in range(2):
            if h == 1 and between is not None:
                between()
            reaches, carry = begin(h), blank
            for part in (2 * h, 2 * h + 1):
                carry = layers(
                    lambda k, c: stress_layer(reaches, h, k, c), carry, count * part, count * part + count
                )
                pack_x(rows_s, pairs_s, buf, part)
                start(halos[0](part))
            send_half(buf, halos, carry, h)

    def velocity_step(begin, out, buf, halos):
        for h in range(2):
            reaches, carry = begin(h), () if buf is None else blank
            for part in (2 * h, 2 * h + 1):
                first = count * part
                if part == 0:
                    for k in range(GROUP):
                        carry = velocity_layer(reaches, out, k == 0, h, k, carry)
                    first = 1
                carry = layers(
                    lambda k, c: velocity_layer(reaches, out, False, h, k, c),
                    carry,
                    first,
                    count * part + count,
                )
                if buf is not None:
                    pack_x(rows_v, pairs_v, buf, part)
                    start(halos[0](part))
            if buf is not None:
                send_half(buf, halos, carry, h)

    loads[10].wait()
    loads[11].wait()
    halos1 = halo_set(3, b1, r1b, 160, 128)

    def begin_first(h):
        if h == 1:
            whole(1, r0b.at[pl.ds(0, 144)]).wait_recv()
            unpack_x(rows_v, pairs_v, r0b, (2, 3))
        return lambda i, k: halo_of(reach_v[i], k)

    stress_step(begin_first, b1, halos1)
    y_parts(sp, (3, 1, 5), (1, 0, 1))
    whole(2, r0b.at[pl.ds(0, 48)]).wait_recv()
    put_rows(rows_m, 0, 34, 0, 24, r0b[pl.ds(320, 32), :])
    packed_b = r0b[pl.ds(480, CX), :]
    layers(average_b, 0)

    all_of(tab, xa, 4).wait_recv()
    row128, lane128 = iota((128, CY), 0), iota((128, CY), 1)
    sel = iota((16, CY), 1) == (iota((16, CY), 0) % 8) * 16 + (iota((16, CY), 0) // 8) * 8 + me_y

    def by_slot(value):
        both = pick_lhs(sel.astype(F32), value, NT)
        return jnp.concatenate([both[0:8], both[8:16]], axis=1)

    params = by_slot(tab[:, 16:32, :].reshape(128, CY))
    r0, c0 = params, pltpu.roll(params, 5, 0)
    sent = tab[:, 0:16, :].reshape(128, CY)
    for p in range(2):
        want = (row128 % CX < FOOT) & (lane128 == 64 * p + (row128 % CX) * FOOT + row128 // CX)
        placed = pick_lhs(want.astype(F32), sent, NT)
        shift = jnp.broadcast_to(params[7:8, 128 * p : 128 * p + 128], (128, CY)).astype(jnp.int32)
        for bit in (1, 2, 4, 8):
            placed = jnp.where((shift & bit) != 0, pltpu.roll(placed, bit, 0), placed)
        wxt[:, 128 * p : 128 * p + 128] = placed
    oyt = (iota((CY, 256), 0).astype(F32) == params[6:7]).astype(F32).astype(BF16)

    def motion():
        total = jnp.zeros((8, 256), F32)
        row = iota((8, 256), 0)
        for f in range(3):
            value = vp[f, 2, 8:24, :]
            turns = [value] + [pltpu.roll(value, CY - c, 1) for c in range(1, FOOT)]
            hi, lo = split(jnp.concatenate(turns, axis=0))
            found = mm(hi, oyt, NN) + mm(lo, oyt, NN)
            one = jnp.sum(found * wxt[...], axis=0, keepdims=True)
            total = jnp.where(row == f, jnp.broadcast_to(one, (8, 256)), total)
        return total

    def push(reaction):
        reaction = reaction * (DT * FOOT)
        for f in range(3):
            hi, lo = split(wxt[...] * reaction[f : f + 1])
            spread = mm(hi, oyt, NT) + mm(lo, oyt, NT)
            total = spread[0:CX]
            for c in range(1, FOOT):
                total = total + pltpu.roll(spread[CX * c : CX * c + CX], c, 1)
            forc[f] = total

    def send_motion(step, value):
        bm_s[step] = jnp.where(row8 < 4, value[:, 0:128], pltpu.roll(value[:, 128:256], 4, 0))
        over(
            GY,
            me_y,
            lambda peer: along(
                bm_s.at[step], m_r.at[step, me_y], xm, 4 * step, me_x, peer
            ).start(),
        )
        m_r[step, me_y] = bm_s[step]

    def pass_motion(step):
        all_of(m_r.at[step], xm, 4 * step).wait_recv()
        want = (iota((GX, CY), 1) == iota((GX, CY), 0) + GX * me_y).astype(F32)
        rows = pick_lhs(want, m_r[step].reshape(GY * 8, CY), NT)
        rows = jnp.concatenate([rows, jnp.zeros((GX, CY - GY * 8), F32)], axis=1)
        m_p[step] = rows.reshape(GX, 1, CY)
        over(
            GX,
            me_x,
            lambda peer: along(
                m_p.at[step, peer], m_q.at[step, me_x], xm, 4 * step + 2, peer, me_y
            ).start(),
        )
        m_q[step, me_x] = m_p[step, me_x]

    want_lane = own_yc * 2.0 + pos_col
    own_gx = (iota((NB, GX), 1).astype(F32) == own_xc).astype(F32)

    def take_motion(step):
        all_of(m_q.at[step], xm, 4 * step + 2).wait_recv()
        found = pick_lhs(own_gx, m_q[step].reshape(GX, CY), NN)
        found = jnp.where((lane // 4).astype(F32) == want_lane, found, 0.0)
        onto = (iota((CY, DOF), 0) % 4 == iota((CY, DOF), 1) % 3).astype(F32)
        return pick_rhs(found, onto, NN)

    bm1 = motion()
    send_motion(0, bm1)
    push(r0 - c0 * bm1)

    all_of(recv_q, xa, 6).wait_recv()
    send_d[...] = recv_q[...].reshape(GX, CY)
    over(GY, me_y, lambda peer: along(send_d, tab_q.at[me_y], xa, 8, me_x, peer).start())
    tab_q[me_y] = send_d[...]

    kinds_s, kinds_v = (False, True, False), (True, False, True)
    halos2 = halo_set(5, b2, r2b, 128, 160)
    velocity_step(received(3, rows_s, pairs_s, r1b, kinds_s), None, b2, halos2)

    bm2 = motion()
    send_motion(1, bm2)
    y_parts(vp, (0, 1, 2), (0, 1, 0))
    pass_motion(0)
    all_of(tab_q, xa, 8).wait_recv()
    params = by_slot(tab_q[...].reshape(128, CY))
    push(pltpu.roll(params, 5, 0) + params * bm1 - c0 * bm2)

    halos3 = halo_set(7, b3, r3b, 160, 128)
    stress_step(received(5, rows_v, pairs_v, r2b, kinds_v), b3, halos3, lambda: pass_motion(1))
    y_parts(sp, (3, 1, 5), (1, 0, 1))

    def advance(rates, drifts, restoring, base):
        relative = jnp.where(mask, rates - base, 0.0)
        rates = jnp.where(mask, rates - DT * restoring - DT * cpl * relative, 0.0)
        return rates, jnp.where(mask, drifts + DT * rates, 0.0)

    rate1, drift1 = advance(rate0, drift0, rest0, take_motion(0))
    restore(drift1)

    velocity_step(received(7, rows_s, pairs_s, r3b, kinds_s), ovel, None, None)
    rate2, drift2 = advance(rate1, drift1, rest[...], take_motion(1))
    odrift[...] = drift2
    orate[...] = rate2

    for slot, n in enumerate((304, 144, 48)):
        whole(slot, r0b.at[pl.ds(0, n)]).wait_send()
    for slot in range(3, 9):
        whole(slot, r1b.at[pl.ds(0, 208)]).wait_send()
    for ref, base in ((recv_w, 0), (recv_p, 2), (tab, 4), (recv_q, 6), (tab_q, 8)):
        all_of(ref, xa, base).wait_send()
    for step in range(2):
        all_of(m_r.at[step], xm, 4 * step).wait_send()
        all_of(m_q.at[step], xm, 4 * step + 2).wait_send()


def finish(vel, drift, rate, ovel, odrift, orate, sem):
    copies = [
        pltpu.make_async_copy(vel, ovel, sem.at[0]),
        pltpu.make_async_copy(drift, odrift, sem.at[1]),
        pltpu.make_async_copy(rate, orate, sem.at[2]),
    ]
    for c in copies:
        c.start()
    for c in copies:
        c.wait()


def body(vel, stress, buoy, lame, shear, stiff, drift, rate, coup, contact, dof, owner, corner):
    anywhere = pl.BlockSpec(memory_space=pltpu.HBM)
    vmem = pltpu.VMEM
    near = pl.BlockSpec(memory_space=vmem)
    dma = pltpu.SemaphoreType.DMA
    halo = [vmem((512, CY), F32), vmem((528, CY), F32)] + [vmem((352, CY), F32), vmem((416, CY), F32)] * 3
    shapes = ((3, NZ, CX, CY), (NB, DOF), (NB, DOF))
    outs = pl.pallas_call(
        kernel,
        out_shape=tuple(vmem(s, F32) for s in shapes),
        in_specs=[anywhere] * 13,
        out_specs=(near,) * 3,
        scratch_shapes=[
            vmem((3, 36, 32, CY), F32),
            vmem((6, 36, 32, CY), F32),
            vmem((2, 34, 32, CY), F32),
            vmem((NZ, CX, CY), F32),
            vmem((6, NZ, CX, CY), F32),
            vmem((NB, DOF, DOF), BF16),
            vmem((3, NB, DOF), F32),
            vmem((NB, 64), F32),
            vmem((1, NB), jnp.int32),
            vmem((1, NB), jnp.int32),
            vmem((1, NB), jnp.int32),
            vmem((3, NZ, CX, CY), F32),
            vmem((3, 256, CY), BF16),
            vmem((NZ, CX, CY), F32),
            vmem((33, 32, CY), F32),
            vmem((GX, GY, CY), F32),
            vmem((GX, GY, CY), F32),
            vmem((GX, 1, CY), F32),
            vmem((GX, 1, CY), F32),
            vmem((GY, 32, CY), F32),
            vmem((GY, 32, CY), F32),
            vmem((GX, 1, CY), F32),
            vmem((GX, 1, CY), F32),
            vmem((GX, CY), F32),
            vmem((GY, GX, CY), F32),
            vmem((128, 256), F32),
            vmem((3, CX, CY), F32),
            vmem((2, 8, CY), F32),
            vmem((2, GY, 8, CY), F32),
            vmem((2, GX, 1, CY), F32),
            vmem((2, GX, 1, CY), F32),
            vmem((NB, DOF), F32),
            vmem((NB, DOF), BF16),
            *halo,
            dma((12,)),
            dma((4,)),
            dma((10,)),
            dma((8,)),
            dma((9,)),
            dma((9,)),
        ],
        compiler_params=pltpu.CompilerParams(
            collective_id=0, has_side_effects=True, vmem_limit_bytes=66_100_000
        ),
    )(
        vel, stress, buoy, lame, shear, stiff, drift, rate, coup, contact,
        dof.reshape(1, NB), owner.reshape(1, NB), corner.reshape(1, NB),
    )
    return pl.pallas_call(
        finish,
        out_shape=tuple(jax.ShapeDtypeStruct(s, F32) for s in shapes),
        in_specs=[near] * 3,
        out_specs=(anywhere,) * 3,
        scratch_shapes=[dma((3,))],
        compiler_params=pltpu.CompilerParams(vmem_limit_bytes=1024 * 1024),
    )(*outs)


def solution(mesh):
    placed = (
        P(None, None, "gx", "gy"),
        P(None, None, "gx", "gy"),
        P(None, "gx", "gy"),
        P(None, "gx", "gy"),
        P(None, "gx", "gy"),
        P(("gx", "gy"), None, None),
        P(("gx", "gy"), None),
        P(("gx", "gy"), None),
        P(("gx", "gy"), None),
        P(("gx", "gy"), None),
        P(("gx", "gy")),
        P(("gx", "gy"), None),
        P(("gx", "gy")),
    )
    return jax.shard_map(
        body,
        mesh=mesh,
        in_specs=placed,
        out_specs=(P(None, None, "gx", "gy"), P(("gx", "gy"), None), P(("gx", "gy"), None)),
        check_vma=False,
    )
```
